32 devices in a mesh: dp: 8 (over y, x, core), tensor: 4 (over z).
Axes of the slice: x: 2, y: 2, z: 4, core: 2. Of those that a mesh axis runs over, the one named last changes fastest.
Arguments:
- tokens: bfloat16 [16384, 1536], P('dp'), may hold values from -6 to 6
- lengths: int32 [8], P('dp'), may hold values from 1024 to 2048, as said below
- cotangent: bfloat16 [16384, 1536], P('dp'), may hold values from -6 to 6
- norm_gain: float32 [1536], replicated, may hold values from 0.1 to 1.9
- query_w: bfloat16 [1536, 1536], P(None, 'tensor'), may hold values from -0.15625 to 0.15625
- key_weight: bfloat16 [1536, 512], P(None, 'tensor'), may hold values from -0.15625 to 0.15625
- value_weight: bfloat16 [1536, 512], P(None, 'tensor'), may hold values from -0.15625 to 0.15625
- out_w: bfloat16 [1536, 1536], P('tensor'), may hold values from -0.625 to 0.625
- query_gain: float32 [64], replicated, may hold values from 0.1 to 1.9
- key_gain: float32 [64], replicated, may hold values from 0.1 to 1.9
- mlp_gain: float32 [1536], replicated, may hold values from 0.1 to 1.9
- gate_w: bfloat16 [1536, 6912], P(None, 'tensor'), may hold values from -0.15625 to 0.15625
- up_w: bfloat16 [1536, 6912], P(None, 'tensor'), may hold values from -0.15625 to 0.15625
- down_w: bfloat16 [6912, 1536], P('tensor'), may hold values from -0.078125 to 0.078125
Outputs:
- block_out: bfloat16 [16384, 1536], P('dp')
- input_grad: float32 [16384, 1536], P('dp')
- norm_gain_grad: float32 [1536], replicated
- query_w_grad: float32 [1536, 1536], P(None, 'tensor')
- key_w_grad: float32 [1536, 512], P(None, 'tensor')
- value_weight_gradient: float32 [1536, 512], P(None, 'tensor')
- out_w_grad: float32 [1536, 1536], P('tensor')
- query_gain_grad: float32 [64], replicated
- key_gain_grad: float32 [64], replicated
- mlp_gain_grad: float32 [1536], replicated
- gate_w_grad: float32 [1536, 6912], P(None, 'tensor')
- up_w_grad: float32 [1536, 6912], P(None, 'tensor')
- down_w_grad: float32 [6912, 1536], P('tensor')
The draws below stay inside these ranges and needn't reach their ends.
Inputs may be any that keep to these rules, and one draw needn't show every extreme that they name: `lengths`: each sequence's live slots are its first ones; some sequence fills all 2048 slots.
All inputs are finite; a program needn't handle non-finite values.
Results may differ from the reference program's by a relative error of at most 0.024.
Values may be sent and summed in bfloat16 or wider, within the bound.
A program may use at most 384 MiB of HBM per device.

```python
import math
import jax
import jax.numpy as jnp
from jax import lax

MODEL_WIDTH = 1536
HQ = 24
KEY_VALUE_HEADS = 8
HEAD_SIZE = 64
FF = 6912
SEQ = 2048
BLK = 512
GROUPS = 8
SPLITS = 4
TOKENS = 16384


def draw_lengths(key, part):
    first_key, second_key = jax.random.split(jax.random.fold_in(key, 11))
    drawn = jax.random.randint(first_key, (GROUPS,), SEQ // 2, SEQ + 1)
    chosen = jax.random.randint(second_key, (), 0, GROUPS)
    return jnp.where(jnp.arange(GROUPS) == chosen, SEQ, drawn).astype(jnp.int32)


def level_of(stream_key, extent, cuts, low, largest):
    level, own = 1.0, jax.random.fold_in(stream_key, 6)
    for axis_at, blocks in cuts:
        heights = jnp.exp(jax.random.uniform(jax.random.fold_in(own, axis_at), (blocks,), jnp.float32, low / len(cuts), largest / len(cuts)))
        level = level * jnp.repeat(heights, extent[axis_at] // blocks).reshape([-1 if axis == axis_at else 1 for axis in range(len(extent))])
    return level


def bell_draw(key, dims, scale, reach, cuts=(), dtype=jnp.bfloat16):
    values = scale * jax.random.normal(key, dims, jnp.float32)
    if cuts:
        values = values * level_of(key, dims, cuts, -0.22, 0.18)
    return jnp.clip(values, -reach, reach).astype(dtype)


def setup_inputs(seed: int = 0) -> dict:
    key_of = jax.random.split(jax.random.key(seed), 15)
    return {
        "tokens": bell_draw(key_of[0], (TOKENS, MODEL_WIDTH), 1.0, 6.0, ((0, 8),)),
        "lengths": draw_lengths(jax.random.fold_in(key_of[14], 71), 0),
        "cotangent": bell_draw(key_of[2], (TOKENS, MODEL_WIDTH), 1.0, 6.0, ((0, 8),)),
        "norm_gain": jnp.clip(1.0 + 0.18 * jax.random.normal(key_of[3], (MODEL_WIDTH,), jnp.float32), 0.1, 1.9),
        "query_w": bell_draw(key_of[4], (MODEL_WIDTH, HQ * HEAD_SIZE), MODEL_WIDTH ** -0.5, 0.15625, ((1, 4),)),
        "key_weight": bell_draw(key_of[5], (MODEL_WIDTH, KEY_VALUE_HEADS * HEAD_SIZE), MODEL_WIDTH ** -0.5, 0.15625, ((1, 4),)),
        "value_weight": bell_draw(key_of[6], (MODEL_WIDTH, KEY_VALUE_HEADS * HEAD_SIZE), MODEL_WIDTH ** -0.5, 0.15625, ((1, 4),)),
        "out_w": bell_draw(key_of[7], (HQ * HEAD_SIZE, MODEL_WIDTH), (HQ * HEAD_SIZE // 16) ** -0.5, 0.625, ((0, 4),)),
        "query_gain": jnp.clip(1.0 + 0.18 * jax.random.normal(key_of[8], (HEAD_SIZE,), jnp.float32), 0.1, 1.9),
        "key_gain": jnp.clip(1.0 + 0.18 * jax.random.normal(key_of[9], (HEAD_SIZE,), jnp.float32), 0.1, 1.9),
        "mlp_gain": jnp.clip(1.0 + 0.18 * jax.random.normal(key_of[10], (MODEL_WIDTH,), jnp.float32), 0.1, 1.9),
        "gate_w": bell_draw(key_of[11], (MODEL_WIDTH, FF), MODEL_WIDTH ** -0.5, 0.15625, ((1, 4),)),
        "up_w": bell_draw(key_of[12], (MODEL_WIDTH, FF), MODEL_WIDTH ** -0.5, 0.15625, ((1, 4),)),
        "down_w": bell_draw(key_of[13], (FF, MODEL_WIDTH), FF ** -0.5, 0.078125, ((0, 4),)),
    }


EPSILON = 1e-05
ROPE_BASE = 1000000.0
PRECISE = lax.Precision.HIGHEST

@jax.custom_vjp
def low(v):
    return lax.optimization_barrier(v.astype(jnp.bfloat16)).astype(jnp.float32)

@jax.custom_vjp
def low_back(v):
    return v

def low_keep(v):
    return (low(v), None)

def low_pass(kept, grad):
    return (grad,)

def back_keep(v):
    return (v, None)

def back_low(kept, grad):
    return (low(grad),)
low.defvjp(low_keep, low_pass)
low_back.defvjp(back_keep, back_low)

def product(left, right):
    return jnp.dot(left, right, precision=PRECISE, preferred_element_type=jnp.float32)

def rms_scale(inputs, gain_vec):
    return inputs * lax.rsqrt(lax.optimization_barrier(jnp.mean(inputs * inputs, axis=-1, keepdims=True)) + EPSILON) * gain_vec

def rotary(inputs, head_count):
    row_count = inputs.shape[0]
    half_dim = HEAD_SIZE // 2
    positions = jnp.arange(row_count).astype(jnp.float32)[:, None]
    inv_freq = jnp.exp(jnp.arange(half_dim).astype(jnp.float32) * (-2.0 * math.log(ROPE_BASE) / HEAD_SIZE))
    angles = positions * inv_freq[None, :]
    cosine = jnp.cos(angles)[:, None, :]
    sine_tab = jnp.sin(angles)[:, None, :]
    split_heads = inputs.reshape(row_count, head_count, HEAD_SIZE)
    lower_half = split_heads[..., :half_dim]
    upper_half = split_heads[..., half_dim:]
    turned = jnp.concatenate([lower_half * cosine - upper_half * sine_tab, upper_half * cosine + lower_half * sine_tab], axis=-1)
    return turned.reshape(row_count, head_count * HEAD_SIZE)

def head_norm(inputs, gain_vec, head_count):
    row_count = inputs.shape[0]
    return rms_scale(inputs.reshape(row_count, head_count, HEAD_SIZE), gain_vec).reshape(row_count, head_count * HEAD_SIZE)

def prepare(queries, keys_val, q_gain, k_gain):
    q_count = queries.shape[1] // HEAD_SIZE
    kv_count = keys_val.shape[1] // HEAD_SIZE
    return (rotary(head_norm(queries, q_gain, q_count), q_count), rotary(head_norm(keys_val, k_gain, kv_count), kv_count))

def swiglu(gate_val, up_val):
    return gate_val * jax.nn.sigmoid(gate_val) * up_val

def attention(q_flat, k_flat, v_flat, length):
    row_count = q_flat.shape[0]
    kv_count = k_flat.shape[1] // HEAD_SIZE
    group_size = q_flat.shape[1] // k_flat.shape[1]
    q_heads = q_flat.reshape(row_count, kv_count, group_size, HEAD_SIZE).transpose(1, 2, 0, 3)
    k_heads = k_flat.reshape(row_count, kv_count, HEAD_SIZE).transpose(1, 0, 2)
    v_heads = v_flat.reshape(row_count, kv_count, HEAD_SIZE).transpose(1, 0, 2)
    block_count = row_count // BLK
    blocks = q_heads.reshape(kv_count, group_size, block_count, BLK, HEAD_SIZE).transpose(2, 0, 1, 3, 4)
    starts = (jnp.arange(block_count) * BLK).astype(jnp.int32)
    key_pos = jnp.arange(row_count).astype(jnp.int32)
    score_scale = float(HEAD_SIZE) ** (-0.5)

    @jax.checkpoint
    def one_block(seq_item):
        q_block, first_row = seq_item
        raw_scores = jnp.einsum('kgqd,kjd->kgqj', q_block, k_heads, precision=PRECISE)
        scaled = low_back(raw_scores) * score_scale
        query_pos = first_row + jnp.arange(BLK).astype(jnp.int32)
        allowed = (key_pos[None, :] <= query_pos[:, None]) & (key_pos[None, :] < length)
        scaled = jnp.where(allowed, scaled, -jnp.inf)
        row_max = lax.optimization_barrier(jnp.max(scaled, axis=-1, keepdims=True))
        weight = jnp.exp(scaled - row_max)
        attn_prob = weight / lax.optimization_barrier(jnp.sum(weight, axis=-1, keepdims=True))
        return jnp.einsum('kgqj,kjd->kgqd', low(attn_prob), v_heads, precision=PRECISE)
    outputs = lax.map(one_block, (blocks, starts))
    return outputs.transpose(0, 3, 1, 2, 4).reshape(row_count, kv_count * group_size * HEAD_SIZE)

def forward(inputs, params, length):
    norm_gain, query_w, key_weight, value_weight, out_w, query_gain, key_gain, mlp_gain, gate_w, up_w, down_w = params
    q_cols = query_w.shape[1] // SPLITS
    k_cols = key_weight.shape[1] // SPLITS
    f_cols = gate_w.shape[1] // SPLITS
    normed = low(rms_scale(inputs, norm_gain))
    q_parts = []
    k_parts = []
    v_parts = []
    for group_idx in range(SPLITS):
        shared = low_back(normed)
        q_parts.append(product(shared, query_w[:, group_idx * q_cols:(group_idx + 1) * q_cols]))
        k_parts.append(product(shared, key_weight[:, group_idx * k_cols:(group_idx + 1) * k_cols]))
        v_parts.append(product(shared, value_weight[:, group_idx * k_cols:(group_idx + 1) * k_cols]))
    queries = low_back(jnp.concatenate(q_parts, axis=1))
    keys_val = low_back(jnp.concatenate(k_parts, axis=1))
    values_b = low(low_back(jnp.concatenate(v_parts, axis=1)))
    query_r, keys_r = prepare(queries, keys_val, query_gain, key_gain)
    mixed = attention(low(query_r), low(keys_r), values_b, length)
    mixed_b = low(low_back(mixed))
    attn_out = jnp.zeros_like(inputs)
    for group_idx in range(SPLITS):
        piece = product(mixed_b[:, group_idx * q_cols:(group_idx + 1) * q_cols], out_w[group_idx * q_cols:(group_idx + 1) * q_cols, :])
        attn_out = attn_out + low(low_back(piece))
    residual = inputs + attn_out
    normed2 = low(rms_scale(residual, mlp_gain))
    g_parts = []
    u_parts = []
    for group_idx in range(SPLITS):
        shared = low_back(normed2)
        g_parts.append(product(shared, gate_w[:, group_idx * f_cols:(group_idx + 1) * f_cols]))
        u_parts.append(product(shared, up_w[:, group_idx * f_cols:(group_idx + 1) * f_cols]))
    gate_val = low_back(jnp.concatenate(g_parts, axis=1))
    up_val = low_back(jnp.concatenate(u_parts, axis=1))
    hidden = low(swiglu(gate_val, up_val))
    mlp_out = jnp.zeros_like(inputs)
    for group_idx in range(SPLITS):
        piece = product(hidden[:, group_idx * f_cols:(group_idx + 1) * f_cols], down_w[group_idx * f_cols:(group_idx + 1) * f_cols, :])
        mlp_out = mlp_out + low(low_back(piece))
    return residual + mlp_out

def reference(tokens, lengths, cotangent, norm_gain, query_w, key_weight, value_weight, out_w, query_gain, key_gain, mlp_gain, gate_w, up_w, down_w):
    params = (norm_gain.astype(jnp.float32), query_w.astype(jnp.float32), key_weight.astype(jnp.float32), value_weight.astype(jnp.float32), out_w.astype(jnp.float32), query_gain.astype(jnp.float32), key_gain.astype(jnp.float32), mlp_gain.astype(jnp.float32), gate_w.astype(jnp.float32), up_w.astype(jnp.float32), down_w.astype(jnp.float32))
    seq_inputs = tokens.astype(jnp.float32).reshape(GROUPS, SEQ, MODEL_WIDTH)
    seq_cots = cotangent.astype(jnp.float32).reshape(GROUPS, SEQ, MODEL_WIDTH)

    def one_seq(running, seq_item):
        inputs, seq_cot, length = seq_item
        live_rows = (jnp.arange(SEQ).astype(jnp.int32) < length).astype(jnp.float32)

        def local_forward(x_value, p_value):
            return forward(x_value, p_value, length)
        result, pullback = jax.vjp(local_forward, inputs, params)
        d_inputs, d_params = pullback(seq_cot * live_rows[:, None])
        running = jax.tree.map(jnp.add, running, d_params)
        return (running, (result.astype(jnp.bfloat16), d_inputs))
    zero_grads = jax.tree.map(jnp.zeros_like, params)
    totals, (outputs, d_inputs) = lax.scan(one_seq, zero_grads, (seq_inputs, seq_cots, lengths))
    return (outputs.reshape(TOKENS, MODEL_WIDTH), d_inputs.reshape(TOKENS, MODEL_WIDTH), totals[0], totals[1], totals[2], totals[3], totals[4], totals[5], totals[6], totals[7], totals[8], totals[9], totals[10])
```

```python
import functools
import math

import jax
import jax.numpy as jnp
from jax import lax
from jax.experimental import pallas as pl
from jax.experimental.pallas import tpu as pltpu
from jax.sharding import PartitionSpec as P

HEAD_SIZE = 64
BLK = 512
LANES=128
SCALE = HEAD_SIZE ** -0.5
LOG2E = math.log2(math.e)
F32=jnp.float32; BF16=jnp.bfloat16

def nt(a,b): return lax.dot_general(a,b,(((1,),(1,)),((),())),preferred_element_type=F32)
def tn(a,b): return lax.dot_general(a,b,(((0,),(0,)),((),())),preferred_element_type=F32)
def nn(a,b): return lax.dot_general(a,b,(((1,),(0,)),((),())),preferred_element_type=F32)

def head_places(heads, group):
    return [(h // 2, h % 2, h // group) for h in range(heads)]

def half_mask(half, dtype=F32):
    lane = lax.broadcasted_iota(jnp.int32, (1, LANES), 1)
    keep = lane < HEAD_SIZE if half == 0 else lane >= HEAD_SIZE
    return keep

def stack_heads(x, places):
    out = []
    for tile, half, kv in places:
        piece = x[:, tile * LANES:(tile + 1) * LANES]
        if half != kv:
            piece = pltpu.roll(piece, HEAD_SIZE, 1)
        out.append(jnp.where(half_mask(kv), piece, 0.0))
    return jnp.concatenate(out, axis=0)

def unstack_heads(x, places, tiles, n):
    pieces = {}
    for h, (tile, half, kv) in enumerate(places):
        piece = x[h * n:(h + 1) * n]
        if half != kv:
            piece = pltpu.roll(piece, HEAD_SIZE, 1)
        pieces[tile, half] = piece
    out = []
    for tile in range(tiles):
        low = pieces[tile, 0]
        high = pieces.get((tile, 1))
        out.append(jnp.where(half_mask(0), low, 0.0 if high is None else high))
    return jnp.concatenate(out, axis=1)

def fwd_kernel(places, tiles, bq, bk, len_ref, q_ref, k_ref, v_ref, o_ref, linv_ref, q6, vx, acc):
    i = pl.program_id(0)
    heads = len(places)
    rows = k_ref.shape[0]
    @pl.when(i == 0)
    def _():
        live = lax.broadcasted_iota(jnp.int32, (rows, LANES), 0) < len_ref[0]
        vx[:, :LANES] = jnp.where(live, v_ref[...].astype(F32), 0.0).astype(BF16)
        vx[:, LANES:] = jnp.where(live, 1.0, 0.0).astype(BF16)
    q6[...] = stack_heads(q_ref[...].astype(F32), places).astype(BF16)
    acc[...] = jnp.zeros_like(acc)
    def step(j, masked):
        ks = pl.ds(pl.multiple_of(j * bk, bk), bk)
        s = nt(q6[...], k_ref[ks, :])
        p = jnp.exp2(s * (SCALE * LOG2E))
        if masked:
            qp = i * bq + (lax.broadcasted_iota(jnp.int32, s.shape, 0) & (bq - 1))
            kp = j * bk + lax.broadcasted_iota(jnp.int32, s.shape, 1)
            p = jnp.where(kp <= qp, p, 0.0)
        acc[...] += nn(p.astype(BF16), vx[ks, :])
    full = (i * bq) // bk
    @pl.loop(0, full)
    def _(j): step(j, False)
    @pl.loop(full, full + max(bq // bk, 1))
    def _(j): step(j, True)
    inv = 1.0 / acc[:, LANES:]
    o_ref[...] = unstack_heads(acc[:, :LANES] * inv, places, tiles, bq).astype(BF16)
    linv_ref[...] = unstack_heads(inv, places, tiles, bq)

def attn_fwd(length, q, k, v, heads, group, bq=256, bk=256):
    rows, width = q.shape
    tiles = width // LANES
    places = head_places(heads, group)
    return pl.pallas_call(
        functools.partial(fwd_kernel, places, tiles, bq, bk),
        out_shape=(jax.ShapeDtypeStruct((rows, width), BF16), jax.ShapeDtypeStruct((rows, width), F32)),
        grid_spec=pltpu.PrefetchScalarGridSpec(
            num_scalar_prefetch=1, grid=(rows // bq,),
            in_specs=[pl.BlockSpec((bq, width), lambda i, n: (i, 0)),
                      pl.BlockSpec((rows, LANES), lambda i, n: (0, 0)),
                      pl.BlockSpec((rows, LANES), lambda i, n: (0, 0))],
            out_specs=[pl.BlockSpec((bq, width), lambda i, n: (i, 0))] * 2,
            scratch_shapes=[pltpu.VMEM((heads * bq, LANES), BF16), pltpu.VMEM((rows, 2 * LANES), BF16),
                            pltpu.VMEM((heads * bq, 2 * LANES), F32)]),
        compiler_params=pltpu.CompilerParams(dimension_semantics=("arbitrary",), vmem_limit_bytes=48 << 20),
        cost_estimate=pl.CostEstimate(flops=heads * rows * rows * 2 * LANES, transcendentals=heads * rows * rows // 2, bytes_accessed=rows * width * 8),
        name="attention_forward",
    )(length, q, k, v)

def bwd_kernel(places, tiles, bq, bk, len_ref, q_ref, do_ref, o_ref, linv_ref, k_ref, v_ref, dq_ref, dk_ref, dv_ref, q6, do6, d_row, kx, dq6):
    i = pl.program_id(0)
    rows = k_ref.shape[0]
    heads = len(places)
    @pl.when(i == 0)
    def _():
        live = lax.broadcasted_iota(jnp.int32, (rows, LANES), 0) < len_ref[0]
        kx[...] = jnp.where(live, k_ref[...].astype(F32), 0.0).astype(BF16)
        dk_ref[...] = jnp.zeros_like(dk_ref)
        dv_ref[...] = jnp.zeros_like(dv_ref)
    q6[...] = stack_heads(q_ref[...].astype(F32), places).astype(BF16)
    dob = do_ref[...].astype(F32) * linv_ref[...]
    do6[...] = stack_heads(dob, places).astype(BF16)
    prod = stack_heads(dob * o_ref[...].astype(F32), places)
    hi = prod.astype(BF16)
    lo = (prod - hi.astype(F32)).astype(BF16)
    ones = jnp.ones((16, LANES), BF16)
    d_row[...] = nt(ones, hi) + nt(ones, lo)
    dq6[...] = jnp.zeros_like(dq6)
    def step(j, masked):
        ks = pl.ds(pl.multiple_of(j * bk, bk), bk)
        st = nt(k_ref[ks, :], q6[...])
        pt = jnp.exp2(st * (SCALE * LOG2E))
        if masked:
            kp = j * bk + lax.broadcasted_iota(jnp.int32, st.shape, 0)
            qp = i * bq + (lax.broadcasted_iota(jnp.int32, st.shape, 1) & (bq - 1))
            pt = jnp.where(kp <= qp, pt, 0.0)
        dv_ref[ks, :] += nn(pt.astype(BF16), do6[...])
        dpt = nt(v_ref[ks, :], do6[...])
        dst = (pt * (dpt - d_row[0:1, :])).astype(BF16)
        dk_ref[ks, :] += nn(dst, q6[...])
        dq6[...] += tn(dst, kx[ks, :])
    full = (i * bq) // bk
    @pl.loop(0, full)
    def _(j): step(j, False)
    @pl.loop(full, full + max(bq // bk, 1))
    def _(j): step(j, True)
    dq_ref[...] = unstack_heads(dq6[...] * SCALE, places, tiles, bq)
    @pl.when(i == pl.num_programs(0) - 1)
    def _():
        live = lax.broadcasted_iota(jnp.int32, (rows, LANES), 0) < len_ref[0]
        dk_ref[...] = jnp.where(live, dk_ref[...] * SCALE, 0.0)
        dv_ref[...] = jnp.where(live, dv_ref[...], 0.0)

def attn_bwd(length, q, do, o, linv, k, v, heads, group, bq=256, bk=256):
    rows, width = q.shape
    tiles = width // LANES
    places = head_places(heads, group)
    blk = pl.BlockSpec((bq, width), lambda i, n: (i, 0))
    whole = pl.BlockSpec((rows, LANES), lambda i, n: (0, 0))
    return pl.pallas_call(
        functools.partial(bwd_kernel, places, tiles, bq, bk),
        out_shape=(jax.ShapeDtypeStruct((rows, width), F32), jax.ShapeDtypeStruct((rows, LANES), F32), jax.ShapeDtypeStruct((rows, LANES), F32)),
        grid_spec=pltpu.PrefetchScalarGridSpec(
            num_scalar_prefetch=1, grid=(rows // bq,),
            in_specs=[blk] * 4 + [whole] * 2,
            out_specs=[blk, whole, whole],
            scratch_shapes=[pltpu.VMEM((heads * bq, LANES), BF16), pltpu.VMEM((heads * bq, LANES), BF16),
                            pltpu.VMEM((16, heads * bq), F32), pltpu.VMEM((rows, LANES), BF16),
                            pltpu.VMEM((heads * bq, LANES), F32)]),
        compiler_params=pltpu.CompilerParams(dimension_semantics=("arbitrary",), vmem_limit_bytes=48 << 20),
        cost_estimate=pl.CostEstimate(flops=heads * rows * rows * 5 * LANES, transcendentals=heads * rows * rows // 2, bytes_accessed=rows * width * 14),
        name="attention_backward",
    )(length, q, do, o, linv, k, v)


EPSILON = 1e-05
ROPE_BASE = 1000000.0


def rms_scale(inputs, gain_vec):
    return (
        inputs * lax.rsqrt(jnp.mean(inputs * inputs, axis=-1, keepdims=True) + EPSILON) * gain_vec
    )


def rotary(inputs, head_count):
    row_count = inputs.shape[0]
    half_dim = HEAD_SIZE // 2
    positions = jnp.arange(row_count).astype(jnp.float32)[:, None]
    inv_freq = jnp.exp(
        jnp.arange(half_dim).astype(jnp.float32) * (-2.0 * math.log(ROPE_BASE) / HEAD_SIZE)
    )
    angles = positions * inv_freq[None, :]
    cosine = jnp.cos(angles)[:, None, :]
    sine_tab = jnp.sin(angles)[:, None, :]
    split_heads = inputs.reshape(row_count, head_count, HEAD_SIZE)
    lower_half = split_heads[..., :half_dim]
    upper_half = split_heads[..., half_dim:]
    turned = jnp.concatenate(
        [lower_half * cosine - upper_half * sine_tab, upper_half * cosine + lower_half * sine_tab],
        axis=-1,
    )
    return turned.reshape(row_count, head_count * HEAD_SIZE)


def head_norm(inputs, gain_vec, head_count):
    row_count = inputs.shape[0]
    return rms_scale(inputs.reshape(row_count, head_count, HEAD_SIZE), gain_vec).reshape(
        row_count, head_count * HEAD_SIZE
    )


def prepare(queries, keys_val, q_gain, k_gain):
    q_count = queries.shape[1] // HEAD_SIZE
    kv_count = keys_val.shape[1] // HEAD_SIZE
    return (
        rotary(head_norm(queries, q_gain, q_count), q_count),
        rotary(head_norm(keys_val, k_gain, kv_count), kv_count),
    )


def swiglu(gate_val, up_val):
    return gate_val * jax.nn.sigmoid(gate_val) * up_val


def left_dot(left, right):
    return lax.dot_general(
        left, right, (((0,), (0,)), ((), ())), preferred_element_type=jnp.float32
    )


def right_dot(left, right):
    return lax.dot_general(
        left, right, (((1,), (1,)), ((), ())), preferred_element_type=jnp.float32
    )


def to_lanes(x):
    short = -x.shape[1] % LANES
    return x if short == 0 else jnp.pad(x, ((0, 0), (0, short)))


def on_device(
    tokens,
    lengths,
    cotangent,
    norm_gain,
    query_w,
    key_weight,
    value_weight,
    out_w,
    query_gain,
    key_gain,
    mlp_gain,
    gate_w,
    up_w,
    down_w,
):
    row_count = tokens.shape[0]
    length = lengths[0]
    live_rows = (jnp.arange(row_count, dtype=jnp.int32) < length).astype(jnp.float32)
    inputs = tokens.astype(jnp.float32)
    normed, norm_pull = jax.vjp(rms_scale, inputs, norm_gain)
    normed_b = normed.astype(jnp.bfloat16)
    queries = jnp.dot(normed_b, query_w, preferred_element_type=jnp.float32)
    keys_val = jnp.dot(normed_b, key_weight, preferred_element_type=jnp.float32)
    values_b = jnp.dot(normed_b, value_weight, preferred_element_type=jnp.float32).astype(
        jnp.bfloat16
    )
    (query_r, keys_r), prep_pull = jax.vjp(prepare, queries, keys_val, query_gain, key_gain)
    kv_count = key_weight.shape[1] // HEAD_SIZE
    q_width = query_w.shape[1]
    k_width = key_weight.shape[1]
    heads = q_width // HEAD_SIZE
    group_size = heads // kv_count
    q_pad = to_lanes(query_r.astype(jnp.bfloat16))
    k_pad = to_lanes(keys_r.astype(jnp.bfloat16))
    v_pad = to_lanes(values_b)
    mixed_pad, inverse_sums = attn_fwd(
        lengths, q_pad, k_pad, v_pad, heads, group_size, min(row_count, 512), min(row_count, 512)
    )
    mixed_b = mixed_pad[:, :q_width]
    attn_out = lax.psum(
        jnp.dot(mixed_b, out_w, preferred_element_type=jnp.float32).astype(jnp.bfloat16), "tensor"
    ).astype(jnp.float32)
    residual = inputs + attn_out
    normed2, norm2_pull = jax.vjp(rms_scale, residual, mlp_gain)
    normed2_b = normed2.astype(jnp.bfloat16)
    gate_val = jnp.dot(normed2_b, gate_w, preferred_element_type=jnp.float32)
    up_val = jnp.dot(normed2_b, up_w, preferred_element_type=jnp.float32)
    hidden, glu_pull = jax.vjp(swiglu, gate_val, up_val)
    hidden_b = hidden.astype(jnp.bfloat16)
    mlp_out = lax.psum(
        jnp.dot(hidden_b, down_w, preferred_element_type=jnp.float32).astype(jnp.bfloat16), "tensor"
    ).astype(jnp.float32)
    block_out = (residual + mlp_out).astype(jnp.bfloat16)
    d_out = cotangent.astype(jnp.float32) * live_rows[:, None]
    d_out_b = d_out.astype(jnp.bfloat16)
    d_down = left_dot(hidden_b, d_out_b)
    d_hidden = right_dot(d_out_b, down_w)
    d_gate, d_up = glu_pull(d_hidden)
    d_gate_b = d_gate.astype(jnp.bfloat16)
    d_up_b = d_up.astype(jnp.bfloat16)
    d_gate_w = left_dot(normed2_b, d_gate_b)
    d_up_w = left_dot(normed2_b, d_up_b)
    d_normed2 = lax.psum(
        (right_dot(d_gate_b, gate_w) + right_dot(d_up_b, up_w)).astype(jnp.bfloat16), "tensor"
    ).astype(jnp.float32)
    d_resid_norm, d_mlp_gain = norm2_pull(d_normed2)
    d_resid = d_out + d_resid_norm
    d_resid_b = d_resid.astype(jnp.bfloat16)
    output_weight_cotangent = left_dot(mixed_b, d_resid_b)
    d_mixed = right_dot(d_resid_b, out_w).astype(jnp.bfloat16)
    d_query_r, d_keys_r, d_values = attn_bwd(
        lengths, q_pad, to_lanes(d_mixed), mixed_pad, inverse_sums, k_pad, v_pad, heads, group_size
    )
    d_query_r = d_query_r[:, :q_width]
    d_keys_r = d_keys_r[:, :k_width]
    d_values_b = d_values[:, :k_width].astype(jnp.bfloat16)
    d_query_f, d_keys_f, d_qgain, d_kgain = prep_pull((d_query_r, d_keys_r))
    d_query_b = d_query_f.astype(jnp.bfloat16)
    d_keys_b = d_keys_f.astype(jnp.bfloat16)
    d_query_w = left_dot(normed_b, d_query_b)
    d_key_w = left_dot(normed_b, d_keys_b)
    d_value_w = left_dot(normed_b, d_values_b)
    d_normed = lax.psum(
        (
            right_dot(d_query_b, query_w)
            + right_dot(d_keys_b, key_weight)
            + right_dot(d_values_b, value_weight)
        ).astype(jnp.bfloat16),
        "tensor",
    ).astype(jnp.float32)
    d_input_norm, norm_gain_cotangent = norm_pull(d_normed)
    d_inputs = d_resid + d_input_norm
    head_totals = lax.psum((d_qgain, d_kgain), ("dp", "tensor"))
    all_totals = (
        lax.psum(norm_gain_cotangent.astype(jnp.bfloat16), "dp").astype(jnp.float32),
        lax.psum(d_query_w.astype(jnp.bfloat16), "dp").astype(jnp.float32),
        lax.psum(d_key_w.astype(jnp.bfloat16), "dp").astype(jnp.float32),
        lax.psum(d_value_w.astype(jnp.bfloat16), "dp").astype(jnp.float32),
        lax.psum(output_weight_cotangent.astype(jnp.bfloat16), "dp").astype(jnp.float32),
        lax.psum(d_gate_w.astype(jnp.bfloat16), "dp").astype(jnp.float32),
        lax.psum(d_up_w.astype(jnp.bfloat16), "dp").astype(jnp.float32),
        lax.psum(d_down.astype(jnp.bfloat16), "dp").astype(jnp.float32),
        lax.psum(d_mlp_gain.astype(jnp.bfloat16), "dp").astype(jnp.float32),
    )
    g_norm, g_query, g_key, g_value, g_out, g_gate, g_up, g_down, g_mlp = all_totals
    return (
        block_out,
        d_inputs,
        g_norm,
        g_query,
        g_key,
        g_value,
        g_out,
        head_totals[0],
        head_totals[1],
        g_mlp,
        g_gate,
        g_up,
        g_down,
    )


def solution(mesh):
    return jax.shard_map(
        on_device,
        mesh=mesh,
        in_specs=(
            P("dp", None),
            P("dp"),
            P("dp", None),
            P(),
            P(None, "tensor"),
            P(None, "tensor"),
            P(None, "tensor"),
            P("tensor", None),
            P(),
            P(),
            P(),
            P(None, "tensor"),
            P(None, "tensor"),
            P("tensor", None),
        ),
        out_specs=(
            P("dp", None),
            P("dp", None),
            P(),
            P(None, "tensor"),
            P(None, "tensor"),
            P(None, "tensor"),
            P("tensor", None),
            P(),
            P(),
            P(),
            P(None, "tensor"),
            P(None, "tensor"),
            P("tensor", None),
        ),
        check_vma=False,
    )
```

```python
import functools
import math

import jax
import jax.numpy as jnp
from jax import lax
from jax.experimental import pallas as pl
from jax.experimental.pallas import tpu as pltpu
from jax.sharding import PartitionSpec as P

HEAD_SIZE = 64
LANES = 128
SCALE = HEAD_SIZE**-0.5
LOG2E = math.log2(math.e)
EPSILON = 1e-05
ROPE_BASE = 1000000.0
PIECES = 8
F32 = jnp.float32
BF16 = jnp.bfloat16
MESH = pl.DeviceIdType.MESH


def nt(a,b): return lax.dot_general(a,b,(((1,),(1,)),((),())),preferred_element_type=F32)
def tn(a,b): return lax.dot_general(a,b,(((0,),(0,)),((),())),preferred_element_type=F32)
def nn(a,b): return lax.dot_general(a,b,(((1,),(0,)),((),())),preferred_element_type=F32)

def head_places(heads, group):
    return [(h // 2, h % 2, h // group) for h in range(heads)]

def half_mask(half, dtype=F32):
    lane = lax.broadcasted_iota(jnp.int32, (1, LANES), 1)
    keep = lane < HEAD_SIZE if half == 0 else lane >= HEAD_SIZE
    return keep

def stack_heads(x, places):
    out = []
    for tile, half, kv in places:
        piece = x[:, tile * LANES:(tile + 1) * LANES]
        if half != kv:
            piece = pltpu.roll(piece, HEAD_SIZE, 1)
        out.append(jnp.where(half_mask(kv), piece, 0.0))
    return jnp.concatenate(out, axis=0)

def unstack_heads(x, places, tiles, n):
    pieces = {}
    for h, (tile, half, kv) in enumerate(places):
        piece = x[h * n:(h + 1) * n]
        if half != kv:
            piece = pltpu.roll(piece, HEAD_SIZE, 1)
        pieces[tile, half] = piece
    out = []
    for tile in range(tiles):
        low = pieces[tile, 0]
        high = pieces.get((tile, 1))
        out.append(jnp.where(half_mask(0), low, 0.0 if high is None else high))
    return jnp.concatenate(out, axis=1)

def fwd_kernel(places, tiles, bq, bk, len_ref, q_ref, k_ref, v_ref, o_ref, linv_ref, q6, vx, acc):
    i = pl.program_id(0)
    heads = len(places)
    rows = k_ref.shape[0]
    @pl.when(i == 0)
    def _():
        live = lax.broadcasted_iota(jnp.int32, (rows, LANES), 0) < len_ref[0]
        vx[:, :LANES] = jnp.where(live, v_ref[...].astype(F32), 0.0).astype(BF16)
        vx[:, LANES:] = jnp.where(live, 1.0, 0.0).astype(BF16)
    q6[...] = stack_heads(q_ref[...].astype(F32), places).astype(BF16)
    acc[...] = jnp.zeros_like(acc)
    def step(j, masked):
        ks = pl.ds(pl.multiple_of(j * bk, bk), bk)
        s = nt(q6[...], k_ref[ks, :])
        p = jnp.exp2(s * (SCALE * LOG2E))
        if masked:
            qp = i * bq + (lax.broadcasted_iota(jnp.int32, s.shape, 0) & (bq - 1))
            kp = j * bk + lax.broadcasted_iota(jnp.int32, s.shape, 1)
            p = jnp.where(kp <= qp, p, 0.0)
        acc[...] += nn(p.astype(BF16), vx[ks, :])
    full = (i * bq) // bk
    @pl.loop(0, full)
    def _(j): step(j, False)
    @pl.loop(full, full + max(bq // bk, 1))
    def _(j): step(j, True)
    inv = 1.0 / acc[:, LANES:]
    o_ref[...] = unstack_heads(acc[:, :LANES] * inv, places, tiles, bq).astype(BF16)
    linv_ref[...] = unstack_heads(inv, places, tiles, bq)

def attn_fwd(length, q, k, v, heads, group, bq=256, bk=256):
    rows, width = q.shape
    tiles = width // LANES
    places = head_places(heads, group)
    return pl.pallas_call(
        functools.partial(fwd_kernel, places, tiles, bq, bk),
        out_shape=(jax.ShapeDtypeStruct((rows, width), BF16), jax.ShapeDtypeStruct((rows, width), F32)),
        grid_spec=pltpu.PrefetchScalarGridSpec(
            num_scalar_prefetch=1, grid=(rows // bq,),
            in_specs=[pl.BlockSpec((bq, width), lambda i, n: (i, 0)),
                      pl.BlockSpec((rows, LANES), lambda i, n: (0, 0)),
                      pl.BlockSpec((rows, LANES), lambda i, n: (0, 0))],
            out_specs=[pl.BlockSpec((bq, width), lambda i, n: (i, 0))] * 2,
            scratch_shapes=[pltpu.VMEM((heads * bq, LANES), BF16), pltpu.VMEM((rows, 2 * LANES), BF16),
                            pltpu.VMEM((heads * bq, 2 * LANES), F32)]),
        compiler_params=pltpu.CompilerParams(dimension_semantics=("arbitrary",), vmem_limit_bytes=48 << 20),
        cost_estimate=pl.CostEstimate(flops=heads * rows * rows * 2 * LANES, transcendentals=heads * rows * rows // 2, bytes_accessed=rows * width * 8),
        name="attention_forward",
    )(length, q, k, v)

def bwd_kernel(places, tiles, bq, bk, len_ref, q_ref, do_ref, o_ref, linv_ref, k_ref, v_ref, dq_ref, dk_ref, dv_ref, q6, do6, d_row, kx, dq6):
    i = pl.program_id(0)
    rows = k_ref.shape[0]
    heads = len(places)
    @pl.when(i == 0)
    def _():
        live = lax.broadcasted_iota(jnp.int32, (rows, LANES), 0) < len_ref[0]
        kx[...] = jnp.where(live, k_ref[...].astype(F32), 0.0).astype(BF16)
        dk_ref[...] = jnp.zeros_like(dk_ref)
        dv_ref[...] = jnp.zeros_like(dv_ref)
    q6[...] = stack_heads(q_ref[...].astype(F32), places).astype(BF16)
    dob = do_ref[...].astype(F32) * linv_ref[...]
    do6[...] = stack_heads(dob, places).astype(BF16)
    prod = stack_heads(dob * o_ref[...].astype(F32), places)
    hi = prod.astype(BF16)
    lo = (prod - hi.astype(F32)).astype(BF16)
    ones = jnp.ones((16, LANES), BF16)
    d_row[...] = nt(ones, hi) + nt(ones, lo)
    dq6[...] = jnp.zeros_like(dq6)
    def step(j, masked):
        ks = pl.ds(pl.multiple_of(j * bk, bk), bk)
        st = nt(k_ref[ks, :], q6[...])
        pt = jnp.exp2(st * (SCALE * LOG2E))
        if masked:
            kp = j * bk + lax.broadcasted_iota(jnp.int32, st.shape, 0)
            qp = i * bq + (lax.broadcasted_iota(jnp.int32, st.shape, 1) & (bq - 1))
            pt = jnp.where(kp <= qp, pt, 0.0)
        dv_ref[ks, :] += nn(pt.astype(BF16), do6[...])
        dpt = nt(v_ref[ks, :], do6[...])
        dst = (pt * (dpt - d_row[0:1, :])).astype(BF16)
        dk_ref[ks, :] += nn(dst, q6[...])
        dq6[...] += tn(dst, kx[ks, :])
    full = (i * bq) // bk
    @pl.loop(0, full)
    def _(j): step(j, False)
    @pl.loop(full, full + max(bq // bk, 1))
    def _(j): step(j, True)
    dq_ref[...] = unstack_heads(dq6[...] * SCALE, places, tiles, bq)
    @pl.when(i == pl.num_programs(0) - 1)
    def _():
        live = lax.broadcasted_iota(jnp.int32, (rows, LANES), 0) < len_ref[0]
        dk_ref[...] = jnp.where(live, dk_ref[...] * SCALE, 0.0)
        dv_ref[...] = jnp.where(live, dv_ref[...], 0.0)

def attn_bwd(length, q, do, o, linv, k, v, heads, group, bq=256, bk=256):
    rows, width = q.shape
    tiles = width // LANES
    places = head_places(heads, group)
    blk = pl.BlockSpec((bq, width), lambda i, n: (i, 0))
    whole = pl.BlockSpec((rows, LANES), lambda i, n: (0, 0))
    return pl.pallas_call(
        functools.partial(bwd_kernel, places, tiles, bq, bk),
        out_shape=(jax.ShapeDtypeStruct((rows, width), F32), jax.ShapeDtypeStruct((rows, LANES), F32), jax.ShapeDtypeStruct((rows, LANES), F32)),
        grid_spec=pltpu.PrefetchScalarGridSpec(
            num_scalar_prefetch=1, grid=(rows // bq,),
            in_specs=[blk] * 4 + [whole] * 2,
            out_specs=[blk, whole, whole],
            scratch_shapes=[pltpu.VMEM((heads * bq, LANES), BF16), pltpu.VMEM((heads * bq, LANES), BF16),
                            pltpu.VMEM((16, heads * bq), F32), pltpu.VMEM((rows, LANES), BF16),
                            pltpu.VMEM((heads * bq, LANES), F32)]),
        compiler_params=pltpu.CompilerParams(dimension_semantics=("arbitrary",), vmem_limit_bytes=48 << 20),
        cost_estimate=pl.CostEstimate(flops=heads * rows * rows * 5 * LANES, transcendentals=heads * rows * rows // 2, bytes_accessed=rows * width * 14),
        name="attention_backward",
    )(length, q, do, o, linv, k, v)


def line_copy(src, dst, sems, where, to):
    return pltpu.make_async_remote_copy(
        src_ref=src,
        dst_ref=dst,
        send_sem=sems[0].at[where],
        recv_sem=sems[1].at[where],
        device_id={"tensor": to},
        device_id_type=MESH,
    )


def greet_line(count):
    me = lax.axis_index("tensor")
    barrier = pltpu.get_barrier_semaphore()

    @pl.when(me > 0)
    def _():
        pl.semaphore_signal(barrier, inc=1, device_id={"tensor": me - 1}, device_id_type=MESH)

    @pl.when(me < count - 1)
    def _():
        pl.semaphore_signal(barrier, inc=1, device_id={"tensor": me + 1}, device_id_type=MESH)

    @pl.when((me > 0) & (me < count - 1))
    def _():
        pl.semaphore_wait(barrier, 2)

    @pl.when((me == 0) | (me == count - 1))
    def _():
        pl.semaphore_wait(barrier, 1)


def line_sum_kernel(
    count, pieces, finish, kinds, part_ref, *refs
):
    (own_refs, full_ref, out_refs), scratch = split_refs(refs, kinds)
    up_buf, down_buf, acc = scratch[:3]
    sems = scratch[3:]
    sum_up, sum_down, give_up, give_down = (sems[0:2], sems[2:4], sems[4:6], sems[6:8])
    me = lax.axis_index("tensor")
    last = count - 1
    own = part_ref.shape[0] // count
    size = own // pieces

    def rows(block, c):
        return pl.ds(pl.multiple_of(block * own + c * size, size), size)

    def sum_copy(c, s, upward):
        buf, sem = (up_buf, sum_up) if upward else (down_buf, sum_down)
        to = me + 1 if upward else me - 1
        return buf, lambda src: line_copy(src, buf.at[c, s - 1], sem, (c, s - 1), to)

    def sum_start(c, s, upward):
        buf, copy = sum_copy(c, s, upward)
        first = me == 0 if upward else me == last
        block = count - s + me if upward else me - (count - s)
        sends = me <= s - 1 if upward else me >= count - s
        sends = sends & (me < last if upward else me > 0)

        @pl.when(sends & first)
        def _():
            copy(part_ref.at[rows(block, c)]).start()

        if s > 1:

            @pl.when(sends & jnp.logical_not(first))
            def _():
                sum_wait(c, s - 1, upward)
                held = buf.at[c, s - 2]
                held[...] = (held[...].astype(F32) + part_ref[rows(block, c), :].astype(F32)).astype(BF16)
                copy(held).start()

    def sum_wait(c, s, upward):
        buf, copy = sum_copy(c, s, upward)
        copy(buf.at[c, s - 1]).wait_recv()

    def give_copy(c, s, upward):
        block = me - s + 1 if upward else me + s - 1
        sem = give_up if upward else give_down
        place = full_ref.at[rows(block, c)]
        return line_copy(place, place, sem, (c, s - 1), me + 1 if upward else me - 1)

    def give_wait(c, s, upward):
        block = me - s if upward else me + s
        sem = give_up if upward else give_down
        place = full_ref.at[rows(block, c)]
        line_copy(place, place, sem, (c, s - 1), me + 1 if upward else me - 1).wait_recv()

    def give_start(c, s, upward):
        sends = (me >= s - 1) & (me < last) if upward else (me > 0) & (me <= count - s)
        if s > 1:
            got = (me >= s - 1) if upward else (me <= count - s)

            @pl.when(got)
            def _():
                give_wait(c, s - 1, upward)

        @pl.when(sends)
        def _():
            give_copy(c, s, upward).start()

    def settle(c):
        acc[...] = part_ref[rows(me, c), :].astype(F32)

        @pl.when(me > 0)
        def _():
            sum_wait(c, last, True)
            acc[...] += up_buf[c, last - 1].astype(F32)

        @pl.when(me < last)
        def _():
            sum_wait(c, last, False)
            acc[...] += down_buf[c, last - 1].astype(F32)

        mine = pl.ds(c * size, size)
        full_ref[rows(me, c), :] = finish(c, mine, acc[...], own_refs, out_refs)

    greet_line(count)
    for slot in range(pieces + 2 * last):
        if slot < pieces:
            for upward in (True, False):
                sum_start(slot, 1, upward)
        for s in range(last, 1, -1):
            c = slot - last - (s - 1)
            if 0 <= c < pieces:
                for upward in (True, False):
                    give_start(c, s, upward)
        c = slot - last
        if 0 <= c < pieces:
            settle(c)
            for upward in (True, False):
                give_start(c, 1, upward)
        for s in range(last, 1, -1):
            c = slot - (s - 1)
            if 0 <= c < pieces:
                for upward in (True, False):
                    sum_start(c, s, upward)
    for c in range(pieces):

        @pl.when(me == last)
        def _():
            give_wait(c, last, True)

        @pl.when(me == 0)
        def _():
            give_wait(c, last, False)

        for s in range(1, count):
            for upward in (True, False):
                sends = me <= s - 1 if upward else me >= count - s
                sends = sends & (me < last if upward else me > 0)

                @pl.when(sends)
                def _():
                    buf, copy = sum_copy(c, s, upward)
                    copy(buf.at[c, s - 1]).wait_send()

                sends = (me >= s - 1) & (me < last) if upward else (me > 0) & (me <= count - s)

                @pl.when(sends)
                def _():
                    give_copy(c, s, upward).wait_send()


def split_refs(refs, kinds):
    n_own, n_out = kinds
    own_refs = refs[:n_own]
    full_ref = refs[n_own]
    out_refs = refs[n_own + 1 : n_own + 1 + n_out]
    return (own_refs, full_ref, out_refs), refs[n_own + 1 + n_out :]


def line_sum(part, owned, outs, finish, pieces, collective_id):
    count = lax.axis_size("tensor")
    rows, width = part.shape
    size = rows // count // pieces
    vmem = pl.BlockSpec(memory_space=pltpu.VMEM)
    hops = (pieces, count - 1)
    return pl.pallas_call(
        functools.partial(line_sum_kernel, count, pieces, finish, (len(owned), len(outs))),
        out_shape=(jax.ShapeDtypeStruct((rows, width), BF16), *outs),
        in_specs=[vmem] * (1 + len(owned)),
        out_specs=(vmem,) * (1 + len(outs)),
        scratch_shapes=[
            pltpu.VMEM((*hops, size, width), BF16),
            pltpu.VMEM((*hops, size, width), BF16),
            pltpu.VMEM((size, width), F32),
        ]
        + [pltpu.SemaphoreType.DMA(hops)] * 8,
        compiler_params=pltpu.CompilerParams(
            collective_id=collective_id, has_side_effects=True, vmem_limit_bytes=56 << 20
        ),
        cost_estimate=pl.CostEstimate(
            flops=rows * width * 8, transcendentals=0, bytes_accessed=rows * width * 8
        ),
        name="line_sum",
    )(part, *owned)


def finish_attention(c, mine, total, own_refs, out_refs):
    inputs, gain = own_refs
    resid = inputs[mine, :] + total
    out_refs[0][mine, :] = resid
    return (resid * inverse_rms(resid) * gain[...]).astype(BF16)


def finish_back(c, mine, total, own_refs, out_refs):
    base, value, gain = own_refs
    x = value[mine, :]
    r = inverse_rms(x)
    y = x * r
    e = gain[...] * total
    out = base[mine, :] + r * (e - y * jnp.mean(e * y, axis=-1, keepdims=True))
    out_refs[0][mine, :] = out
    term = jnp.sum(total * y, axis=0, keepdims=True)
    if c == 0:
        out_refs[1][...] = term
    else:
        out_refs[1][...] += term
    return out.astype(BF16)


def finish_add(c, mine, total, own_refs, out_refs):
    return (own_refs[0][mine, :] + total).astype(BF16)


def inverse_rms(x):
    return lax.rsqrt(jnp.mean(x * x, axis=-1, keepdims=True) + EPSILON)


def norm_back(x, r, gain, grad):
    y = x * r
    e = gain * grad
    return r * (e - y * jnp.mean(e * y, axis=-1, keepdims=True)), jnp.sum(grad * y, axis=0)


def rope_tables(row_count):
    half = HEAD_SIZE // 2
    positions = jnp.arange(row_count).astype(F32)[:, None]
    freq = jnp.exp(jnp.arange(half).astype(F32) * (-2.0 * math.log(ROPE_BASE) / HEAD_SIZE))
    angles = positions * freq[None, :]
    return jnp.cos(angles)[:, None, :], jnp.sin(angles)[:, None, :]


def turn(x, cosine, sine):
    half = HEAD_SIZE // 2
    low, high = x[..., :half], x[..., half:]
    return jnp.concatenate([low * cosine - high * sine, high * cosine + low * sine], axis=-1)


def by_head(x):
    return x.reshape(x.shape[0], x.shape[1] // HEAD_SIZE, HEAD_SIZE)


def flat(x):
    return x.reshape(x.shape[0], x.shape[1] * x.shape[2])


def prepare(x, gain, tables):
    heads = by_head(x)
    return flat(turn(heads * inverse_rms(heads) * gain, *tables))


def prepare_back(x, gain, tables, grad):
    heads = by_head(x)
    back = turn(by_head(grad), tables[0], -tables[1])
    dx, d_gain = norm_back(heads, inverse_rms(heads), gain, back)
    return flat(dx), jnp.sum(d_gain, axis=0)


def to_lanes(x):
    short = -x.shape[1] % LANES
    return x if short == 0 else jnp.pad(x, ((0, 0), (0, short)))


def on_device(
    tokens,
    lengths,
    cotangent,
    norm_gain,
    query_w,
    key_weight,
    value_weight,
    out_w,
    query_gain,
    key_gain,
    mlp_gain,
    gate_w,
    up_w,
    down_w,
):
    row_count, width = tokens.shape
    me = lax.axis_index("tensor")
    count = lax.axis_size("tensor")
    m = row_count // count
    q_width = query_w.shape[1]
    k_width = key_weight.shape[1]
    heads = q_width // HEAD_SIZE
    group = q_width // k_width
    own_shape = jax.ShapeDtypeStruct((m, width), F32)
    gain_shape = jax.ShapeDtypeStruct((1, width), F32)

    def own(x):
        return lax.dynamic_slice_in_dim(x, me * m, m, axis=0)

    live = (jnp.arange(row_count, dtype=jnp.int32) < lengths[0])[:, None]
    d_out = jnp.where(live, cotangent, jnp.zeros_like(cotangent))
    inputs = tokens.astype(F32)
    normed = (inputs * inverse_rms(inputs) * norm_gain).astype(BF16)
    inputs_own = own(tokens).astype(F32)
    queries = nn(normed, query_w)
    keys_val = nn(normed, key_weight)
    tables = rope_tables(row_count)
    q_pad = to_lanes(prepare(queries, query_gain, tables).astype(BF16))
    k_pad = to_lanes(prepare(keys_val, key_gain, tables).astype(BF16))
    v_pad = to_lanes(nn(normed, value_weight).astype(BF16))
    mixed_pad, inverse_sums = attn_fwd(lengths, q_pad, k_pad, v_pad, heads, group, 512, 512)
    mixed = mixed_pad[:, :q_width]

    normed2, resid_own = line_sum(
        nn(mixed, out_w).astype(BF16),
        (inputs_own, mlp_gain[None]),
        (own_shape,),
        finish_attention,
        PIECES,
        1,
    )
    gate = nn(normed2, gate_w)
    up = nn(normed2, up_w)
    sig = jax.nn.sigmoid(gate)
    hidden = (gate * sig * up).astype(BF16)
    d_hidden = nt(d_out, down_w)
    d_gate = (d_hidden * up * sig * (1.0 + gate * (1.0 - sig))).astype(BF16)
    d_up = (d_hidden * gate * sig).astype(BF16)
    d_normed2 = (nt(d_gate, gate_w) + nt(d_up, up_w)).astype(BF16)
    mlp_own = lax.psum_scatter(
        nn(hidden, down_w).astype(BF16), "tensor", scatter_dimension=0, tiled=True
    )
    block_out = lax.all_gather(
        (resid_own + mlp_own.astype(F32)).astype(BF16), "tensor", axis=0, tiled=True
    )
    d_resid, d_resid_own, d_mlp_gain = line_sum(
        d_normed2,
        (own(d_out).astype(F32), resid_own, mlp_gain[None]),
        (own_shape, gain_shape),
        finish_back,
        PIECES,
        2,
    )
    g_gate = tn(normed2, d_gate).astype(BF16)
    g_up = tn(normed2, d_up).astype(BF16)
    g_down = tn(hidden, d_out).astype(BF16)
    g_gate, g_up, g_down = lax.psum((g_gate, g_up, g_down), "dp")

    d_mixed = nt(d_resid, out_w).astype(BF16)
    dq, dk, dv = attn_bwd(
        lengths, q_pad, to_lanes(d_mixed), mixed_pad, inverse_sums, k_pad, v_pad, heads, group
    )
    dq, d_qgain = prepare_back(queries, query_gain, tables, dq[:, :q_width])
    dk, d_kgain = prepare_back(keys_val, key_gain, tables, dk[:, :k_width])
    d_q, d_k, d_v = dq.astype(BF16), dk.astype(BF16), dv[:, :k_width].astype(BF16)
    d_normed = (nt(d_q, query_w) + nt(d_k, key_weight) + nt(d_v, value_weight)).astype(BF16)
    d_inputs, _, d_norm_gain = line_sum(
        d_normed,
        (d_resid_own, inputs_own, norm_gain[None]),
        (own_shape, gain_shape),
        finish_back,
        PIECES,
        3,
    )
    g_out = tn(mixed, d_resid).astype(BF16)
    g_query = tn(normed, d_q).astype(BF16)
    g_key = tn(normed, d_k).astype(BF16)
    g_value = tn(normed, d_v).astype(BF16)
    g_out, g_query, g_key, g_value, g_gate, g_up, g_down = lax.optimization_barrier(
        (g_out, g_query, g_key, g_value, g_gate, g_up, g_down)
    )
    g_out, g_query, g_key, g_value = lax.psum((g_out, g_query, g_key, g_value), "dp")
    g_norm, g_mlp, g_qgain, g_kgain = lax.psum(
        (d_norm_gain[0], d_mlp_gain[0], d_qgain, d_kgain), ("dp", "tensor")
    )
    return (
        block_out,
        d_inputs.astype(F32),
        g_norm,
        g_query.astype(F32),
        g_key.astype(F32),
        g_value.astype(F32),
        g_out.astype(F32),
        g_qgain,
        g_kgain,
        g_mlp,
        g_gate.astype(F32),
        g_up.astype(F32),
        g_down.astype(F32),
    )


def solution(mesh):
    rows, whole = P("dp", None), P()
    columns, depth = P(None, "tensor"), P("tensor", None)
    return jax.shard_map(
        on_device,
        mesh=mesh,
        in_specs=(
            rows,
            P("dp"),
            rows,
            whole,
            columns,
            columns,
            columns,
            depth,
            whole,
            whole,
            whole,
            columns,
            columns,
            depth,
        ),
        out_specs=(
            rows,
            rows,
            whole,
            columns,
            columns,
            columns,
            depth,
            whole,
            whole,
            whole,
            columns,
            columns,
            depth,
        ),
        check_vma=False,
    )
```

```python
import functools
import math

import jax
import jax.numpy as jnp
from jax import lax
from jax.experimental import pallas as pl
from jax.experimental.pallas import tpu as pltpu
from jax.sharding import PartitionSpec as P

HEAD_SIZE = 64
LANES = 128
SCALE = HEAD_SIZE**-0.5
LOG2E = math.log2(math.e)
EPSILON = 1e-05
ROPE_BASE = 1000000.0
PIECES = 8
F32 = jnp.float32
BF16 = jnp.bfloat16
MESH = pl.DeviceIdType.MESH


def nt(a,b): return lax.dot_general(a,b,(((1,),(1,)),((),())),preferred_element_type=F32)
def tn(a,b): return lax.dot_general(a,b,(((0,),(0,)),((),())),preferred_element_type=F32)
def nn(a,b): return lax.dot_general(a,b,(((1,),(0,)),((),())),preferred_element_type=F32)

def head_places(heads, group):
    return [(h // 2, h % 2, h // group) for h in range(heads)]

def half_mask(half, dtype=F32):
    lane = lax.broadcasted_iota(jnp.int32, (1, LANES), 1)
    keep = lane < HEAD_SIZE if half == 0 else lane >= HEAD_SIZE
    return keep

def stack_heads(x, places):
    out = []
    for tile, half, kv in places:
        piece = x[:, tile * LANES:(tile + 1) * LANES]
        if half != kv:
            piece = pltpu.roll(piece, HEAD_SIZE, 1)
        out.append(jnp.where(half_mask(kv), piece, 0.0))
    return jnp.concatenate(out, axis=0)

def unstack_heads(x, places, tiles, n):
    pieces = {}
    for h, (tile, half, kv) in enumerate(places):
        piece = x[h * n:(h + 1) * n]
        if half != kv:
            piece = pltpu.roll(piece, HEAD_SIZE, 1)
        pieces[tile, half] = piece
    out = []
    for tile in range(tiles):
        low = pieces[tile, 0]
        high = pieces.get((tile, 1))
        out.append(jnp.where(half_mask(0), low, 0.0 if high is None else high))
    return jnp.concatenate(out, axis=1)

def bwd_kernel(places, tiles, bq, bk, len_ref, q_ref, do_ref, o_ref, linv_ref, k_ref, v_ref, dq_ref, dk_ref, dv_ref, q6, do6, d_row, kx, dq6):
    i = pl.program_id(0)
    rows = k_ref.shape[0]
    heads = len(places)
    @pl.when(i == 0)
    def _():
        live = lax.broadcasted_iota(jnp.int32, (rows, LANES), 0) < len_ref[0]
        kx[...] = jnp.where(live, k_ref[...].astype(F32), 0.0).astype(BF16)
        dk_ref[...] = jnp.zeros_like(dk_ref)
        dv_ref[...] = jnp.zeros_like(dv_ref)
    q6[...] = stack_heads(q_ref[...].astype(F32), places).astype(BF16)
    dob = do_ref[...].astype(F32) * linv_ref[...]
    do6[...] = stack_heads(dob, places).astype(BF16)
    prod = stack_heads(dob * o_ref[...].astype(F32), places)
    hi = prod.astype(BF16)
    lo = (prod - hi.astype(F32)).astype(BF16)
    ones = jnp.ones((16, LANES), BF16)
    d_row[...] = nt(ones, hi) + nt(ones, lo)
    dq6[...] = jnp.zeros_like(dq6)
    def step(j, masked):
        ks = pl.ds(pl.multiple_of(j * bk, bk), bk)
        st = nt(k_ref[ks, :], q6[...])
        pt = jnp.exp2(st * (SCALE * LOG2E))
        if masked:
            kp = j * bk + lax.broadcasted_iota(jnp.int32, st.shape, 0)
            qp = i * bq + (lax.broadcasted_iota(jnp.int32, st.shape, 1) & (bq - 1))
            pt = jnp.where(kp <= qp, pt, 0.0)
        dv_ref[ks, :] += nn(pt.astype(BF16), do6[...])
        dpt = nt(v_ref[ks, :], do6[...])
        dst = (pt * (dpt - d_row[0:1, :])).astype(BF16)
        dk_ref[ks, :] += nn(dst, q6[...])
        dq6[...] += tn(dst, kx[ks, :])
    full = (i * bq) // bk
    @pl.loop(0, full)
    def _(j): step(j, False)
    @pl.loop(full, full + max(bq // bk, 1))
    def _(j): step(j, True)
    dq_ref[...] = unstack_heads(dq6[...] * SCALE, places, tiles, bq)
    @pl.when(i == pl.num_programs(0) - 1)
    def _():
        live = lax.broadcasted_iota(jnp.int32, (rows, LANES), 0) < len_ref[0]
        dk_ref[...] = jnp.where(live, dk_ref[...] * SCALE, 0.0)
        dv_ref[...] = jnp.where(live, dv_ref[...], 0.0)

def attn_bwd(length, q, do, o, linv, k, v, heads, group, bq=256, bk=256):
    rows, width = q.shape
    tiles = width // LANES
    places = head_places(heads, group)
    blk = pl.BlockSpec((bq, width), lambda i, n: (i, 0))
    whole = pl.BlockSpec((rows, LANES), lambda i, n: (0, 0))
    return pl.pallas_call(
        functools.partial(bwd_kernel, places, tiles, bq, bk),
        out_shape=(jax.ShapeDtypeStruct((rows, width), F32), jax.ShapeDtypeStruct((rows, LANES), F32), jax.ShapeDtypeStruct((rows, LANES), F32)),
        grid_spec=pltpu.PrefetchScalarGridSpec(
            num_scalar_prefetch=1, grid=(rows // bq,),
            in_specs=[blk] * 4 + [whole] * 2,
            out_specs=[blk, whole, whole],
            scratch_shapes=[pltpu.VMEM((heads * bq, LANES), BF16), pltpu.VMEM((heads * bq, LANES), BF16),
                            pltpu.VMEM((16, heads * bq), F32), pltpu.VMEM((rows, LANES), BF16),
                            pltpu.VMEM((heads * bq, LANES), F32)]),
        compiler_params=pltpu.CompilerParams(dimension_semantics=("arbitrary",), vmem_limit_bytes=48 << 20),
        cost_estimate=pl.CostEstimate(flops=rows * width, transcendentals=0, bytes_accessed=rows * width * 2),
        name="attention_backward",
    )(length, q, do, o, linv, k, v)


def line_copy(src, dst, sems, where, to):
    return pltpu.make_async_remote_copy(
        src_ref=src,
        dst_ref=dst,
        send_sem=sems[0].at[where],
        recv_sem=sems[1].at[where],
        device_id={"tensor": to},
        device_id_type=MESH,
    )


def greet_line(count, everyone=False):
    me = lax.axis_index("tensor")
    barrier = pltpu.get_barrier_semaphore()

    def greet(peer):
        pl.semaphore_signal(barrier, inc=1, device_id={"tensor": peer}, device_id_type=MESH)

    if everyone:
        for peer in range(count):

            @pl.when(peer != me)
            def _():
                greet(peer)

        pl.semaphore_wait(barrier, count - 1)
        return

    @pl.when(me > 0)
    def _():
        greet(me - 1)

    @pl.when(me < count - 1)
    def _():
        greet(me + 1)

    @pl.when((me > 0) & (me < count - 1))
    def _():
        pl.semaphore_wait(barrier, 2)

    @pl.when((me == 0) | (me == count - 1))
    def _():
        pl.semaphore_wait(barrier, 1)


def line_sum_kernel(
    count, pieces, finish, kinds, share_terms, part_ref, *refs
):
    (own_refs, full_ref, out_refs), scratch = split_refs(refs, kinds)
    up_buf, down_buf, acc, shared = scratch[:4]
    sems = scratch[4:]
    sum_up, sum_down, give_up, give_down = (sems[0:2], sems[2:4], sems[4:6], sems[6:8])
    me = lax.axis_index("tensor")
    last = count - 1
    own = part_ref.shape[0] // count
    size = own // pieces

    def rows(block, c):
        return pl.ds(pl.multiple_of(block * own + c * size, size), size)

    def sum_copy(c, s, upward):
        buf, sem = (up_buf, sum_up) if upward else (down_buf, sum_down)
        to = me + 1 if upward else me - 1
        return buf, lambda src: line_copy(src, buf.at[c, s - 1], sem, (c, s - 1), to)

    def sum_start(c, s, upward):
        buf, copy = sum_copy(c, s, upward)
        first = me == 0 if upward else me == last
        block = count - s + me if upward else me - (count - s)
        sends = me <= s - 1 if upward else me >= count - s
        sends = sends & (me < last if upward else me > 0)

        @pl.when(sends & first)
        def _():
            copy(part_ref.at[rows(block, c)]).start()

        if s > 1:

            @pl.when(sends & jnp.logical_not(first))
            def _():
                sum_wait(c, s - 1, upward)
                held = buf.at[c, s - 2]
                held[...] = (held[...].astype(F32) + part_ref[rows(block, c), :].astype(F32)).astype(BF16)
                copy(held).start()

    def sum_wait(c, s, upward):
        buf, copy = sum_copy(c, s, upward)
        copy(buf.at[c, s - 1]).wait_recv()

    def give_copy(c, s, upward):
        block = me - s + 1 if upward else me + s - 1
        sem = give_up if upward else give_down
        place = full_ref.at[rows(block, c)]
        return line_copy(place, place, sem, (c, s - 1), me + 1 if upward else me - 1)

    def give_wait(c, s, upward):
        block = me - s if upward else me + s
        sem = give_up if upward else give_down
        place = full_ref.at[rows(block, c)]
        line_copy(place, place, sem, (c, s - 1), me + 1 if upward else me - 1).wait_recv()

    def give_start(c, s, upward):
        sends = (me >= s - 1) & (me < last) if upward else (me > 0) & (me <= count - s)
        if s > 1:
            got = (me >= s - 1) if upward else (me <= count - s)

            @pl.when(got)
            def _():
                give_wait(c, s - 1, upward)

        @pl.when(sends)
        def _():
            give_copy(c, s, upward).start()

    def settle(c):
        acc[...] = part_ref[rows(me, c), :].astype(F32)

        @pl.when(me > 0)
        def _():
            sum_wait(c, last, True)
            acc[...] += up_buf[c, last - 1].astype(F32)

        @pl.when(me < last)
        def _():
            sum_wait(c, last, False)
            acc[...] += down_buf[c, last - 1].astype(F32)

        mine = pl.ds(c * size, size)
        full_ref[rows(me, c), :] = finish(c, mine, acc[...], own_refs, out_refs)

    def share(to):
        return pltpu.make_async_remote_copy(
            src_ref=out_refs[1],
            dst_ref=shared.at[me],
            send_sem=sems[8].at[to],
            recv_sem=sems[9].at[me],
            device_id={"tensor": to},
            device_id_type=MESH,
        )

    greet_line(count, share_terms)
    for slot in range(pieces + 2 * last):
        if slot < pieces:
            for upward in (True, False):
                sum_start(slot, 1, upward)
        for s in range(last, 1, -1):
            c = slot - last - (s - 1)
            if 0 <= c < pieces:
                for upward in (True, False):
                    give_start(c, s, upward)
        c = slot - last
        if 0 <= c < pieces:
            settle(c)
            for upward in (True, False):
                give_start(c, 1, upward)
            if share_terms and c == pieces - 1:
                for to in range(count):

                    @pl.when(to != me)
                    def _():
                        share(to).start()
        for s in range(last, 1, -1):
            c = slot - (s - 1)
            if 0 <= c < pieces:
                for upward in (True, False):
                    sum_start(c, s, upward)
    for c in range(pieces):

        @pl.when(me == last)
        def _():
            give_wait(c, last, True)

        @pl.when(me == 0)
        def _():
            give_wait(c, last, False)

        for s in range(1, count):
            for upward in (True, False):
                sends = me <= s - 1 if upward else me >= count - s
                sends = sends & (me < last if upward else me > 0)

                @pl.when(sends)
                def _():
                    buf, copy = sum_copy(c, s, upward)
                    copy(buf.at[c, s - 1]).wait_send()

                sends = (me >= s - 1) & (me < last) if upward else (me > 0) & (me <= count - s)

                @pl.when(sends)
                def _():
                    give_copy(c, s, upward).wait_send()

    if share_terms:
        for peer in range(count):

            @pl.when(peer != me)
            def _():
                share(peer).wait_send()
                pltpu.make_async_remote_copy(
                    src_ref=out_refs[1],
                    dst_ref=shared.at[peer],
                    send_sem=sems[8].at[peer],
                    recv_sem=sems[9].at[peer],
                    device_id={"tensor": peer},
                    device_id_type=MESH,
                ).wait_recv()

            @pl.when(peer == me)
            def _():
                shared[peer] = out_refs[1][...]

        terms = shared[0]
        for peer in range(1, count):
            terms = terms + shared[peer]
        out_refs[1][...] = terms


def split_refs(refs, kinds):
    n_own, n_out = kinds
    own_refs = refs[:n_own]
    full_ref = refs[n_own]
    out_refs = refs[n_own + 1 : n_own + 1 + n_out]
    return (own_refs, full_ref, out_refs), refs[n_own + 1 + n_out :]


def line_sum(part, owned, outs, finish, pieces, collective_id, share_terms=False):
    count = lax.axis_size("tensor")
    rows, width = part.shape
    size = rows // count // pieces
    vmem = pl.BlockSpec(memory_space=pltpu.VMEM)
    hops = (pieces, count - 1)
    return pl.pallas_call(
        functools.partial(line_sum_kernel, count, pieces, finish, (len(owned), len(outs)), share_terms),
        out_shape=(jax.ShapeDtypeStruct((rows, width), BF16), *outs),
        in_specs=[vmem] * (1 + len(owned)),
        out_specs=(vmem,) * (1 + len(outs)),
        scratch_shapes=[
            pltpu.VMEM((*hops, size, width), BF16),
            pltpu.VMEM((*hops, size, width), BF16),
            pltpu.VMEM((size, width), F32),
            pltpu.VMEM((count, 8, width), F32),
        ]
        + [pltpu.SemaphoreType.DMA(hops)] * 8
        + [pltpu.SemaphoreType.DMA((count,))] * 2,
        compiler_params=pltpu.CompilerParams(
            collective_id=collective_id, has_side_effects=True, vmem_limit_bytes=56 << 20
        ),
        cost_estimate=pl.CostEstimate(
            flops=rows * width * 8, transcendentals=0, bytes_accessed=rows * width * 200
        ),
        name="line_sum",
    )(part, *owned)


def finish_back(c, mine, total, own_refs, out_refs):
    base, value, gain = own_refs[:3]
    x = value[mine, :]
    r = inverse_rms(x)
    y = x * r
    e = gain[...] * total
    out = base[mine, :] + r * (e - y * jnp.mean(e * y, axis=-1, keepdims=True))
    out_refs[0][mine, :] = out
    term = jnp.sum(total * y, axis=0, keepdims=True)
    row = lax.broadcasted_iota(jnp.int32, (8, 1), 0)
    if c == 0:
        more = own_refs[3][...] if len(own_refs) > 3 else 0.0
        out_refs[1][...] = jnp.where(row == 0, term, more)
    else:
        out_refs[1][...] += jnp.where(row == 0, term, 0.0)
    return out.astype(BF16)


def attn_gather_kernel(
    count,
    ways,
    places,
    tiles,
    bq,
    len_ref,
    q_ref,
    k_ref,
    v_ref,
    w_ref,
    full_ref,
    linv_ref,
    whole_ref,
    q6,
    vx,
    acc,
    *sems,
):
    give_up, give_down, line_sems, way_sems = sems[0:2], sems[2:4], sems[4:6], sems[6:8]
    me = lax.axis_index("tensor")
    spot = lax.axis_index("dp")
    piece = w_ref.shape[0] // ways
    weight_slots = [1, 3, 4, 5]
    levels = ways.bit_length() - 1
    last = count - 1
    rows, width = q_ref.shape
    chunks = rows // bq

    def place(block, c):
        at = pl.multiple_of(block * width, width)
        return full_ref.at[pl.ds(c * bq, bq), pl.ds(at, width)]

    def copy(c, s, upward):
        there = place(me - s + 1 if upward else me + s - 1, c)
        sem = give_up if upward else give_down
        return line_copy(there, there, sem, (c, s - 1), me + 1 if upward else me - 1)

    def wait(c, s, upward):
        there = place(me - s if upward else me + s, c)
        sem = give_up if upward else give_down
        line_copy(there, there, sem, (c, s - 1), me + 1 if upward else me - 1).wait_recv()

    def sends(s, upward):
        return (me >= s - 1) & (me < last) if upward else (me > 0) & (me <= count - s)

    def start(c, s, upward):
        if s > 1:

            @pl.when((me >= s - 1) if upward else (me <= count - s))
            def _():
                wait(c, s - 1, upward)

        @pl.when(sends(s, upward))
        def _():
            copy(c, s, upward).start()

    def attend(c):
        first = c * bq
        span = pl.ds(first, bq)
        q6[...] = stack_heads(q_ref[span, :].astype(F32), places).astype(BF16)
        acc[...] = jnp.zeros_like(acc)

        def step(j, masked):
            ks = pl.ds(pl.multiple_of(j * bq, bq), bq)
            prob = jnp.exp2(nt(q6[...], k_ref[ks, :]) * (SCALE * LOG2E))
            if masked:
                q_pos = lax.broadcasted_iota(jnp.int32, prob.shape, 0) & (bq - 1)
                k_pos = lax.broadcasted_iota(jnp.int32, prob.shape, 1)
                prob = jnp.where(k_pos <= q_pos, prob, 0.0)
            acc[...] += nn(prob.astype(BF16), vx[ks, :])

        if c > 0:

            @pl.loop(0, c)
            def _(j):
                step(j, False)

        step(c, True)
        inv = 1.0 / acc[:, LANES:]
        out = unstack_heads(acc[:, :LANES] * inv, places, tiles, bq)
        place(me, c)[...] = out.astype(BF16)
        linv_ref[span, :] = unstack_heads(inv, places, tiles, bq)


    bits = [(spot // (1 << (levels - 1 - level))) % 2 for level in range(levels)]

    def own_part(peer, sender):
        return pltpu.make_async_remote_copy(
            src_ref=whole_ref.at[(me, *bits)],
            dst_ref=whole_ref.at[(sender, *bits)],
            send_sem=line_sems[0].at[peer],
            recv_sem=line_sems[1].at[sender],
            device_id={"tensor": peer},
            device_id_type=MESH,
        )

    def partner(level):
        return spot + (1 - 2 * bits[level]) * (1 << (levels - 1 - level))

    def held_parts(level, theirs=False):
        ours = [1 - bits[level] if theirs else bits[level], *bits[level + 1 :]]
        there = whole_ref.at[(slice(None),) * (level + 1) + tuple(ours)]
        return pltpu.make_async_remote_copy(
            src_ref=there,
            dst_ref=there,
            send_sem=way_sems[0].at[level],
            recv_sem=way_sems[1].at[level],
            device_id={"dp": partner(level)},
            device_id_type=MESH,
        )

    def weight_step(step):
        if step == 0:
            mine = pl.ds(pl.multiple_of(spot * piece, piece), piece)
            whole_ref[(me, *bits)] = w_ref[mine, :]
            for peer in range(count):

                @pl.when(peer != me)
                def _():
                    own_part(peer, me).start()

            return
        if step == 1:
            for peer in range(count):

                @pl.when(peer != me)
                def _():
                    own_part(peer, peer).wait_recv()

        else:
            held_parts(step - 2, True).wait_recv()
        if step - 1 < levels:
            held_parts(step - 1).start()

    barrier = pltpu.get_barrier_semaphore()
    for peer in range(count):

        @pl.when(peer != me)
        def _():
            pl.semaphore_signal(barrier, inc=1, device_id={"tensor": peer}, device_id_type=MESH)

    for level in range(levels):
        pl.semaphore_signal(
            barrier, inc=1, device_id={"dp": partner(level)}, device_id_type=MESH
        )
    pl.semaphore_wait(barrier, count - 1 + levels)
    weight_step(0)
    live = lax.broadcasted_iota(jnp.int32, (rows, LANES), 0) < len_ref[0]
    vx[:, :LANES] = jnp.where(live, v_ref[...].astype(F32), 0.0).astype(BF16)
    vx[:, LANES:] = jnp.where(live, 1.0, 0.0).astype(BF16)
    for slot in range(chunks + last):
        if slot < chunks:
            attend(slot)
            for upward in (True, False):
                start(slot, 1, upward)
        for s in range(last, 1, -1):
            c = slot - (s - 1)
            if 0 <= c < chunks:
                for upward in (True, False):
                    start(c, s, upward)
        if slot in weight_slots:
            weight_step(1 + weight_slots.index(slot))
    for step in range(1 + len(weight_slots), levels + 2):
        weight_step(step)
    for peer in range(count):

        @pl.when(peer != me)
        def _():
            own_part(peer, me).wait_send()

    for level in range(levels):
        held_parts(level).wait_send()
    for c in range(chunks):

        @pl.when(me == last)
        def _():
            wait(c, last, True)

        @pl.when(me == 0)
        def _():
            wait(c, last, False)

        for s in range(1, count):
            for upward in (True, False):

                @pl.when(sends(s, upward))
                def _():
                    copy(c, s, upward).wait_send()


def attn_gather(length, q, k, v, w, heads, group, bq, collective_id):
    count = lax.axis_size("tensor")
    ways = lax.axis_size("dp")
    rows, width = q.shape
    vmem = pl.BlockSpec(memory_space=pltpu.VMEM)
    hops = (rows // bq, count - 1)
    return pl.pallas_call(
        functools.partial(
            attn_gather_kernel, count, ways, head_places(heads, group), width // LANES, bq
        ),
        out_shape=(
            jax.ShapeDtypeStruct((rows, count * width), BF16),
            jax.ShapeDtypeStruct((rows, width), F32),
            jax.ShapeDtypeStruct((count, *(2,) * (ways.bit_length() - 1), w.shape[0] // ways, w.shape[1]), BF16),
        ),
        in_specs=[pl.BlockSpec(memory_space=pltpu.SMEM), vmem, vmem, vmem, vmem],
        out_specs=(vmem, vmem, vmem),
        scratch_shapes=[
            pltpu.VMEM((heads * bq, LANES), BF16),
            pltpu.VMEM((rows, 2 * LANES), BF16),
            pltpu.VMEM((heads * bq, 2 * LANES), F32),
        ]
        + [pltpu.SemaphoreType.DMA(hops)] * 4
        + [pltpu.SemaphoreType.DMA((count,))] * 2
        + [pltpu.SemaphoreType.DMA((ways,))] * 2,
        compiler_params=pltpu.CompilerParams(
            collective_id=collective_id, has_side_effects=True, vmem_limit_bytes=56 << 20
        ),
        cost_estimate=pl.CostEstimate(
            flops=heads * rows * rows * 2 * LANES,
            transcendentals=heads * rows * rows // 2,
            bytes_accessed=rows * count * width * 120,
        ),
        name="attention_gather",
    )(length, q, k, v, w)


def inverse_rms(x):
    return lax.rsqrt(jnp.mean(x * x, axis=-1, keepdims=True) + EPSILON)


def norm_back(x, r, gain, grad):
    y = x * r
    e = gain * grad
    return r * (e - y * jnp.mean(e * y, axis=-1, keepdims=True)), jnp.sum(grad * y, axis=0)


def rope_tables(row_count):
    half = HEAD_SIZE // 2
    positions = jnp.arange(row_count).astype(F32)[:, None]
    freq = jnp.exp(jnp.arange(half).astype(F32) * (-2.0 * math.log(ROPE_BASE) / HEAD_SIZE))
    angles = positions * freq[None, :]
    return jnp.cos(angles)[:, None, :], jnp.sin(angles)[:, None, :]


def turn(x, cosine, sine):
    half = HEAD_SIZE // 2
    low, high = x[..., :half], x[..., half:]
    return jnp.concatenate([low * cosine - high * sine, high * cosine + low * sine], axis=-1)


def by_head(x):
    return x.reshape(x.shape[0], x.shape[1] // HEAD_SIZE, HEAD_SIZE)


def flat(x):
    return x.reshape(x.shape[0], x.shape[1] * x.shape[2])


def prepare(x, gain, tables):
    heads = by_head(x)
    return flat(turn(heads * inverse_rms(heads) * gain, *tables))


def prepare_back(x, gain, tables, grad):
    heads = by_head(x)
    back = turn(by_head(grad), tables[0], -tables[1])
    dx, d_gain = norm_back(heads, inverse_rms(heads), gain, back)
    return flat(dx), jnp.sum(d_gain, axis=0)


def to_lanes(x):
    short = -x.shape[1] % LANES
    return x if short == 0 else jnp.pad(x, ((0, 0), (0, short)))


def pad_rows(w):
    short = -w.shape[0] % LANES
    return w if short == 0 else jnp.pad(w, ((0, short), (0, 0)))


def on_device(
    tokens,
    lengths,
    cotangent,
    norm_gain,
    query_w,
    key_weight,
    value_weight,
    out_w,
    query_gain,
    key_gain,
    mlp_gain,
    gate_w,
    up_w,
    down_w,
):
    row_count, width = tokens.shape
    me = lax.axis_index("tensor")
    count = lax.axis_size("tensor")
    m = row_count // count
    q_width = query_w.shape[1]
    k_width = key_weight.shape[1]
    heads = q_width // HEAD_SIZE
    group = q_width // k_width
    own_shape = jax.ShapeDtypeStruct((m, width), F32)
    gain_shape = jax.ShapeDtypeStruct((8, width), F32)

    def own(x):
        return lax.dynamic_slice_in_dim(x, me * m, m, axis=0)

    live = (jnp.arange(row_count, dtype=jnp.int32) < lengths[0])[:, None]
    d_out = jnp.where(live, cotangent, jnp.zeros_like(cotangent))
    inputs = tokens.astype(F32)
    normed = (inputs * inverse_rms(inputs) * norm_gain).astype(BF16)
    inputs_own = own(tokens).astype(F32)
    queries = nn(normed, query_w)
    keys_val = nn(normed, key_weight)
    tables = rope_tables(row_count)
    q_pad = to_lanes(prepare(queries, query_gain, tables).astype(BF16))
    k_pad = to_lanes(prepare(keys_val, key_gain, tables).astype(BF16))
    v_pad = to_lanes(nn(normed, value_weight).astype(BF16))
    mixed_all, inverse_sums, out_whole = attn_gather(
        lengths, q_pad, k_pad, v_pad, pad_rows(out_w), heads, group, min(512, row_count), 1
    )
    resid = inputs + nn(mixed_all, out_whole.reshape(-1, width))
    normed2 = (resid * inverse_rms(resid) * mlp_gain).astype(BF16)
    resid_own = own(resid)
    padded = q_pad.shape[1]
    mixed_pad = lax.dynamic_slice_in_dim(mixed_all, me * padded, padded, axis=1)
    mixed = mixed_pad[:, :q_width]
    gate = nn(normed2, gate_w)
    up = nn(normed2, up_w)
    sig = jax.nn.sigmoid(gate)
    hidden = (gate * sig * up).astype(BF16)
    mlp_part = nn(hidden, down_w).astype(BF16)
    mlp_part, gate, up = lax.optimization_barrier((mlp_part, gate, up))
    mlp_own = lax.psum_scatter(mlp_part, "tensor", scatter_dimension=0, tiled=True)
    sig = jax.nn.sigmoid(gate)
    d_hidden = nt(d_out, down_w)
    d_gate = (d_hidden * up * sig * (1.0 + gate * (1.0 - sig))).astype(BF16)
    d_up = (d_hidden * gate * sig).astype(BF16)
    d_normed2 = (nt(d_gate, gate_w) + nt(d_up, up_w)).astype(BF16)
    d_normed2, mlp_own = lax.optimization_barrier((d_normed2, mlp_own))
    d_resid, d_resid_own, d_mlp_gain = line_sum(
        d_normed2,
        (own(d_out).astype(F32), resid_own, mlp_gain[None]),
        (own_shape, gain_shape),
        finish_back,
        PIECES,
        2,
    )
    g_gate = tn(normed2, d_gate).astype(BF16)
    g_up = tn(normed2, d_up).astype(BF16)
    g_down = tn(hidden, d_out).astype(BF16)
    g_gate, g_up, g_down = lax.psum((g_gate, g_up, g_down), "dp")

    after = d_mlp_gain[7, 0]
    block_own = (resid_own + after + mlp_own.astype(F32)).astype(BF16)
    block_own, d_resid = lax.optimization_barrier((block_own, d_resid))
    block_out = lax.all_gather(block_own, "tensor", axis=0, tiled=True)
    d_mixed = nt(d_resid, out_w).astype(BF16)
    dq, dk, dv = attn_bwd(
        lengths, q_pad, to_lanes(d_mixed), mixed_pad, inverse_sums, k_pad, v_pad, heads, group
    )
    dq, d_qgain = prepare_back(queries, query_gain, tables, dq[:, :q_width])
    dk, d_kgain = prepare_back(keys_val, key_gain, tables, dk[:, :k_width])
    d_q, d_k, d_v = dq.astype(BF16), dk.astype(BF16), dv[:, :k_width].astype(BF16)
    d_q, d_k, d_v, block_out = lax.optimization_barrier((d_q, d_k, d_v, block_out))
    d_normed = (nt(d_q, query_w) + nt(d_k, key_weight) + nt(d_v, value_weight)).astype(BF16)
    head_terms = jnp.concatenate([d_qgain, d_kgain])
    terms = jnp.concatenate(
        [
            jnp.zeros((1, width), F32),
            d_mlp_gain[:1],
            jnp.pad(head_terms[None], ((0, 0), (0, width - 2 * HEAD_SIZE))),
            jnp.zeros((5, width), F32),
        ]
    )
    whole_grads = tuple(g.astype(F32) + after for g in (g_gate, g_up, g_down))
    d_normed, *whole_grads = lax.optimization_barrier((d_normed, *whole_grads))
    d_inputs, _, d_gains = line_sum(
        d_normed,
        (d_resid_own, inputs_own, norm_gain[None], terms),
        (own_shape, gain_shape),
        finish_back,
        PIECES,
        3,
        True,
    )
    g_out = tn(mixed, d_resid).astype(BF16)
    g_query = tn(normed, d_q).astype(BF16)
    g_key = tn(normed, d_k).astype(BF16)
    g_value = tn(normed, d_v).astype(BF16)
    g_out, g_query, g_key, g_value, *whole_grads = lax.optimization_barrier(
        (g_out, g_query, g_key, g_value, *whole_grads)
    )
    g_out, g_query, g_key, g_value = lax.psum((g_out, g_query, g_key, g_value), "dp")
    d_gains = lax.psum(d_gains[:3], "dp")
    return (
        block_out,
        d_inputs.astype(F32),
        d_gains[0],
        g_query.astype(F32),
        g_key.astype(F32),
        g_value.astype(F32),
        g_out.astype(F32),
        d_gains[2, :HEAD_SIZE],
        d_gains[2, HEAD_SIZE : 2 * HEAD_SIZE],
        d_gains[1],
        *whole_grads,
    )


def solution(mesh):
    rows, whole = P("dp", None), P()
    columns, depth = P(None, "tensor"), P("tensor", None)
    return jax.shard_map(
        on_device,
        mesh=mesh,
        in_specs=(
            rows,
            P("dp"),
            rows,
            whole,
            columns,
            columns,
            columns,
            depth,
            whole,
            whole,
            whole,
            columns,
            columns,
            depth,
        ),
        out_specs=(
            rows,
            rows,
            whole,
            columns,
            columns,
            columns,
            depth,
            whole,
            whole,
            whole,
            columns,
            columns,
            depth,
        ),
        check_vma=False,
    )
```

```python
import functools
import math

import jax
import jax.numpy as jnp
from jax import lax
from jax.experimental import pallas as pl
from jax.experimental.pallas import tpu as pltpu
from jax.sharding import PartitionSpec as P

HEAD_SIZE = 64
LANES = 128
SCALE = HEAD_SIZE**-0.5
LOG2E = math.log2(math.e)
EPSILON = 1e-05
ROPE_BASE = 1000000.0
F32 = jnp.float32
BF16 = jnp.bfloat16
MESH = pl.DeviceIdType.MESH


def nt(a,b): return lax.dot_general(a,b,(((1,),(1,)),((),())),preferred_element_type=F32)
def tn(a,b): return lax.dot_general(a,b,(((0,),(0,)),((),())),preferred_element_type=F32)
def nn(a,b): return lax.dot_general(a,b,(((1,),(0,)),((),())),preferred_element_type=F32)

def head_places(heads, group):
    return [(h // 2, h % 2, h // group) for h in range(heads)]

def half_mask(half, dtype=F32):
    lane = lax.broadcasted_iota(jnp.int32, (1, LANES), 1)
    keep = lane < HEAD_SIZE if half == 0 else lane >= HEAD_SIZE
    return keep

def stack_heads(x, places):
    out = []
    for tile, half, kv in places:
        piece = x[:, tile * LANES:(tile + 1) * LANES]
        if half != kv:
            piece = pltpu.roll(piece, HEAD_SIZE, 1)
        out.append(jnp.where(half_mask(kv), piece, 0.0))
    return jnp.concatenate(out, axis=0)

def unstack_heads(x, places, tiles, n):
    pieces = {}
    for h, (tile, half, kv) in enumerate(places):
        piece = x[h * n:(h + 1) * n]
        if half != kv:
            piece = pltpu.roll(piece, HEAD_SIZE, 1)
        pieces[tile, half] = piece
    out = []
    for tile in range(tiles):
        low = pieces[tile, 0]
        high = pieces.get((tile, 1))
        out.append(jnp.where(half_mask(0), low, 0.0 if high is None else high))
    return jnp.concatenate(out, axis=1)

def bwd_kernel(places, tiles, bq, bk, len_ref, q_ref, do_ref, o_ref, linv_ref, k_ref, v_ref, dq_ref, dk_ref, dv_ref, q6, do6, d_row, kx, dq6):
    i = pl.program_id(0)
    rows = k_ref.shape[0]
    heads = len(places)
    @pl.when(i == 0)
    def _():
        live = lax.broadcasted_iota(jnp.int32, (rows, LANES), 0) < len_ref[0]
        kx[...] = jnp.where(live, k_ref[...].astype(F32), 0.0).astype(BF16)
        dk_ref[...] = jnp.zeros_like(dk_ref)
        dv_ref[...] = jnp.zeros_like(dv_ref)
    q6[...] = stack_heads(q_ref[...].astype(F32), places).astype(BF16)
    dob = do_ref[...].astype(F32) * linv_ref[...]
    do6[...] = stack_heads(dob, places).astype(BF16)
    prod = stack_heads(dob * o_ref[...].astype(F32), places)
    hi = prod.astype(BF16)
    lo = (prod - hi.astype(F32)).astype(BF16)
    ones = jnp.ones((16, LANES), BF16)
    d_row[...] = nt(ones, hi) + nt(ones, lo)
    dq6[...] = jnp.zeros_like(dq6)
    def step(j, masked):
        ks = pl.ds(pl.multiple_of(j * bk, bk), bk)
        st = nt(k_ref[ks, :], q6[...])
        pt = jnp.exp2(st * (SCALE * LOG2E))
        if masked:
            kp = j * bk + lax.broadcasted_iota(jnp.int32, st.shape, 0)
            qp = i * bq + (lax.broadcasted_iota(jnp.int32, st.shape, 1) & (bq - 1))
            pt = jnp.where(kp <= qp, pt, 0.0)
        dv_ref[ks, :] += nn(pt.astype(BF16), do6[...])
        dpt = nt(v_ref[ks, :], do6[...])
        dst = (pt * (dpt - d_row[0:1, :])).astype(BF16)
        dk_ref[ks, :] += nn(dst, q6[...])
        dq6[...] += tn(dst, kx[ks, :])
    full = (i * bq) // bk
    @pl.loop(0, full)
    def _(j): step(j, False)
    @pl.loop(full, full + max(bq // bk, 1))
    def _(j): step(j, True)
    dq_ref[...] = unstack_heads(dq6[...] * SCALE, places, tiles, bq)
    @pl.when(i == pl.num_programs(0) - 1)
    def _():
        live = lax.broadcasted_iota(jnp.int32, (rows, LANES), 0) < len_ref[0]
        dk_ref[...] = jnp.where(live, dk_ref[...] * SCALE, 0.0)
        dv_ref[...] = jnp.where(live, dv_ref[...], 0.0)

def attn_bwd(length, q, do, o, linv, k, v, heads, group, bq=256, bk=256):
    rows, width = q.shape
    tiles = width // LANES
    places = head_places(heads, group)
    blk = pl.BlockSpec((bq, width), lambda i, n: (i, 0))
    whole = pl.BlockSpec((rows, LANES), lambda i, n: (0, 0))
    return pl.pallas_call(
        functools.partial(bwd_kernel, places, tiles, bq, bk),
        out_shape=(jax.ShapeDtypeStruct((rows, width), F32), jax.ShapeDtypeStruct((rows, LANES), F32), jax.ShapeDtypeStruct((rows, LANES), F32)),
        grid_spec=pltpu.PrefetchScalarGridSpec(
            num_scalar_prefetch=1, grid=(rows // bq,),
            in_specs=[blk] * 4 + [whole] * 2,
            out_specs=[blk, whole, whole],
            scratch_shapes=[pltpu.VMEM((heads * bq, LANES), BF16), pltpu.VMEM((heads * bq, LANES), BF16),
                            pltpu.VMEM((16, heads * bq), F32), pltpu.VMEM((rows, LANES), BF16),
                            pltpu.VMEM((heads * bq, LANES), F32)]),
        compiler_params=pltpu.CompilerParams(dimension_semantics=("arbitrary",), vmem_limit_bytes=48 << 20),
        cost_estimate=pl.CostEstimate(flops=rows * width, transcendentals=0, bytes_accessed=rows * width * 2),
        name="attention_backward",
    )(length, q, do, o, linv, k, v)


def line_copy(src, dst, sems, where, to):
    return pltpu.make_async_remote_copy(
        src_ref=src,
        dst_ref=dst,
        send_sem=sems[0].at[where],
        recv_sem=sems[1].at[where],
        device_id={"tensor": to},
        device_id_type=MESH,
    )


def greet_line(count, ways=0):
    me = lax.axis_index("tensor")
    barrier = pltpu.get_barrier_semaphore()

    def greet(peer):
        pl.semaphore_signal(barrier, inc=1, device_id={"tensor": peer}, device_id_type=MESH)

    if ways:
        spot = lax.axis_index("dp")
        for peer in range(count):

            @pl.when(peer != me)
            def _():
                greet(peer)

        for peer in range(ways):

            @pl.when(peer != spot)
            def _():
                pl.semaphore_signal(barrier, inc=1, device_id={"dp": peer}, device_id_type=MESH)

        pl.semaphore_wait(barrier, count - 1 + ways - 1)
        return

    @pl.when(me > 0)
    def _():
        greet(me - 1)

    @pl.when(me < count - 1)
    def _():
        greet(me + 1)

    @pl.when((me > 0) & (me < count - 1))
    def _():
        pl.semaphore_wait(barrier, 2)

    @pl.when((me == 0) | (me == count - 1))
    def _():
        pl.semaphore_wait(barrier, 1)


def line_sum_kernel(
    count, pieces, finish, kinds, share_terms, part_ref, *refs
):
    (own_refs, full_ref, out_refs), scratch = split_refs(refs, kinds)
    up_buf, down_buf, acc, shared, shared_ways = scratch[:5]
    sems = scratch[5:]
    ways = shared_ways.shape[0]
    spot = lax.axis_index("dp")
    sum_up, sum_down, give_up, give_down = (sems[0:2], sems[2:4], sems[4:6], sems[6:8])
    me = lax.axis_index("tensor")
    last = count - 1
    own = part_ref.shape[0] // count
    size = own // pieces

    def rows(block, c):
        return pl.ds(pl.multiple_of(block * own + c * size, size), size)

    def sum_copy(c, s, upward):
        buf, sem = (up_buf, sum_up) if upward else (down_buf, sum_down)
        to = me + 1 if upward else me - 1
        return buf, lambda src: line_copy(src, buf.at[c, s - 1], sem, (c, s - 1), to)

    def sum_start(c, s, upward):
        buf, copy = sum_copy(c, s, upward)
        first = me == 0 if upward else me == last
        block = count - s + me if upward else me - (count - s)
        sends = me <= s - 1 if upward else me >= count - s
        sends = sends & (me < last if upward else me > 0)

        @pl.when(sends & first)
        def _():
            copy(part_ref.at[rows(block, c)]).start()

        if s > 1:

            @pl.when(sends & jnp.logical_not(first))
            def _():
                sum_wait(c, s - 1, upward)
                held = buf.at[c, s - 2]
                held[...] = (held[...].astype(F32) + part_ref[rows(block, c), :].astype(F32)).astype(BF16)
                copy(held).start()

    def sum_wait(c, s, upward):
        buf, copy = sum_copy(c, s, upward)
        copy(buf.at[c, s - 1]).wait_recv()

    def give_copy(c, s, upward):
        block = me - s + 1 if upward else me + s - 1
        sem = give_up if upward else give_down
        place = full_ref.at[rows(block, c)]
        return line_copy(place, place, sem, (c, s - 1), me + 1 if upward else me - 1)

    def give_wait(c, s, upward):
        block = me - s if upward else me + s
        sem = give_up if upward else give_down
        place = full_ref.at[rows(block, c)]
        line_copy(place, place, sem, (c, s - 1), me + 1 if upward else me - 1).wait_recv()

    def give_start(c, s, upward):
        sends = (me >= s - 1) & (me < last) if upward else (me > 0) & (me <= count - s)
        if s > 1:
            got = (me >= s - 1) if upward else (me <= count - s)

            @pl.when(got)
            def _():
                give_wait(c, s - 1, upward)

        @pl.when(sends)
        def _():
            give_copy(c, s, upward).start()

    def settle(c):
        acc[...] = part_ref[rows(me, c), :].astype(F32)

        @pl.when(me > 0)
        def _():
            sum_wait(c, last, True)
            acc[...] += up_buf[c, last - 1].astype(F32)

        @pl.when(me < last)
        def _():
            sum_wait(c, last, False)
            acc[...] += down_buf[c, last - 1].astype(F32)

        mine = pl.ds(c * size, size)
        full_ref[rows(me, c), :] = finish(c, mine, acc[...], own_refs, out_refs)

    def share(axis, to, sender, at):
        here, place, sem = (me, shared, 8) if axis == "tensor" else (spot, shared_ways, 10)
        return pltpu.make_async_remote_copy(
            src_ref=out_refs[1],
            dst_ref=place.at[sender],
            send_sem=sems[sem].at[to],
            recv_sem=sems[sem + 1].at[sender],
            device_id={axis: to},
            device_id_type=MESH,
        )

    def share_start(axis, size_of, here):
        for to in range(size_of):

            @pl.when(to != here)
            def _():
                share(axis, to, here, here).start()

    def share_finish(axis, size_of, here, place):
        for peer in range(size_of):

            @pl.when(peer != here)
            def _():
                share(axis, peer, here, here).wait_send()
                share(axis, peer, peer, here).wait_recv()

            @pl.when(peer == here)
            def _():
                place[peer] = out_refs[1][...]

        terms = place[0]
        for peer in range(1, size_of):
            terms = terms + place[peer]
        out_refs[1][...] = terms

    greet_line(count, ways if share_terms else 0)
    for slot in range(pieces + 2 * last):
        if slot < pieces:
            for upward in (True, False):
                sum_start(slot, 1, upward)
        for s in range(last, 1, -1):
            c = slot - last - (s - 1)
            if 0 <= c < pieces:
                for upward in (True, False):
                    give_start(c, s, upward)
        c = slot - last
        if 0 <= c < pieces:
            settle(c)
            for upward in (True, False):
                give_start(c, 1, upward)
            if share_terms and c == pieces - 1:
                share_start("tensor", count, me)
        if share_terms and c == pieces + last - 2:
            share_finish("tensor", count, me, shared)
            share_start("dp", ways, spot)
        for s in range(last, 1, -1):
            c = slot - (s - 1)
            if 0 <= c < pieces:
                for upward in (True, False):
                    sum_start(c, s, upward)
    for c in range(pieces):

        @pl.when(me == last)
        def _():
            give_wait(c, last, True)

        @pl.when(me == 0)
        def _():
            give_wait(c, last, False)

        for s in range(1, count):
            for upward in (True, False):
                sends = me <= s - 1 if upward else me >= count - s
                sends = sends & (me < last if upward else me > 0)

                @pl.when(sends)
                def _():
                    buf, copy = sum_copy(c, s, upward)
                    copy(buf.at[c, s - 1]).wait_send()

                sends = (me >= s - 1) & (me < last) if upward else (me > 0) & (me <= count - s)

                @pl.when(sends)
                def _():
                    give_copy(c, s, upward).wait_send()

    if share_terms:
        share_finish("dp", ways, spot, shared_ways)


def split_refs(refs, kinds):
    n_own, n_out = kinds
    own_refs = refs[:n_own]
    full_ref = refs[n_own]
    out_refs = refs[n_own + 1 : n_own + 1 + n_out]
    return (own_refs, full_ref, out_refs), refs[n_own + 1 + n_out :]


def line_sum(part, owned, outs, finish, pieces, collective_id, share_terms=False):
    count = lax.axis_size("tensor")
    ways = lax.axis_size("dp")
    rows, width = part.shape
    size = rows // count // pieces
    vmem = pl.BlockSpec(memory_space=pltpu.VMEM)
    hops = (pieces, count - 1)
    return pl.pallas_call(
        functools.partial(line_sum_kernel, count, pieces, finish, (len(owned), len(outs)), share_terms),
        out_shape=(jax.ShapeDtypeStruct((rows, width), BF16), *outs),
        in_specs=[vmem] * (1 + len(owned)),
        out_specs=(vmem,) * (1 + len(outs)),
        scratch_shapes=[
            pltpu.VMEM((*hops, size, width), BF16),
            pltpu.VMEM((*hops, size, width), BF16),
            pltpu.VMEM((size, width), F32),
            pltpu.VMEM((count, 8, width), F32),
            pltpu.VMEM((ways, 8, width), F32),
        ]
        + [pltpu.SemaphoreType.DMA(hops)] * 8
        + [pltpu.SemaphoreType.DMA((count,))] * 2
        + [pltpu.SemaphoreType.DMA((ways,))] * 2,
        compiler_params=pltpu.CompilerParams(
            collective_id=collective_id, has_side_effects=True, vmem_limit_bytes=56 << 20
        ),
        cost_estimate=pl.CostEstimate(
            flops=rows * width * 8, transcendentals=0, bytes_accessed=rows * width * 200
        ),
        name="line_sum",
    )(part, *owned)


def finish_back(c, mine, total, own_refs, out_refs):
    base, value, gain = own_refs[:3]
    x = value[mine, :]
    r = inverse_rms(x)
    y = x * r
    e = gain[...] * total
    out = base[mine, :] + r * (e - y * jnp.mean(e * y, axis=-1, keepdims=True))
    out_refs[0][mine, :] = out
    term = jnp.sum(total * y, axis=0, keepdims=True)
    row = lax.broadcasted_iota(jnp.int32, (8, 1), 0)
    if c == 0:
        more = own_refs[3][...] if len(own_refs) > 3 else 0.0
        out_refs[1][...] = jnp.where(row == 0, term, more)
    else:
        out_refs[1][...] += jnp.where(row == 0, term, 0.0)
    return out.astype(BF16)


def attn_gather_kernel(
    count,
    ways,
    places,
    tiles,
    bq,
    len_ref,
    q_ref,
    k_ref,
    v_ref,
    w_ref,
    tokens_ref,
    gain_ref,
    normed_ref,
    resid_ref,
    mixed_ref,
    linv_ref,
    full_ref,
    whole_ref,
    q6,
    vx,
    acc,
    *sems,
):
    give_up, give_down, line_sems, way_sems = sems[0:2], sems[2:4], sems[4:6], sems[6:8]
    load_tokens = pltpu.make_async_copy(tokens_ref, normed_ref, sems[8])
    me = lax.axis_index("tensor")
    spot = lax.axis_index("dp")
    piece = w_ref.shape[0] // ways
    weight_slots = {1: (1,), 3: (2,), 4: tuple(range(3, ways.bit_length() + 1))}
    levels = ways.bit_length() - 1
    last = count - 1
    rows, width = q_ref.shape
    chunks = rows // bq

    def place(block, c):
        at = pl.multiple_of(block * width, width)
        return full_ref.at[pl.ds(c * bq, bq), pl.ds(at, width)]

    def copy(c, s, upward):
        there = place(me - s + 1 if upward else me + s - 1, c)
        sem = give_up if upward else give_down
        return line_copy(there, there, sem, (c, s - 1), me + 1 if upward else me - 1)

    def wait(c, s, upward):
        there = place(me - s if upward else me + s, c)
        sem = give_up if upward else give_down
        line_copy(there, there, sem, (c, s - 1), me + 1 if upward else me - 1).wait_recv()

    def sends(s, upward):
        return (me >= s - 1) & (me < last) if upward else (me > 0) & (me <= count - s)

    def start(c, s, upward):
        if s > 1:

            @pl.when((me >= s - 1) if upward else (me <= count - s))
            def _():
                wait(c, s - 1, upward)

        @pl.when(sends(s, upward))
        def _():
            copy(c, s, upward).start()

    def attend(c):
        first = c * bq
        span = pl.ds(first, bq)
        q6[...] = stack_heads(q_ref[span, :].astype(F32), places).astype(BF16)
        acc[...] = jnp.zeros_like(acc)

        def step(j, masked):
            ks = pl.ds(pl.multiple_of(j * bq, bq), bq)
            prob = jnp.exp2(nt(q6[...], k_ref[ks, :]) * (SCALE * LOG2E))
            if masked:
                q_pos = lax.broadcasted_iota(jnp.int32, prob.shape, 0) & (bq - 1)
                k_pos = lax.broadcasted_iota(jnp.int32, prob.shape, 1)
                prob = jnp.where(k_pos <= q_pos, prob, 0.0)
            acc[...] += nn(prob.astype(BF16), vx[ks, :])

        if c > 0:

            @pl.loop(0, c)
            def _(j):
                step(j, False)

        step(c, True)
        inv = 1.0 / acc[:, LANES:]
        out = unstack_heads(acc[:, :LANES] * inv, places, tiles, bq)
        place(me, c)[...] = out.astype(BF16)
        mixed_ref[span, :] = out.astype(BF16)
        linv_ref[span, :] = unstack_heads(inv, places, tiles, bq)


    bits = [(spot // (1 << (levels - 1 - level))) % 2 for level in range(levels)]

    def own_part(peer, sender):
        return pltpu.make_async_remote_copy(
            src_ref=whole_ref.at[(me, *bits)],
            dst_ref=whole_ref.at[(sender, *bits)],
            send_sem=line_sems[0].at[peer],
            recv_sem=line_sems[1].at[sender],
            device_id={"tensor": peer},
            device_id_type=MESH,
        )

    def partner(level):
        return spot + (1 - 2 * bits[level]) * (1 << (levels - 1 - level))

    def held_parts(level, theirs=False):
        ours = [1 - bits[level] if theirs else bits[level], *bits[level + 1 :]]
        there = whole_ref.at[(slice(None),) * (level + 1) + tuple(ours)]
        return pltpu.make_async_remote_copy(
            src_ref=there,
            dst_ref=there,
            send_sem=way_sems[0].at[level],
            recv_sem=way_sems[1].at[level],
            device_id={"dp": partner(level)},
            device_id_type=MESH,
        )

    def weight_step(step):
        if step == 0:
            mine = pl.ds(pl.multiple_of(spot * piece, piece), piece)
            whole_ref[(me, *bits)] = w_ref[mine, :]
            for peer in range(count):

                @pl.when(peer != me)
                def _():
                    own_part(peer, me).start()

            return
        if step == 1:
            for peer in range(count):

                @pl.when(peer != me)
                def _():
                    own_part(peer, peer).wait_recv()

        else:
            held_parts(step - 2, True).wait_recv()
        if step - 1 < levels:
            held_parts(step - 1).start()

    def project(c):
        @pl.when(me == last)
        def _():
            wait(c, last, True)

        @pl.when(me == 0)
        def _():
            wait(c, last, False)

        span = pl.ds(c * bq, bq)
        resid = normed_ref[span, :].astype(F32)
        for block in range(count):
            weight = whole_ref[block].reshape(width, resid.shape[1])
            resid += nn(full_ref[span, pl.ds(block * width, width)], weight)
        normed_ref[span, :] = (resid * inverse_rms(resid) * gain_ref[...]).astype(BF16)
        own = resid_ref.shape[0]
        for j in range(bq // own):

            @pl.when(me == c * (bq // own) + j)
            def _():
                resid_ref[...] = resid[j * own : (j + 1) * own]

    load_tokens.start()
    barrier = pltpu.get_barrier_semaphore()
    for peer in range(count):

        @pl.when(peer != me)
        def _():
            pl.semaphore_signal(barrier, inc=1, device_id={"tensor": peer}, device_id_type=MESH)

    for level in range(levels):
        pl.semaphore_signal(
            barrier, inc=1, device_id={"dp": partner(level)}, device_id_type=MESH
        )
    pl.semaphore_wait(barrier, count - 1 + levels)
    weight_step(0)
    live = lax.broadcasted_iota(jnp.int32, (rows, LANES), 0) < len_ref[0]
    vx[:, :LANES] = jnp.where(live, v_ref[...].astype(F32), 0.0).astype(BF16)
    vx[:, LANES:] = jnp.where(live, 1.0, 0.0).astype(BF16)
    for slot in range(chunks + last - 1):
        if slot < chunks:
            attend(slot)
            for upward in (True, False):
                start(slot, 1, upward)
        for s in range(last, 1, -1):
            c = slot - (s - 1)
            if 0 <= c < chunks:
                for upward in (True, False):
                    start(c, s, upward)
        for step in weight_slots.get(slot, ()):
            weight_step(step)
        if slot == 4:
            load_tokens.wait()
        if slot >= max(4, last) and slot - max(4, last) < chunks:
            project(slot - max(4, last))
    for c in range(max(0, chunks + last - 1 - max(4, last)), chunks):
        project(c)
    for peer in range(count):

        @pl.when(peer != me)
        def _():
            own_part(peer, me).wait_send()

    for level in range(levels):
        held_parts(level).wait_send()
    for c in range(chunks):
        for s in range(1, count):
            for upward in (True, False):

                @pl.when(sends(s, upward))
                def _():
                    copy(c, s, upward).wait_send()


def attn_gather(length, q, k, v, w, tokens, gain, heads, group, bq, collective_id):
    count = lax.axis_size("tensor")
    ways = lax.axis_size("dp")
    rows, width = q.shape
    model = tokens.shape[1]
    vmem = pl.BlockSpec(memory_space=pltpu.VMEM)
    hops = (rows // bq, count - 1)
    levels = ways.bit_length() - 1
    return pl.pallas_call(
        functools.partial(
            attn_gather_kernel, count, ways, head_places(heads, group), width // LANES, bq
        ),
        out_shape=(
            jax.ShapeDtypeStruct((rows, model), BF16),
            jax.ShapeDtypeStruct((rows // count, model), F32),
            jax.ShapeDtypeStruct((rows, width), BF16),
            jax.ShapeDtypeStruct((rows, width), F32),
        ),
        in_specs=[pl.BlockSpec(memory_space=pltpu.SMEM)]
        + [vmem] * 4
        + [pl.BlockSpec(memory_space=pl.ANY), vmem],
        out_specs=(vmem,) * 4,
        scratch_shapes=[
            pltpu.VMEM((rows, count * width), BF16),
            pltpu.VMEM((count, *(2,) * levels, w.shape[0] // ways, model), BF16),
            pltpu.VMEM((heads * bq, LANES), BF16),
            pltpu.VMEM((rows, 2 * LANES), BF16),
            pltpu.VMEM((heads * bq, 2 * LANES), F32),
        ]
        + [pltpu.SemaphoreType.DMA(hops)] * 4
        + [pltpu.SemaphoreType.DMA((count,))] * 2
        + [pltpu.SemaphoreType.DMA((ways,))] * 2
        + [pltpu.SemaphoreType.DMA(())],
        compiler_params=pltpu.CompilerParams(
            collective_id=collective_id, has_side_effects=True, vmem_limit_bytes=58 << 20
        ),
        cost_estimate=pl.CostEstimate(
            flops=heads * rows * rows * 2 * LANES,
            transcendentals=heads * rows * rows // 2,
            bytes_accessed=rows * count * width * 120,
        ),
        name="attention_gather",
    )(length, q, k, v, w, tokens, gain)


def inverse_rms(x):
    return lax.rsqrt(jnp.mean(x * x, axis=-1, keepdims=True) + EPSILON)


def norm_back(x, r, gain, grad):
    y = x * r
    e = gain * grad
    return r * (e - y * jnp.mean(e * y, axis=-1, keepdims=True)), jnp.sum(grad * y, axis=0)


def rope_tables(row_count):
    half = HEAD_SIZE // 2
    positions = jnp.arange(row_count).astype(F32)[:, None]
    freq = jnp.exp(jnp.arange(half).astype(F32) * (-2.0 * math.log(ROPE_BASE) / HEAD_SIZE))
    angles = positions * freq[None, :]
    return jnp.cos(angles)[:, None, :], jnp.sin(angles)[:, None, :]


def turn(x, cosine, sine):
    half = HEAD_SIZE // 2
    low, high = x[..., :half], x[..., half:]
    return jnp.concatenate([low * cosine - high * sine, high * cosine + low * sine], axis=-1)


def by_head(x):
    return x.reshape(x.shape[0], x.shape[1] // HEAD_SIZE, HEAD_SIZE)


def flat(x):
    return x.reshape(x.shape[0], x.shape[1] * x.shape[2])


def prepare(x, gain, tables):
    heads = by_head(x)
    return flat(turn(heads * inverse_rms(heads) * gain, *tables))


def prepare_back(x, gain, tables, grad):
    heads = by_head(x)
    back = turn(by_head(grad), tables[0], -tables[1])
    dx, d_gain = norm_back(heads, inverse_rms(heads), gain, back)
    return flat(dx), jnp.sum(d_gain, axis=0)


def to_lanes(x):
    short = -x.shape[1] % LANES
    return x if short == 0 else jnp.pad(x, ((0, 0), (0, short)))


def pad_rows(w):
    short = -w.shape[0] % LANES
    return w if short == 0 else jnp.pad(w, ((0, short), (0, 0)))


def on_device(
    tokens,
    lengths,
    cotangent,
    norm_gain,
    query_w,
    key_weight,
    value_weight,
    out_w,
    query_gain,
    key_gain,
    mlp_gain,
    gate_w,
    up_w,
    down_w,
):
    row_count, width = tokens.shape
    me = lax.axis_index("tensor")
    count = lax.axis_size("tensor")
    m = row_count // count
    q_width = query_w.shape[1]
    k_width = key_weight.shape[1]
    heads = q_width // HEAD_SIZE
    group = q_width // k_width
    pieces = 64 // count
    own_shape = jax.ShapeDtypeStruct((m, width), F32)
    gain_shape = jax.ShapeDtypeStruct((8, width), F32)

    def own(x):
        return lax.dynamic_slice_in_dim(x, me * m, m, axis=0)

    live = (jnp.arange(row_count, dtype=jnp.int32) < lengths[0])[:, None]
    d_out = jnp.where(live, cotangent, jnp.zeros_like(cotangent))
    inputs = tokens.astype(F32)
    normed = (inputs * inverse_rms(inputs) * norm_gain).astype(BF16)
    inputs_own = own(tokens).astype(F32)
    queries = nn(normed, query_w)
    keys_val = nn(normed, key_weight)
    tables = rope_tables(row_count)
    q_pad = to_lanes(prepare(queries, query_gain, tables).astype(BF16))
    k_pad = to_lanes(prepare(keys_val, key_gain, tables).astype(BF16))
    v_pad = to_lanes(nn(normed, value_weight).astype(BF16))
    normed2, resid_own, mixed_pad, inverse_sums = attn_gather(
        lengths,
        q_pad,
        k_pad,
        v_pad,
        pad_rows(out_w),
        tokens,
        mlp_gain[None],
        heads,
        group,
        min(512, row_count),
        1,
    )
    mixed = mixed_pad[:, :q_width]
    gate = nn(normed2, gate_w)
    up = nn(normed2, up_w)
    sig = jax.nn.sigmoid(gate)
    hidden = (gate * sig * up).astype(BF16)
    mlp_part = nn(hidden, down_w).astype(BF16)
    mlp_part, gate, up = lax.optimization_barrier((mlp_part, gate, up))
    mlp_own = lax.psum_scatter(mlp_part, "tensor", scatter_dimension=0, tiled=True)
    sig = jax.nn.sigmoid(gate)
    d_hidden = nt(d_out, down_w)
    d_gate = (d_hidden * up * sig * (1.0 + gate * (1.0 - sig))).astype(BF16)
    d_up = (d_hidden * gate * sig).astype(BF16)
    d_normed2 = (nt(d_gate, gate_w) + nt(d_up, up_w)).astype(BF16)
    d_normed2, mlp_own = lax.optimization_barrier((d_normed2, mlp_own))
    d_resid, d_resid_own, d_mlp_gain = line_sum(
        d_normed2,
        (own(d_out).astype(F32), resid_own, mlp_gain[None]),
        (own_shape, gain_shape),
        finish_back,
        pieces,
        2,
    )
    g_gate = tn(normed2, d_gate).astype(BF16)
    g_up = tn(normed2, d_up).astype(BF16)
    g_down = tn(hidden, d_out).astype(BF16)
    g_gate, g_up, g_down = lax.psum((g_gate, g_up, g_down), "dp")

    after = d_mlp_gain[7, 0]
    block_own = (resid_own + after + mlp_own.astype(F32)).astype(BF16)
    block_own, d_resid = lax.optimization_barrier((block_own, d_resid))
    block_out = lax.all_gather(block_own, "tensor", axis=0, tiled=True)
    d_mixed = nt(d_resid, out_w).astype(BF16)
    dq, dk, dv = attn_bwd(
        lengths, q_pad, to_lanes(d_mixed), mixed_pad, inverse_sums, k_pad, v_pad, heads, group
    )
    dq, d_qgain = prepare_back(queries, query_gain, tables, dq[:, :q_width])
    dk, d_kgain = prepare_back(keys_val, key_gain, tables, dk[:, :k_width])
    d_q, d_k, d_v = dq.astype(BF16), dk.astype(BF16), dv[:, :k_width].astype(BF16)
    d_q, d_k, d_v, block_out = lax.optimization_barrier((d_q, d_k, d_v, block_out))
    d_normed = (nt(d_q, query_w) + nt(d_k, key_weight) + nt(d_v, value_weight)).astype(BF16)
    head_terms = jnp.concatenate([d_qgain, d_kgain])
    terms = jnp.concatenate(
        [
            jnp.zeros((1, width), F32),
            d_mlp_gain[:1],
            jnp.pad(head_terms[None], ((0, 0), (0, width - 2 * HEAD_SIZE))),
            jnp.zeros((5, width), F32),
        ]
    )
    whole_grads = tuple(g.astype(F32) + after for g in (g_gate, g_up, g_down))
    d_normed, *whole_grads = lax.optimization_barrier((d_normed, *whole_grads))
    d_inputs, _, d_gains = line_sum(
        d_normed,
        (d_resid_own, inputs_own, norm_gain[None], terms),
        (own_shape, gain_shape),
        finish_back,
        pieces,
        3,
        True,
    )
    g_out = tn(mixed, d_resid).astype(BF16)
    g_query = tn(normed, d_q).astype(BF16)
    g_key = tn(normed, d_k).astype(BF16)
    g_value = tn(normed, d_v).astype(BF16)
    g_out, g_query, g_key, g_value, *whole_grads = lax.optimization_barrier(
        (g_out, g_query, g_key, g_value, *whole_grads)
    )
    g_out, g_query, g_key, g_value = lax.psum((g_out, g_query, g_key, g_value), "dp")
    return (
        block_out,
        d_inputs.astype(F32),
        d_gains[0],
        g_query.astype(F32),
        g_key.astype(F32),
        g_value.astype(F32),
        g_out.astype(F32),
        d_gains[2, :HEAD_SIZE],
        d_gains[2, HEAD_SIZE : 2 * HEAD_SIZE],
        d_gains[1],
        *whole_grads,
    )


def solution(mesh):
    rows, whole = P("dp", None), P()
    columns, depth = P(None, "tensor"), P("tensor", None)
    return jax.shard_map(
        on_device,
        mesh=mesh,
        in_specs=(
            rows,
            P("dp"),
            rows,
            whole,
            columns,
            columns,
            columns,
            depth,
            whole,
            whole,
            whole,
            columns,
            columns,
            depth,
        ),
        out_specs=(
            rows,
            rows,
            whole,
            columns,
            columns,
            columns,
            depth,
            whole,
            whole,
            whole,
            columns,
            columns,
            depth,
        ),
        check_vma=False,
    )
```

```python
import functools
import math

import jax
import jax.numpy as jnp
from jax import lax
from jax.experimental import pallas as pl
from jax.experimental.pallas import tpu as pltpu
from jax.sharding import PartitionSpec as P

HEAD_SIZE = 64
LANES = 128
SCALE = HEAD_SIZE**-0.5
LOG2E = math.log2(math.e)
EPSILON = 1e-05
ROPE_BASE = 1000000.0
F32 = jnp.float32
BF16 = jnp.bfloat16
MESH = pl.DeviceIdType.MESH


def nt(a,b): return lax.dot_general(a,b,(((1,),(1,)),((),())),preferred_element_type=F32)
def tn(a,b): return lax.dot_general(a,b,(((0,),(0,)),((),())),preferred_element_type=F32)
def nn(a,b): return lax.dot_general(a,b,(((1,),(0,)),((),())),preferred_element_type=F32)

def head_places(heads, group):
    return [(h // 2, h % 2, h // group) for h in range(heads)]

def half_mask(half, dtype=F32):
    lane = lax.broadcasted_iota(jnp.int32, (1, LANES), 1)
    keep = lane < HEAD_SIZE if half == 0 else lane >= HEAD_SIZE
    return keep

def stack_heads(x, places):
    out = []
    for tile, half, kv in places:
        piece = x[:, tile * LANES:(tile + 1) * LANES]
        if half != kv:
            piece = pltpu.roll(piece, HEAD_SIZE, 1)
        out.append(jnp.where(half_mask(kv), piece, 0.0))
    return jnp.concatenate(out, axis=0)

def unstack_heads(x, places, tiles, n):
    pieces = {}
    for h, (tile, half, kv) in enumerate(places):
        piece = x[h * n:(h + 1) * n]
        if half != kv:
            piece = pltpu.roll(piece, HEAD_SIZE, 1)
        pieces[tile, half] = piece
    out = []
    for tile in range(tiles):
        low = pieces[tile, 0]
        high = pieces.get((tile, 1))
        out.append(jnp.where(half_mask(0), low, 0.0 if high is None else high))
    return jnp.concatenate(out, axis=1)

def bwd_kernel(places, tiles, bq, bk, len_ref, q_ref, do_ref, o_ref, linv_ref, k_ref, v_ref, dq_ref, dk_ref, dv_ref, q6, do6, d_row, kx, dq6):
    i = pl.program_id(0)
    rows = k_ref.shape[0]
    heads = len(places)
    @pl.when(i == 0)
    def _():
        live = lax.broadcasted_iota(jnp.int32, (rows, LANES), 0) < len_ref[0]
        kx[...] = jnp.where(live, k_ref[...].astype(F32), 0.0).astype(BF16)
        dk_ref[...] = jnp.zeros_like(dk_ref)
        dv_ref[...] = jnp.zeros_like(dv_ref)
    q6[...] = stack_heads(q_ref[...].astype(F32), places).astype(BF16)
    dob = do_ref[...].astype(F32) * linv_ref[...]
    do6[...] = stack_heads(dob, places).astype(BF16)
    prod = stack_heads(dob * o_ref[...].astype(F32), places)
    hi = prod.astype(BF16)
    lo = (prod - hi.astype(F32)).astype(BF16)
    ones = jnp.ones((16, LANES), BF16)
    d_row[...] = nt(ones, hi) + nt(ones, lo)
    dq6[...] = jnp.zeros_like(dq6)
    def step(j, masked):
        ks = pl.ds(pl.multiple_of(j * bk, bk), bk)
        st = nt(k_ref[ks, :], q6[...])
        pt = jnp.exp2(st * (SCALE * LOG2E))
        if masked:
            kp = j * bk + lax.broadcasted_iota(jnp.int32, st.shape, 0)
            qp = i * bq + (lax.broadcasted_iota(jnp.int32, st.shape, 1) & (bq - 1))
            pt = jnp.where(kp <= qp, pt, 0.0)
        dv_ref[ks, :] += nn(pt.astype(BF16), do6[...])
        dpt = nt(v_ref[ks, :], do6[...])
        dst = (pt * (dpt - d_row[0:1, :])).astype(BF16)
        dk_ref[ks, :] += nn(dst, q6[...])
        dq6[...] += tn(dst, kx[ks, :])
    full = (i * bq) // bk
    @pl.loop(0, full)
    def _(j): step(j, False)
    @pl.loop(full, full + max(bq // bk, 1))
    def _(j): step(j, True)
    dq_ref[...] = unstack_heads(dq6[...] * SCALE, places, tiles, bq)
    @pl.when(i == pl.num_programs(0) - 1)
    def _():
        live = lax.broadcasted_iota(jnp.int32, (rows, LANES), 0) < len_ref[0]
        dk_ref[...] = jnp.where(live, dk_ref[...] * SCALE, 0.0)
        dv_ref[...] = jnp.where(live, dv_ref[...], 0.0)

def attn_bwd(length, q, do, o, linv, k, v, heads, group, bq=256, bk=256):
    rows, width = q.shape
    tiles = width // LANES
    places = head_places(heads, group)
    blk = pl.BlockSpec((bq, width), lambda i, n: (i, 0))
    whole = pl.BlockSpec((rows, LANES), lambda i, n: (0, 0))
    return pl.pallas_call(
        functools.partial(bwd_kernel, places, tiles, bq, bk),
        out_shape=(jax.ShapeDtypeStruct((rows, width), F32), jax.ShapeDtypeStruct((rows, LANES), F32), jax.ShapeDtypeStruct((rows, LANES), F32)),
        grid_spec=pltpu.PrefetchScalarGridSpec(
            num_scalar_prefetch=1, grid=(rows // bq,),
            in_specs=[blk] * 4 + [whole] * 2,
            out_specs=[blk, whole, whole],
            scratch_shapes=[pltpu.VMEM((heads * bq, LANES), BF16), pltpu.VMEM((heads * bq, LANES), BF16),
                            pltpu.VMEM((16, heads * bq), F32), pltpu.VMEM((rows, LANES), BF16),
                            pltpu.VMEM((heads * bq, LANES), F32)]),
        compiler_params=pltpu.CompilerParams(dimension_semantics=("arbitrary",), vmem_limit_bytes=48 << 20),
        cost_estimate=pl.CostEstimate(flops=rows * width, transcendentals=0, bytes_accessed=rows * width * 2),
        name="attention_backward",
    )(length, q, do, o, linv, k, v)


def line_copy(src, dst, sems, where, to):
    return pltpu.make_async_remote_copy(
        src_ref=src,
        dst_ref=dst,
        send_sem=sems[0].at[where],
        recv_sem=sems[1].at[where],
        device_id={"tensor": to},
        device_id_type=MESH,
    )


def greet_line(count, ways=0):
    me = lax.axis_index("tensor")
    barrier = pltpu.get_barrier_semaphore()

    def greet(peer):
        pl.semaphore_signal(barrier, inc=1, device_id={"tensor": peer}, device_id_type=MESH)

    if ways:
        spot = lax.axis_index("dp")
        for peer in range(count):

            @pl.when(peer != me)
            def _():
                greet(peer)

        for peer in range(ways):

            @pl.when(peer != spot)
            def _():
                pl.semaphore_signal(barrier, inc=1, device_id={"dp": peer}, device_id_type=MESH)

        pl.semaphore_wait(barrier, count - 1 + ways - 1)
        return

    @pl.when(me > 0)
    def _():
        greet(me - 1)

    @pl.when(me < count - 1)
    def _():
        greet(me + 1)

    @pl.when((me > 0) & (me < count - 1))
    def _():
        pl.semaphore_wait(barrier, 2)

    @pl.when((me == 0) | (me == count - 1))
    def _():
        pl.semaphore_wait(barrier, 1)


def line_sum_kernel(
    count, pieces, finish, kinds, share_terms, part_ref, *refs
):
    (own_refs, full_ref, out_refs), scratch = split_refs(refs, kinds)
    up_buf, down_buf, acc, shared, shared_ways = scratch[:5]
    sems = scratch[5:]
    ways = shared_ways.shape[0]
    spot = lax.axis_index("dp")
    sum_up, sum_down, give_up, give_down = (sems[0:2], sems[2:4], sems[4:6], sems[6:8])
    me = lax.axis_index("tensor")
    last = count - 1
    own = part_ref.shape[0] // count
    size = own // pieces

    def rows(block, c):
        return pl.ds(pl.multiple_of(block * own + c * size, size), size)

    def sum_copy(c, s, upward):
        buf, sem = (up_buf, sum_up) if upward else (down_buf, sum_down)
        to = me + 1 if upward else me - 1
        return buf, lambda src: line_copy(src, buf.at[c, s - 1], sem, (c, s - 1), to)

    def sum_start(c, s, upward):
        buf, copy = sum_copy(c, s, upward)
        first = me == 0 if upward else me == last
        block = count - s + me if upward else me - (count - s)
        sends = me <= s - 1 if upward else me >= count - s
        sends = sends & (me < last if upward else me > 0)

        @pl.when(sends & first)
        def _():
            copy(part_ref.at[rows(block, c)]).start()

        if s > 1:

            @pl.when(sends & jnp.logical_not(first))
            def _():
                sum_wait(c, s - 1, upward)
                held = buf.at[c, s - 2]
                held[...] = (held[...].astype(F32) + part_ref[rows(block, c), :].astype(F32)).astype(BF16)
                copy(held).start()

    def sum_wait(c, s, upward):
        buf, copy = sum_copy(c, s, upward)
        copy(buf.at[c, s - 1]).wait_recv()

    def give_copy(c, s, upward):
        block = me - s + 1 if upward else me + s - 1
        sem = give_up if upward else give_down
        place = full_ref.at[rows(block, c)]
        return line_copy(place, place, sem, (c, s - 1), me + 1 if upward else me - 1)

    def give_wait(c, s, upward):
        block = me - s if upward else me + s
        sem = give_up if upward else give_down
        place = full_ref.at[rows(block, c)]
        line_copy(place, place, sem, (c, s - 1), me + 1 if upward else me - 1).wait_recv()

    def give_start(c, s, upward):
        sends = (me >= s - 1) & (me < last) if upward else (me > 0) & (me <= count - s)
        if s > 1:
            got = (me >= s - 1) if upward else (me <= count - s)

            @pl.when(got)
            def _():
                give_wait(c, s - 1, upward)

        @pl.when(sends)
        def _():
            give_copy(c, s, upward).start()

    def settle(c):
        acc[...] = part_ref[rows(me, c), :].astype(F32)

        @pl.when(me > 0)
        def _():
            sum_wait(c, last, True)
            acc[...] += up_buf[c, last - 1].astype(F32)

        @pl.when(me < last)
        def _():
            sum_wait(c, last, False)
            acc[...] += down_buf[c, last - 1].astype(F32)

        mine = pl.ds(c * size, size)
        full_ref[rows(me, c), :] = finish(c, mine, acc[...], own_refs, out_refs)

    def share(axis, to, sender, at):
        here, place, sem = (me, shared, 8) if axis == "tensor" else (spot, shared_ways, 10)
        return pltpu.make_async_remote_copy(
            src_ref=out_refs[1],
            dst_ref=place.at[sender],
            send_sem=sems[sem].at[to],
            recv_sem=sems[sem + 1].at[sender],
            device_id={axis: to},
            device_id_type=MESH,
        )

    def share_start(axis, size_of, here):
        for to in range(size_of):

            @pl.when(to != here)
            def _():
                share(axis, to, here, here).start()

    def share_finish(axis, size_of, here, place):
        for peer in range(size_of):

            @pl.when(peer != here)
            def _():
                share(axis, peer, here, here).wait_send()
                share(axis, peer, peer, here).wait_recv()

            @pl.when(peer == here)
            def _():
                place[peer] = out_refs[1][...]

        terms = place[0]
        for peer in range(1, size_of):
            terms = terms + place[peer]
        out_refs[1][...] = terms

    greet_line(count, ways if share_terms else 0)
    for slot in range(pieces + 2 * last):
        if slot < pieces:
            for upward in (True, False):
                sum_start(slot, 1, upward)
        for s in range(last, 1, -1):
            c = slot - last - (s - 1)
            if 0 <= c < pieces:
                for upward in (True, False):
                    give_start(c, s, upward)
        c = slot - last
        if 0 <= c < pieces:
            settle(c)
            for upward in (True, False):
                give_start(c, 1, upward)
            if share_terms and c == pieces - 1:
                share_start("tensor", count, me)
        if share_terms and c == pieces + last - 2:
            share_finish("tensor", count, me, shared)
            share_start("dp", ways, spot)
        for s in range(last, 1, -1):
            c = slot - (s - 1)
            if 0 <= c < pieces:
                for upward in (True, False):
                    sum_start(c, s, upward)
    for c in range(pieces):

        @pl.when(me == last)
        def _():
            give_wait(c, last, True)

        @pl.when(me == 0)
        def _():
            give_wait(c, last, False)

        for s in range(1, count):
            for upward in (True, False):
                sends = me <= s - 1 if upward else me >= count - s
                sends = sends & (me < last if upward else me > 0)

                @pl.when(sends)
                def _():
                    buf, copy = sum_copy(c, s, upward)
                    copy(buf.at[c, s - 1]).wait_send()

                sends = (me >= s - 1) & (me < last) if upward else (me > 0) & (me <= count - s)

                @pl.when(sends)
                def _():
                    give_copy(c, s, upward).wait_send()

    if share_terms:
        share_finish("dp", ways, spot, shared_ways)


def split_refs(refs, kinds):
    n_own, n_out = kinds
    own_refs = refs[:n_own]
    full_ref = refs[n_own]
    out_refs = refs[n_own + 1 : n_own + 1 + n_out]
    return (own_refs, full_ref, out_refs), refs[n_own + 1 + n_out :]


def line_sum(part, owned, outs, finish, pieces, collective_id, share_terms=False):
    count = lax.axis_size("tensor")
    ways = lax.axis_size("dp")
    rows, width = part.shape
    size = rows // count // pieces
    vmem = pl.BlockSpec(memory_space=pltpu.VMEM)
    hops = (pieces, count - 1)
    return pl.pallas_call(
        functools.partial(line_sum_kernel, count, pieces, finish, (len(owned), len(outs)), share_terms),
        out_shape=(jax.ShapeDtypeStruct((rows, width), BF16), *outs),
        in_specs=[vmem] * (1 + len(owned)),
        out_specs=(vmem,) * (1 + len(outs)),
        scratch_shapes=[
            pltpu.VMEM((*hops, size, width), BF16),
            pltpu.VMEM((*hops, size, width), BF16),
            pltpu.VMEM((size, width), F32),
            pltpu.VMEM((count, 8, width), F32),
            pltpu.VMEM((ways, 8, width), F32),
        ]
        + [pltpu.SemaphoreType.DMA(hops)] * 8
        + [pltpu.SemaphoreType.DMA((count,))] * 2
        + [pltpu.SemaphoreType.DMA((ways,))] * 2,
        compiler_params=pltpu.CompilerParams(
            collective_id=collective_id, has_side_effects=True, vmem_limit_bytes=56 << 20
        ),
        cost_estimate=pl.CostEstimate(
            flops=rows * width * 8, transcendentals=0, bytes_accessed=rows * width * 200
        ),
        name="line_sum",
    )(part, *owned)


def finish_back(c, mine, total, own_refs, out_refs):
    base, value, gain = own_refs[:3]
    x = value[mine, :]
    r = inverse_rms(x)
    y = x * r
    e = gain[...] * total
    out = base[mine, :] + r * (e - y * jnp.mean(e * y, axis=-1, keepdims=True))
    out_refs[0][mine, :] = out
    term = jnp.sum(total * y, axis=0, keepdims=True)
    row = lax.broadcasted_iota(jnp.int32, (8, 1), 0)
    if c == 0:
        more = own_refs[3][...] if len(own_refs) > 3 else 0.0
        out_refs[1][...] = jnp.where(row == 0, term, more)
    else:
        out_refs[1][...] += jnp.where(row == 0, term, 0.0)
    return out.astype(BF16)


def attn_gather_kernel(
    count,
    ways,
    places,
    tiles,
    bq,
    len_ref,
    q_ref,
    k_ref,
    v_ref,
    w_ref,
    tokens_ref,
    gain_ref,
    normed_ref,
    resid_ref,
    mixed_ref,
    linv_ref,
    full_ref,
    whole_ref,
    q6,
    vx,
    acc,
    *sems,
):
    give_up, give_down, line_sems, way_sems = sems[0:2], sems[2:4], sems[4:6], sems[6:8]
    load_tokens = pltpu.make_async_copy(tokens_ref, normed_ref, sems[8])
    me = lax.axis_index("tensor")
    spot = lax.axis_index("dp")
    piece = w_ref.shape[0] // ways
    weight_slots = {1: (1,), 3: (2,), 4: tuple(range(3, ways.bit_length() + 1))}
    levels = ways.bit_length() - 1
    last = count - 1
    rows, width = q_ref.shape
    chunks = rows // bq

    def place(block, c):
        at = pl.multiple_of(block * width, width)
        return full_ref.at[pl.ds(c * bq, bq), pl.ds(at, width)]

    def copy(c, s, upward):
        there = place(me - s + 1 if upward else me + s - 1, c)
        sem = give_up if upward else give_down
        return line_copy(there, there, sem, (c, s - 1), me + 1 if upward else me - 1)

    def wait(c, s, upward):
        there = place(me - s if upward else me + s, c)
        sem = give_up if upward else give_down
        line_copy(there, there, sem, (c, s - 1), me + 1 if upward else me - 1).wait_recv()

    def sends(s, upward):
        return (me >= s - 1) & (me < last) if upward else (me > 0) & (me <= count - s)

    def start(c, s, upward):
        if s > 1:

            @pl.when((me >= s - 1) if upward else (me <= count - s))
            def _():
                wait(c, s - 1, upward)

        @pl.when(sends(s, upward))
        def _():
            copy(c, s, upward).start()

    def attend(c):
        first = c * bq
        span = pl.ds(first, bq)
        q6[...] = stack_heads(q_ref[span, :].astype(F32), places).astype(BF16)
        acc[...] = jnp.zeros_like(acc)

        def step(j, masked):
            ks = pl.ds(pl.multiple_of(j * bq, bq), bq)
            prob = jnp.exp2(nt(q6[...], k_ref[ks, :]) * (SCALE * LOG2E))
            if masked:
                q_pos = lax.broadcasted_iota(jnp.int32, prob.shape, 0) & (bq - 1)
                k_pos = lax.broadcasted_iota(jnp.int32, prob.shape, 1)
                prob = jnp.where(k_pos <= q_pos, prob, 0.0)
            acc[...] += nn(prob.astype(BF16), vx[ks, :])

        if c > 0:

            @pl.loop(0, c)
            def _(j):
                step(j, False)

        step(c, True)
        inv = 1.0 / acc[:, LANES:]
        out = unstack_heads(acc[:, :LANES] * inv, places, tiles, bq)
        place(me, c)[...] = out.astype(BF16)
        mixed_ref[span, :] = out.astype(BF16)
        linv_ref[span, :] = unstack_heads(inv, places, tiles, bq)


    bits = [(spot // (1 << (levels - 1 - level))) % 2 for level in range(levels)]

    def own_part(peer, sender):
        return pltpu.make_async_remote_copy(
            src_ref=whole_ref.at[(me, *bits)],
            dst_ref=whole_ref.at[(sender, *bits)],
            send_sem=line_sems[0].at[peer],
            recv_sem=line_sems[1].at[sender],
            device_id={"tensor": peer},
            device_id_type=MESH,
        )

    def partner(level):
        return spot + (1 - 2 * bits[level]) * (1 << (levels - 1 - level))

    def held_parts(level, theirs=False):
        ours = [1 - bits[level] if theirs else bits[level], *bits[level + 1 :]]
        there = whole_ref.at[(slice(None),) * (level + 1) + tuple(ours)]
        return pltpu.make_async_remote_copy(
            src_ref=there,
            dst_ref=there,
            send_sem=way_sems[0].at[level],
            recv_sem=way_sems[1].at[level],
            device_id={"dp": partner(level)},
            device_id_type=MESH,
        )

    def weight_step(step):
        if step == 0:
            mine = pl.ds(pl.multiple_of(spot * piece, piece), piece)
            whole_ref[(me, *bits)] = w_ref[mine, :]
            for peer in range(count):

                @pl.when(peer != me)
                def _():
                    own_part(peer, me).start()

            return
        if step == 1:
            for peer in range(count):

                @pl.when(peer != me)
                def _():
                    own_part(peer, peer).wait_recv()

        else:
            held_parts(step - 2, True).wait_recv()
        if step - 1 < levels:
            held_parts(step - 1).start()

    def project(c):
        @pl.when(me == last)
        def _():
            wait(c, last, True)

        @pl.when(me == 0)
        def _():
            wait(c, last, False)

        span = pl.ds(c * bq, bq)
        resid = normed_ref[span, :].astype(F32)
        for block in range(count):
            weight = whole_ref[block].reshape(width, resid.shape[1])
            resid += nn(full_ref[span, pl.ds(block * width, width)], weight)
        normed_ref[span, :] = (resid * inverse_rms(resid) * gain_ref[...]).astype(BF16)
        own = resid_ref.shape[0]
        for j in range(bq // own):

            @pl.when(me == c * (bq // own) + j)
            def _():
                resid_ref[...] = resid[j * own : (j + 1) * own]

    load_tokens.start()
    barrier = pltpu.get_barrier_semaphore()
    for peer in range(count):

        @pl.when(peer != me)
        def _():
            pl.semaphore_signal(barrier, inc=1, device_id={"tensor": peer}, device_id_type=MESH)

    for level in range(levels):
        pl.semaphore_signal(
            barrier, inc=1, device_id={"dp": partner(level)}, device_id_type=MESH
        )
    pl.semaphore_wait(barrier, count - 1 + levels)
    weight_step(0)
    live = lax.broadcasted_iota(jnp.int32, (rows, LANES), 0) < len_ref[0]
    vx[:, :LANES] = jnp.where(live, v_ref[...].astype(F32), 0.0).astype(BF16)
    vx[:, LANES:] = jnp.where(live, 1.0, 0.0).astype(BF16)
    for slot in range(chunks + last - 1):
        if slot < chunks:
            attend(slot)
            for upward in (True, False):
                start(slot, 1, upward)
        for s in range(last, 1, -1):
            c = slot - (s - 1)
            if 0 <= c < chunks:
                for upward in (True, False):
                    start(c, s, upward)
        for step in weight_slots.get(slot, ()):
            weight_step(step)
        if slot == 4:
            load_tokens.wait()
        if slot >= max(4, last) and slot - max(4, last) < chunks:
            project(slot - max(4, last))
    for c in range(max(0, chunks + last - 1 - max(4, last)), chunks):
        project(c)
    for peer in range(count):

        @pl.when(peer != me)
        def _():
            own_part(peer, me).wait_send()

    for level in range(levels):
        held_parts(level).wait_send()
    for c in range(chunks):
        for s in range(1, count):
            for upward in (True, False):

                @pl.when(sends(s, upward))
                def _():
                    copy(c, s, upward).wait_send()


def attn_gather(length, q, k, v, w, tokens, gain, heads, group, bq, collective_id):
    count = lax.axis_size("tensor")
    ways = lax.axis_size("dp")
    rows, width = q.shape
    model = tokens.shape[1]
    vmem = pl.BlockSpec(memory_space=pltpu.VMEM)
    hops = (rows // bq, count - 1)
    levels = ways.bit_length() - 1
    return pl.pallas_call(
        functools.partial(
            attn_gather_kernel, count, ways, head_places(heads, group), width // LANES, bq
        ),
        out_shape=(
            jax.ShapeDtypeStruct((rows, model), BF16),
            jax.ShapeDtypeStruct((rows // count, model), F32),
            jax.ShapeDtypeStruct((rows, width), BF16),
            jax.ShapeDtypeStruct((rows, width), F32),
        ),
        in_specs=[pl.BlockSpec(memory_space=pltpu.SMEM)]
        + [vmem] * 4
        + [pl.BlockSpec(memory_space=pl.ANY), vmem],
        out_specs=(vmem,) * 4,
        scratch_shapes=[
            pltpu.VMEM((rows, count * width), BF16),
            pltpu.VMEM((count, *(2,) * levels, w.shape[0] // ways, model), BF16),
            pltpu.VMEM((heads * bq, LANES), BF16),
            pltpu.VMEM((rows, 2 * LANES), BF16),
            pltpu.VMEM((heads * bq, 2 * LANES), F32),
        ]
        + [pltpu.SemaphoreType.DMA(hops)] * 4
        + [pltpu.SemaphoreType.DMA((count,))] * 2
        + [pltpu.SemaphoreType.DMA((ways,))] * 2
        + [pltpu.SemaphoreType.DMA(())],
        compiler_params=pltpu.CompilerParams(
            collective_id=collective_id, has_side_effects=True, vmem_limit_bytes=58 << 20
        ),
        cost_estimate=pl.CostEstimate(
            flops=heads * rows * rows * 2 * LANES,
            transcendentals=heads * rows * rows // 2,
            bytes_accessed=rows * count * width * 120,
        ),
        name="attention_gather",
    )(length, q, k, v, w, tokens, gain)


def widen_kernel(after_ref, *refs):
    half = len(refs) // 2
    for narrow, wide in zip(refs[:half], refs[half:]):
        wide[...] = narrow[...].astype(F32)


def widen(arrays, after):
    rows, width = arrays[0].shape
    size = next(s for s in (288, 144, 96, 16, rows) if rows % s == 0)
    block = pl.BlockSpec((size, width), lambda i: (i, 0))
    return pl.pallas_call(
        widen_kernel,
        grid=(rows // size,),
        out_shape=(jax.ShapeDtypeStruct((rows, width), F32),) * len(arrays),
        in_specs=[pl.BlockSpec(after.shape, lambda i: (0, 0))] + [block] * len(arrays),
        out_specs=(block,) * len(arrays),
        compiler_params=pltpu.CompilerParams(
            dimension_semantics=("arbitrary",), vmem_limit_bytes=32 << 20
        ),
        cost_estimate=pl.CostEstimate(flops=rows, transcendentals=0, bytes_accessed=rows * width),
        name="widen",
    )(after, *arrays)


def inverse_rms(x):
    return lax.rsqrt(jnp.mean(x * x, axis=-1, keepdims=True) + EPSILON)


def norm_back(x, r, gain, grad):
    y = x * r
    e = gain * grad
    return r * (e - y * jnp.mean(e * y, axis=-1, keepdims=True)), jnp.sum(grad * y, axis=0)


def rope_tables(row_count):
    half = HEAD_SIZE // 2
    positions = jnp.arange(row_count).astype(F32)[:, None]
    freq = jnp.exp(jnp.arange(half).astype(F32) * (-2.0 * math.log(ROPE_BASE) / HEAD_SIZE))
    angles = positions * freq[None, :]
    return jnp.cos(angles)[:, None, :], jnp.sin(angles)[:, None, :]


def turn(x, cosine, sine):
    half = HEAD_SIZE // 2
    low, high = x[..., :half], x[..., half:]
    return jnp.concatenate([low * cosine - high * sine, high * cosine + low * sine], axis=-1)


def by_head(x):
    return x.reshape(x.shape[0], x.shape[1] // HEAD_SIZE, HEAD_SIZE)


def flat(x):
    return x.reshape(x.shape[0], x.shape[1] * x.shape[2])


def prepare(x, gain, tables):
    heads = by_head(x)
    return flat(turn(heads * inverse_rms(heads) * gain, *tables))


def prepare_back(x, gain, tables, grad):
    heads = by_head(x)
    back = turn(by_head(grad), tables[0], -tables[1])
    dx, d_gain = norm_back(heads, inverse_rms(heads), gain, back)
    return flat(dx), jnp.sum(d_gain, axis=0)


def to_lanes(x):
    short = -x.shape[1] % LANES
    return x if short == 0 else jnp.pad(x, ((0, 0), (0, short)))


def pad_rows(w):
    short = -w.shape[0] % LANES
    return w if short == 0 else jnp.pad(w, ((0, short), (0, 0)))


def on_device(
    tokens,
    lengths,
    cotangent,
    norm_gain,
    query_w,
    key_weight,
    value_weight,
    out_w,
    query_gain,
    key_gain,
    mlp_gain,
    gate_w,
    up_w,
    down_w,
):
    row_count, width = tokens.shape
    me = lax.axis_index("tensor")
    count = lax.axis_size("tensor")
    m = row_count // count
    q_width = query_w.shape[1]
    k_width = key_weight.shape[1]
    heads = q_width // HEAD_SIZE
    group = q_width // k_width
    pieces = 64 // count
    own_shape = jax.ShapeDtypeStruct((m, width), F32)
    gain_shape = jax.ShapeDtypeStruct((8, width), F32)

    def own(x):
        return lax.dynamic_slice_in_dim(x, me * m, m, axis=0)

    live = (jnp.arange(row_count, dtype=jnp.int32) < lengths[0])[:, None]
    d_out = jnp.where(live, cotangent, jnp.zeros_like(cotangent))
    inputs = tokens.astype(F32)
    normed = (inputs * inverse_rms(inputs) * norm_gain).astype(BF16)
    inputs_own = own(tokens).astype(F32)
    qkv_w = jnp.concatenate([query_w, key_weight, value_weight], axis=1)
    edges = (q_width, q_width + k_width)
    queries, keys_val, values = jnp.split(nn(normed, qkv_w), edges, axis=1)
    tables = rope_tables(row_count)
    q_pad = to_lanes(prepare(queries, query_gain, tables).astype(BF16))
    k_pad = to_lanes(prepare(keys_val, key_gain, tables).astype(BF16))
    v_pad = to_lanes(values.astype(BF16))
    normed2, resid_own, mixed_pad, inverse_sums = attn_gather(
        lengths,
        q_pad,
        k_pad,
        v_pad,
        pad_rows(out_w),
        tokens,
        mlp_gain[None],
        heads,
        group,
        min(512, row_count),
        1,
    )
    mixed = mixed_pad[:, :q_width]
    gate = nn(normed2, gate_w)
    up = nn(normed2, up_w)
    sig = jax.nn.sigmoid(gate)
    hidden = (gate * sig * up).astype(BF16)
    mlp_part = nn(hidden, down_w).astype(BF16)
    mlp_part, gate, up = lax.optimization_barrier((mlp_part, gate, up))
    mlp_own = lax.psum_scatter(mlp_part, "tensor", scatter_dimension=0, tiled=True)
    sig = jax.nn.sigmoid(gate)
    d_hidden = nt(d_out, down_w)
    d_gate = (d_hidden * up * sig * (1.0 + gate * (1.0 - sig))).astype(BF16)
    d_up = (d_hidden * gate * sig).astype(BF16)
    d_normed2 = (nt(d_gate, gate_w) + nt(d_up, up_w)).astype(BF16)
    d_normed2, mlp_own = lax.optimization_barrier((d_normed2, mlp_own))
    d_resid, d_resid_own, d_mlp_gain = line_sum(
        d_normed2,
        (own(d_out).astype(F32), resid_own, mlp_gain[None]),
        (own_shape, gain_shape),
        finish_back,
        pieces,
        2,
    )
    g_gate = tn(d_gate, normed2).astype(BF16)
    g_up = tn(d_up, normed2).astype(BF16)
    g_down = tn(hidden, d_out).astype(BF16)
    g_gate, g_up, g_down = lax.psum((g_gate, g_up, g_down), "dp")

    after = d_mlp_gain[7, 0]
    block_own = (resid_own + after + mlp_own.astype(F32)).astype(BF16)
    block_own, d_resid = lax.optimization_barrier((block_own, d_resid))
    block_out = lax.all_gather(block_own, "tensor", axis=0, tiled=True)
    d_mixed = nt(d_resid, out_w).astype(BF16)
    dq, dk, dv = attn_bwd(
        lengths, q_pad, to_lanes(d_mixed), mixed_pad, inverse_sums, k_pad, v_pad, heads, group
    )
    dq, d_qgain = prepare_back(queries, query_gain, tables, dq[:, :q_width])
    dk, d_kgain = prepare_back(keys_val, key_gain, tables, dk[:, :k_width])
    d_q, d_k, d_v = dq.astype(BF16), dk.astype(BF16), dv[:, :k_width].astype(BF16)
    d_qkv = jnp.concatenate([d_q, d_k, d_v], axis=1)
    late_qkv, block_out = lax.optimization_barrier((d_qkv, block_out))
    d_normed = nt(late_qkv, qkv_w).astype(BF16)
    head_terms = jnp.concatenate([d_qgain, d_kgain])
    terms = jnp.concatenate(
        [
            jnp.zeros((1, width), F32),
            d_mlp_gain[:1],
            jnp.pad(head_terms[None], ((0, 0), (0, width - 2 * HEAD_SIZE))),
            jnp.zeros((5, width), F32),
        ]
    )
    whole_grads = widen((g_gate, g_up, g_down), d_mlp_gain)
    d_normed, *whole_grads = lax.optimization_barrier((d_normed, *whole_grads))
    d_inputs, _, d_gains = line_sum(
        d_normed,
        (d_resid_own, inputs_own, norm_gain[None], terms),
        (own_shape, gain_shape),
        finish_back,
        pieces,
        3,
        True,
    )
    g_out = tn(mixed, d_resid).astype(BF16)
    g_qkv = tn(normed, d_qkv).astype(BF16)
    g_out, g_qkv, *whole_grads = lax.optimization_barrier((g_out, g_qkv, *whole_grads))
    g_out, g_qkv = lax.psum((g_out, g_qkv), "dp")
    g_query, g_key, g_value = jnp.split(g_qkv.astype(F32), edges, axis=1)
    return (
        block_out,
        d_inputs.astype(F32),
        d_gains[0],
        g_query,
        g_key,
        g_value,
        g_out.astype(F32),
        d_gains[2, :HEAD_SIZE],
        d_gains[2, HEAD_SIZE : 2 * HEAD_SIZE],
        d_gains[1],
        whole_grads[0].T,
        whole_grads[1].T,
        whole_grads[2],
    )


def solution(mesh):
    rows, whole = P("dp", None), P()
    columns, depth = P(None, "tensor"), P("tensor", None)
    return jax.shard_map(
        on_device,
        mesh=mesh,
        in_specs=(
            rows,
            P("dp"),
            rows,
            whole,
            columns,
            columns,
            columns,
            depth,
            whole,
            whole,
            whole,
            columns,
            columns,
            depth,
        ),
        out_specs=(
            rows,
            rows,
            whole,
            columns,
            columns,
            columns,
            depth,
            whole,
            whole,
            whole,
            columns,
            columns,
            depth,
        ),
        check_vma=False,
    )
```

```python
import functools
import math

import jax
import jax.numpy as jnp
from jax import lax
from jax.experimental import pallas as pl
from jax.experimental.pallas import tpu as pltpu
from jax.sharding import PartitionSpec as P

HEAD_SIZE = 64
LANES = 128
SCALE = HEAD_SIZE**-0.5
LOG2E = math.log2(math.e)
EPSILON = 1e-05
ROPE_BASE = 1000000.0
F32 = jnp.float32
BF16 = jnp.bfloat16
MESH = pl.DeviceIdType.MESH


def nt(a,b): return lax.dot_general(a,b,(((1,),(1,)),((),())),preferred_element_type=F32)
def tn(a,b): return lax.dot_general(a,b,(((0,),(0,)),((),())),preferred_element_type=F32)
def nn(a,b): return lax.dot_general(a,b,(((1,),(0,)),((),())),preferred_element_type=F32)

def head_places(heads, group):
    return [(h // 2, h % 2, h // group) for h in range(heads)]

def half_mask(half, dtype=F32):
    lane = lax.broadcasted_iota(jnp.int32, (1, LANES), 1)
    keep = lane < HEAD_SIZE if half == 0 else lane >= HEAD_SIZE
    return keep

def stack_heads(x, places):
    out = []
    for tile, half, kv in places:
        piece = x[:, tile * LANES:(tile + 1) * LANES]
        if half != kv:
            piece = pltpu.roll(piece, HEAD_SIZE, 1)
        out.append(jnp.where(half_mask(kv), piece, 0.0))
    return jnp.concatenate(out, axis=0)

def unstack_heads(x, places, tiles, n):
    pieces = {}
    for h, (tile, half, kv) in enumerate(places):
        piece = x[h * n:(h + 1) * n]
        if half != kv:
            piece = pltpu.roll(piece, HEAD_SIZE, 1)
        pieces[tile, half] = piece
    out = []
    for tile in range(tiles):
        low = pieces[tile, 0]
        high = pieces.get((tile, 1))
        out.append(jnp.where(half_mask(0), low, 0.0 if high is None else high))
    return jnp.concatenate(out, axis=1)

def bwd_kernel(places, tiles, bq, bk, len_ref, q_ref, do_ref, o_ref, linv_ref, k_ref, v_ref, dq_ref, dk_ref, dv_ref, q6, do6, d_row, kx, dq6):
    i = pl.program_id(0)
    rows = k_ref.shape[0]
    heads = len(places)
    @pl.when(i == 0)
    def _():
        live = lax.broadcasted_iota(jnp.int32, (rows, LANES), 0) < len_ref[0]
        kx[...] = jnp.where(live, k_ref[...].astype(F32), 0.0).astype(BF16)
        dk_ref[...] = jnp.zeros_like(dk_ref)
        dv_ref[...] = jnp.zeros_like(dv_ref)
    q6[...] = stack_heads(q_ref[...].astype(F32), places).astype(BF16)
    dob = do_ref[...].astype(F32) * linv_ref[...]
    do6[...] = stack_heads(dob, places).astype(BF16)
    prod = stack_heads(dob * o_ref[...].astype(F32), places)
    hi = prod.astype(BF16)
    lo = (prod - hi.astype(F32)).astype(BF16)
    ones = jnp.ones((16, LANES), BF16)
    d_row[...] = nt(ones, hi) + nt(ones, lo)
    dq6[...] = jnp.zeros_like(dq6)
    def step(j, masked):
        ks = pl.ds(pl.multiple_of(j * bk, bk), bk)
        st = nt(k_ref[ks, :], q6[...])
        pt = jnp.exp2(st * (SCALE * LOG2E))
        if masked:
            kp = j * bk + lax.broadcasted_iota(jnp.int32, st.shape, 0)
            qp = i * bq + (lax.broadcasted_iota(jnp.int32, st.shape, 1) & (bq - 1))
            pt = jnp.where(kp <= qp, pt, 0.0)
        dv_ref[ks, :] += nn(pt.astype(BF16), do6[...])
        dpt = nt(v_ref[ks, :], do6[...])
        dst = (pt * (dpt - d_row[0:1, :])).astype(BF16)
        dk_ref[ks, :] += nn(dst, q6[...])
        dq6[...] += tn(dst, kx[ks, :])
    full = (i * bq) // bk
    @pl.loop(0, full)
    def _(j): step(j, False)
    @pl.loop(full, full + max(bq // bk, 1))
    def _(j): step(j, True)
    dq_ref[...] = unstack_heads(dq6[...] * SCALE, places, tiles, bq)
    @pl.when(i == pl.num_programs(0) - 1)
    def _():
        live = lax.broadcasted_iota(jnp.int32, (rows, LANES), 0) < len_ref[0]
        dk_ref[...] = jnp.where(live, dk_ref[...] * SCALE, 0.0)
        dv_ref[...] = jnp.where(live, dv_ref[...], 0.0)

def attn_bwd(length, q, do, o, linv, k, v, heads, group, bq=256, bk=256):
    rows, width = q.shape
    tiles = width // LANES
    places = head_places(heads, group)
    blk = pl.BlockSpec((bq, width), lambda i, n: (i, 0))
    whole = pl.BlockSpec((rows, LANES), lambda i, n: (0, 0))
    return pl.pallas_call(
        functools.partial(bwd_kernel, places, tiles, bq, bk),
        out_shape=(jax.ShapeDtypeStruct((rows, width), F32), jax.ShapeDtypeStruct((rows, LANES), F32), jax.ShapeDtypeStruct((rows, LANES), F32)),
        grid_spec=pltpu.PrefetchScalarGridSpec(
            num_scalar_prefetch=1, grid=(rows // bq,),
            in_specs=[blk] * 4 + [whole] * 2,
            out_specs=[blk, whole, whole],
            scratch_shapes=[pltpu.VMEM((heads * bq, LANES), BF16), pltpu.VMEM((heads * bq, LANES), BF16),
                            pltpu.VMEM((16, heads * bq), F32), pltpu.VMEM((rows, LANES), BF16),
                            pltpu.VMEM((heads * bq, LANES), F32)]),
        compiler_params=pltpu.CompilerParams(dimension_semantics=("arbitrary",), vmem_limit_bytes=48 << 20),
        cost_estimate=pl.CostEstimate(flops=rows * width, transcendentals=0, bytes_accessed=rows * width * 2),
        name="attention_backward",
    )(length, q, do, o, linv, k, v)


def line_copy(src, dst, sems, where, to):
    return pltpu.make_async_remote_copy(
        src_ref=src,
        dst_ref=dst,
        send_sem=sems[0].at[where],
        recv_sem=sems[1].at[where],
        device_id={"tensor": to},
        device_id_type=MESH,
    )


def greet_line(count, ways=0):
    me = lax.axis_index("tensor")
    barrier = pltpu.get_barrier_semaphore()

    def greet(peer):
        pl.semaphore_signal(barrier, inc=1, device_id={"tensor": peer}, device_id_type=MESH)

    if ways:
        spot = lax.axis_index("dp")
        for peer in range(count):

            @pl.when(peer != me)
            def _():
                greet(peer)

        for peer in range(ways):

            @pl.when(peer != spot)
            def _():
                pl.semaphore_signal(barrier, inc=1, device_id={"dp": peer}, device_id_type=MESH)

        pl.semaphore_wait(barrier, count - 1 + ways - 1)
        return

    @pl.when(me > 0)
    def _():
        greet(me - 1)

    @pl.when(me < count - 1)
    def _():
        greet(me + 1)

    @pl.when((me > 0) & (me < count - 1))
    def _():
        pl.semaphore_wait(barrier, 2)

    @pl.when((me == 0) | (me == count - 1))
    def _():
        pl.semaphore_wait(barrier, 1)


def line_sum_kernel(
    count, pieces, finish, kinds, share_terms, part_ref, *refs
):
    (own_refs, full_ref, out_refs), scratch = split_refs(refs, kinds)
    up_buf, down_buf, acc, shared, shared_ways = scratch[:5]
    sems = scratch[5:]
    ways = shared_ways.shape[0]
    spot = lax.axis_index("dp")
    sum_up, sum_down, give_up, give_down = (sems[0:2], sems[2:4], sems[4:6], sems[6:8])
    me = lax.axis_index("tensor")
    last = count - 1
    own = part_ref.shape[0] // count
    size = own // pieces

    def rows(block, c):
        return pl.ds(pl.multiple_of(block * own + c * size, size), size)

    def sum_copy(c, s, upward):
        buf, sem = (up_buf, sum_up) if upward else (down_buf, sum_down)
        to = me + 1 if upward else me - 1
        return buf, lambda src: line_copy(src, buf.at[c, s - 1], sem, (c, s - 1), to)

    def sum_start(c, s, upward):
        buf, copy = sum_copy(c, s, upward)
        first = me == 0 if upward else me == last
        block = count - s + me if upward else me - (count - s)
        sends = me <= s - 1 if upward else me >= count - s
        sends = sends & (me < last if upward else me > 0)

        @pl.when(sends & first)
        def _():
            copy(part_ref.at[rows(block, c)]).start()

        if s > 1:

            @pl.when(sends & jnp.logical_not(first))
            def _():
                sum_wait(c, s - 1, upward)
                held = buf.at[c, s - 2]
                held[...] = (held[...].astype(F32) + part_ref[rows(block, c), :].astype(F32)).astype(BF16)
                copy(held).start()

    def sum_wait(c, s, upward):
        buf, copy = sum_copy(c, s, upward)
        copy(buf.at[c, s - 1]).wait_recv()

    def give_copy(c, s, upward):
        block = me - s + 1 if upward else me + s - 1
        sem = give_up if upward else give_down
        place = full_ref.at[rows(block, c)]
        return line_copy(place, place, sem, (c, s - 1), me + 1 if upward else me - 1)

    def give_wait(c, s, upward):
        block = me - s if upward else me + s
        sem = give_up if upward else give_down
        place = full_ref.at[rows(block, c)]
        line_copy(place, place, sem, (c, s - 1), me + 1 if upward else me - 1).wait_recv()

    def give_start(c, s, upward):
        sends = (me >= s - 1) & (me < last) if upward else (me > 0) & (me <= count - s)
        if s > 1:
            got = (me >= s - 1) if upward else (me <= count - s)

            @pl.when(got)
            def _():
                give_wait(c, s - 1, upward)

        @pl.when(sends)
        def _():
            give_copy(c, s, upward).start()

    def settle(c):
        acc[...] = part_ref[rows(me, c), :].astype(F32)

        @pl.when(me > 0)
        def _():
            sum_wait(c, last, True)
            acc[...] += up_buf[c, last - 1].astype(F32)

        @pl.when(me < last)
        def _():
            sum_wait(c, last, False)
            acc[...] += down_buf[c, last - 1].astype(F32)

        mine = pl.ds(pl.multiple_of(c * size, size), size)
        full_ref[rows(me, c), :] = finish(mine, acc[...], own_refs, out_refs)

    def share(axis, to, sender, at):
        here, place, sem = (me, shared, 8) if axis == "tensor" else (spot, shared_ways, 10)
        return pltpu.make_async_remote_copy(
            src_ref=out_refs[1],
            dst_ref=place.at[sender],
            send_sem=sems[sem].at[to],
            recv_sem=sems[sem + 1].at[sender],
            device_id={axis: to},
            device_id_type=MESH,
        )

    def share_start(axis, size_of, here):
        for to in range(size_of):

            @pl.when(to != here)
            def _():
                share(axis, to, here, here).start()

    def share_finish(axis, size_of, here, place):
        for peer in range(size_of):

            @pl.when(peer != here)
            def _():
                share(axis, peer, here, here).wait_send()
                share(axis, peer, peer, here).wait_recv()

            @pl.when(peer == here)
            def _():
                place[peer] = out_refs[1][...]

        terms = place[0]
        for peer in range(1, size_of):
            terms = terms + place[peer]
        out_refs[1][...] = terms

    greet_line(count, ways if share_terms else 0)
    if len(out_refs) > 1:
        out_refs[1][...] = own_refs[3][...] if len(own_refs) > 3 else jnp.zeros_like(out_refs[1])

    def stage(c, run):
        @pl.when((c >= 0) & (c < pieces))
        def _():
            run(c)

    def both(start, s):
        def run(c):
            for upward in (True, False):
                start(c, s, upward)

        return run

    def owner_turn(c):
        settle(c)
        both(give_start, 1)(c)

    @pl.loop(0, pieces + 2 * last)
    def _(slot):
        stage(slot, both(sum_start, 1))
        for s in range(last, 1, -1):
            stage(slot - last - (s - 1), both(give_start, s))
        stage(slot - last, owner_turn)
        if share_terms:

            @pl.when(slot == pieces - 1 + last)
            def _():
                share_start("tensor", count, me)

            @pl.when(slot == pieces + 2 * last - 2)
            def _():
                share_finish("tensor", count, me, shared)
                share_start("dp", ways, spot)

        for s in range(last, 1, -1):
            stage(slot - (s - 1), both(sum_start, s))

    @pl.loop(0, pieces)
    def _(c):
        @pl.when(me == last)
        def _():
            give_wait(c, last, True)

        @pl.when(me == 0)
        def _():
            give_wait(c, last, False)

        for s in range(1, count):
            for upward in (True, False):
                sends = me <= s - 1 if upward else me >= count - s
                sends = sends & (me < last if upward else me > 0)

                @pl.when(sends)
                def _():
                    buf, copy = sum_copy(c, s, upward)
                    copy(buf.at[c, s - 1]).wait_send()

                sends = (me >= s - 1) & (me < last) if upward else (me > 0) & (me <= count - s)

                @pl.when(sends)
                def _():
                    give_copy(c, s, upward).wait_send()

    if share_terms:
        share_finish("dp", ways, spot, shared_ways)


def split_refs(refs, kinds):
    n_own, n_out = kinds
    own_refs = refs[:n_own]
    full_ref = refs[n_own]
    out_refs = refs[n_own + 1 : n_own + 1 + n_out]
    return (own_refs, full_ref, out_refs), refs[n_own + 1 + n_out :]


def line_sum(part, owned, outs, finish, pieces, collective_id, share_terms=False):
    count = lax.axis_size("tensor")
    ways = lax.axis_size("dp")
    rows, width = part.shape
    size = rows // count // pieces
    vmem = pl.BlockSpec(memory_space=pltpu.VMEM)
    hops = (pieces, count - 1)
    return pl.pallas_call(
        functools.partial(line_sum_kernel, count, pieces, finish, (len(owned), len(outs)), share_terms),
        out_shape=(jax.ShapeDtypeStruct((rows, width), BF16), *outs),
        in_specs=[vmem] * (1 + len(owned)),
        out_specs=(vmem,) * (1 + len(outs)),
        scratch_shapes=[
            pltpu.VMEM((*hops, size, width), BF16),
            pltpu.VMEM((*hops, size, width), BF16),
            pltpu.VMEM((size, width), F32),
            pltpu.VMEM((count, 8, width), F32),
            pltpu.VMEM((ways, 8, width), F32),
        ]
        + [pltpu.SemaphoreType.DMA(hops)] * 8
        + [pltpu.SemaphoreType.DMA((count,))] * 2
        + [pltpu.SemaphoreType.DMA((ways,))] * 2,
        compiler_params=pltpu.CompilerParams(
            collective_id=collective_id, has_side_effects=True, vmem_limit_bytes=56 << 20
        ),
        cost_estimate=pl.CostEstimate(
            flops=rows * width * 8, transcendentals=0, bytes_accessed=rows * width * 200
        ),
        name="line_sum",
    )(part, *owned)


def finish_back(mine, total, own_refs, out_refs):
    base, value, gain = own_refs[:3]
    x = value[mine, :].astype(F32)
    r = inverse_rms(x)
    y = x * r
    e = gain[...] * total
    out = base[mine, :].astype(F32) + r * (e - y * jnp.mean(e * y, axis=-1, keepdims=True))
    out_refs[0][mine, :] = out
    out_refs[1][0:1, :] += jnp.sum(total * y, axis=0, keepdims=True)
    return out.astype(BF16)


def attn_gather_kernel(
    count,
    ways,
    places,
    tiles,
    bq,
    len_ref,
    q_ref,
    k_ref,
    v_ref,
    w_ref,
    tokens_ref,
    gain_ref,
    normed_ref,
    resid_ref,
    mixed_ref,
    linv_ref,
    full_ref,
    whole_ref,
    q6,
    vx,
    acc,
    *sems,
):
    give_up, give_down, line_sems, way_sems = sems[0:2], sems[2:4], sems[4:6], sems[6:8]
    load_tokens = pltpu.make_async_copy(tokens_ref, normed_ref, sems[8])
    me = lax.axis_index("tensor")
    spot = lax.axis_index("dp")
    piece = w_ref.shape[0] // ways
    weight_slots = {1: (1,), 3: (2,), 4: tuple(range(3, ways.bit_length() + 1))}
    levels = ways.bit_length() - 1
    last = count - 1
    rows, width = q_ref.shape
    chunks = rows // bq

    def place(block, c):
        at = pl.multiple_of(block * width, width)
        return full_ref.at[pl.ds(c * bq, bq), pl.ds(at, width)]

    def copy(c, s, upward):
        there = place(me - s + 1 if upward else me + s - 1, c)
        sem = give_up if upward else give_down
        return line_copy(there, there, sem, (c, s - 1), me + 1 if upward else me - 1)

    def wait(c, s, upward):
        there = place(me - s if upward else me + s, c)
        sem = give_up if upward else give_down
        line_copy(there, there, sem, (c, s - 1), me + 1 if upward else me - 1).wait_recv()

    def sends(s, upward):
        return (me >= s - 1) & (me < last) if upward else (me > 0) & (me <= count - s)

    def start(c, s, upward):
        if s > 1:

            @pl.when((me >= s - 1) if upward else (me <= count - s))
            def _():
                wait(c, s - 1, upward)

        @pl.when(sends(s, upward))
        def _():
            copy(c, s, upward).start()

    def attend(c):
        first = c * bq
        span = pl.ds(first, bq)
        q6[...] = stack_heads(q_ref[span, :].astype(F32), places).astype(BF16)
        acc[...] = jnp.zeros_like(acc)

        def step(j, masked):
            ks = pl.ds(pl.multiple_of(j * bq, bq), bq)
            prob = jnp.exp2(nt(q6[...], k_ref[ks, :]) * (SCALE * LOG2E))
            if masked:
                q_pos = lax.broadcasted_iota(jnp.int32, prob.shape, 0) & (bq - 1)
                k_pos = lax.broadcasted_iota(jnp.int32, prob.shape, 1)
                prob = jnp.where(k_pos <= q_pos, prob, 0.0)
            acc[...] += nn(prob.astype(BF16), vx[ks, :])

        if c > 0:

            @pl.loop(0, c)
            def _(j):
                step(j, False)

        step(c, True)
        inv = 1.0 / acc[:, LANES:]
        out = unstack_heads(acc[:, :LANES] * inv, places, tiles, bq)
        place(me, c)[...] = out.astype(BF16)
        mixed_ref[span, :] = out.astype(BF16)
        linv_ref[span, :] = unstack_heads(inv, places, tiles, bq)


    bits = [(spot // (1 << (levels - 1 - level))) % 2 for level in range(levels)]

    def own_part(peer, sender):
        return pltpu.make_async_remote_copy(
            src_ref=whole_ref.at[(me, *bits)],
            dst_ref=whole_ref.at[(sender, *bits)],
            send_sem=line_sems[0].at[peer],
            recv_sem=line_sems[1].at[sender],
            device_id={"tensor": peer},
            device_id_type=MESH,
        )

    def partner(level):
        return spot + (1 - 2 * bits[level]) * (1 << (levels - 1 - level))

    def held_parts(level, theirs=False):
        ours = [1 - bits[level] if theirs else bits[level], *bits[level + 1 :]]
        there = whole_ref.at[(slice(None),) * (level + 1) + tuple(ours)]
        return pltpu.make_async_remote_copy(
            src_ref=there,
            dst_ref=there,
            send_sem=way_sems[0].at[level],
            recv_sem=way_sems[1].at[level],
            device_id={"dp": partner(level)},
            device_id_type=MESH,
        )

    def weight_step(step):
        if step == 0:
            mine = pl.ds(pl.multiple_of(spot * piece, piece), piece)
            whole_ref[(me, *bits)] = w_ref[mine, :]
            for peer in range(count):

                @pl.when(peer != me)
                def _():
                    own_part(peer, me).start()

            return
        if step == 1:
            for peer in range(count):

                @pl.when(peer != me)
                def _():
                    own_part(peer, peer).wait_recv()

        else:
            held_parts(step - 2, True).wait_recv()
        if step - 1 < levels:
            held_parts(step - 1).start()

    def project(c):
        @pl.when(me == last)
        def _():
            wait(c, last, True)

        @pl.when(me == 0)
        def _():
            wait(c, last, False)

        span = pl.ds(c * bq, bq)
        resid = normed_ref[span, :].astype(F32)
        for block in range(count):
            weight = whole_ref[block].reshape(width, resid.shape[1])
            resid += nn(full_ref[span, pl.ds(block * width, width)], weight)
        normed_ref[span, :] = (resid * inverse_rms(resid) * gain_ref[...]).astype(BF16)
        own = resid_ref.shape[0]
        for j in range(bq // own):

            @pl.when(me == c * (bq // own) + j)
            def _():
                resid_ref[...] = resid[j * own : (j + 1) * own]

    load_tokens.start()
    barrier = pltpu.get_barrier_semaphore()
    for peer in range(count):

        @pl.when(peer != me)
        def _():
            pl.semaphore_signal(barrier, inc=1, device_id={"tensor": peer}, device_id_type=MESH)

    for level in range(levels):
        pl.semaphore_signal(
            barrier, inc=1, device_id={"dp": partner(level)}, device_id_type=MESH
        )
    pl.semaphore_wait(barrier, count - 1 + levels)
    weight_step(0)
    live = lax.broadcasted_iota(jnp.int32, (rows, LANES), 0) < len_ref[0]
    vx[:, :LANES] = jnp.where(live, v_ref[...].astype(F32), 0.0).astype(BF16)
    vx[:, LANES:] = jnp.where(live, 1.0, 0.0).astype(BF16)
    for slot in range(chunks + last - 1):
        if slot < chunks:
            attend(slot)
            for upward in (True, False):
                start(slot, 1, upward)
        for s in range(last, 1, -1):
            c = slot - (s - 1)
            if 0 <= c < chunks:
                for upward in (True, False):
                    start(c, s, upward)
        for step in weight_slots.get(slot, ()):
            weight_step(step)
        if slot == 4:
            load_tokens.wait()
        if slot >= max(4, last) and slot - max(4, last) < chunks:
            project(slot - max(4, last))
    for c in range(max(0, chunks + last - 1 - max(4, last)), chunks):
        project(c)
    for peer in range(count):

        @pl.when(peer != me)
        def _():
            own_part(peer, me).wait_send()

    for level in range(levels):
        held_parts(level).wait_send()
    for c in range(chunks):
        for s in range(1, count):
            for upward in (True, False):

                @pl.when(sends(s, upward))
                def _():
                    copy(c, s, upward).wait_send()


def attn_gather(length, q, k, v, w, tokens, gain, heads, group, bq, collective_id):
    count = lax.axis_size("tensor")
    ways = lax.axis_size("dp")
    rows, width = q.shape
    model = tokens.shape[1]
    vmem = pl.BlockSpec(memory_space=pltpu.VMEM)
    hops = (rows // bq, count - 1)
    levels = ways.bit_length() - 1
    return pl.pallas_call(
        functools.partial(
            attn_gather_kernel, count, ways, head_places(heads, group), width // LANES, bq
        ),
        out_shape=(
            jax.ShapeDtypeStruct((rows, model), BF16),
            jax.ShapeDtypeStruct((rows // count, model), F32),
            jax.ShapeDtypeStruct((rows, width), BF16),
            jax.ShapeDtypeStruct((rows, width), F32),
        ),
        in_specs=[pl.BlockSpec(memory_space=pltpu.SMEM)]
        + [vmem] * 4
        + [pl.BlockSpec(memory_space=pl.ANY), vmem],
        out_specs=(vmem,) * 4,
        scratch_shapes=[
            pltpu.VMEM((rows, count * width), BF16),
            pltpu.VMEM((count, *(2,) * levels, w.shape[0] // ways, model), BF16),
            pltpu.VMEM((heads * bq, LANES), BF16),
            pltpu.VMEM((rows, 2 * LANES), BF16),
            pltpu.VMEM((heads * bq, 2 * LANES), F32),
        ]
        + [pltpu.SemaphoreType.DMA(hops)] * 4
        + [pltpu.SemaphoreType.DMA((count,))] * 2
        + [pltpu.SemaphoreType.DMA((ways,))] * 2
        + [pltpu.SemaphoreType.DMA(())],
        compiler_params=pltpu.CompilerParams(
            collective_id=collective_id, has_side_effects=True, vmem_limit_bytes=58 << 20
        ),
        cost_estimate=pl.CostEstimate(
            flops=heads * rows * rows * 2 * LANES,
            transcendentals=heads * rows * rows // 2,
            bytes_accessed=rows * count * width * 120,
        ),
        name="attention_gather",
    )(length, q, k, v, w, tokens, gain)


def widen_kernel(after_ref, *refs):
    half = len(refs) // 2
    for narrow, wide in zip(refs[:half], refs[half:]):
        wide[...] = narrow[...].astype(wide.dtype)


def widen(arrays, types, sizes, after):
    rows, width = arrays[0].shape
    size = next(s for s in (*sizes, rows) if rows % s == 0)
    block = pl.BlockSpec((size, width), lambda i: (i, 0))
    return pl.pallas_call(
        widen_kernel,
        grid=(rows // size,),
        out_shape=tuple(jax.ShapeDtypeStruct((rows, width), t) for t in types),
        in_specs=[pl.BlockSpec((8, LANES), lambda i: (0, 0))] + [block] * len(arrays),
        out_specs=(block,) * len(arrays),
        compiler_params=pltpu.CompilerParams(
            dimension_semantics=("arbitrary",), vmem_limit_bytes=58 << 20
        ),
        cost_estimate=pl.CostEstimate(flops=rows, transcendentals=0, bytes_accessed=rows * width),
        name="widen",
    )(after, *arrays)


def inverse_rms(x):
    return lax.rsqrt(jnp.mean(x * x, axis=-1, keepdims=True) + EPSILON)


def norm_back(x, r, gain, grad):
    y = x * r
    e = gain * grad
    return r * (e - y * jnp.mean(e * y, axis=-1, keepdims=True)), jnp.sum(grad * y, axis=0)


def rope_tables(row_count):
    half = HEAD_SIZE // 2
    positions = jnp.arange(row_count).astype(F32)[:, None]
    freq = jnp.exp(jnp.arange(half).astype(F32) * (-2.0 * math.log(ROPE_BASE) / HEAD_SIZE))
    angles = positions * freq[None, :]
    return jnp.cos(angles)[:, None, :], jnp.sin(angles)[:, None, :]


def turn(x, cosine, sine):
    half = HEAD_SIZE // 2
    low, high = x[..., :half], x[..., half:]
    return jnp.concatenate([low * cosine - high * sine, high * cosine + low * sine], axis=-1)


def by_head(x):
    return x.reshape(x.shape[0], x.shape[1] // HEAD_SIZE, HEAD_SIZE)


def flat(x):
    return x.reshape(x.shape[0], x.shape[1] * x.shape[2])


def prepare(x, gain, tables):
    heads = by_head(x)
    return flat(turn(heads * inverse_rms(heads) * gain, *tables))


def prepare_back(x, gain, tables, grad):
    heads = by_head(x)
    back = turn(by_head(grad), tables[0], -tables[1])
    dx, d_gain = norm_back(heads, inverse_rms(heads), gain, back)
    return flat(dx), jnp.sum(d_gain, axis=0)


def to_lanes(x):
    short = -x.shape[1] % LANES
    return x if short == 0 else jnp.pad(x, ((0, 0), (0, short)))


def pad_rows(w):
    short = -w.shape[0] % LANES
    return w if short == 0 else jnp.pad(w, ((0, short), (0, 0)))


def on_device(
    tokens,
    lengths,
    cotangent,
    norm_gain,
    query_w,
    key_weight,
    value_weight,
    out_w,
    query_gain,
    key_gain,
    mlp_gain,
    gate_w,
    up_w,
    down_w,
):
    row_count, width = tokens.shape
    me = lax.axis_index("tensor")
    count = lax.axis_size("tensor")
    m = row_count // count
    q_width = query_w.shape[1]
    k_width = key_weight.shape[1]
    heads = q_width // HEAD_SIZE
    group = q_width // k_width
    pieces = 64 // count
    own_shape = jax.ShapeDtypeStruct((m, width), F32)
    gain_shape = jax.ShapeDtypeStruct((8, width), F32)

    def own(x):
        return lax.dynamic_slice_in_dim(x, me * m, m, axis=0)

    live = (jnp.arange(row_count, dtype=jnp.int32) < lengths[0])[:, None]
    d_out = jnp.where(live, cotangent, jnp.zeros_like(cotangent))
    inputs = tokens.astype(F32)
    normed = (inputs * inverse_rms(inputs) * norm_gain).astype(BF16)
    inputs_own = own(tokens)
    qkv_w = jnp.concatenate([query_w, key_weight, value_weight], axis=1)
    edges = (q_width, q_width + k_width)
    queries, keys_val, values = jnp.split(nn(normed, qkv_w), edges, axis=1)
    tables = rope_tables(row_count)
    q_pad = to_lanes(prepare(queries, query_gain, tables).astype(BF16))
    k_pad = to_lanes(prepare(keys_val, key_gain, tables).astype(BF16))
    v_pad = to_lanes(values.astype(BF16))
    normed2, resid_own, mixed_pad, inverse_sums = attn_gather(
        lengths,
        q_pad,
        k_pad,
        v_pad,
        pad_rows(out_w),
        tokens,
        mlp_gain[None],
        heads,
        group,
        min(512, row_count),
        1,
    )
    mixed = mixed_pad[:, :q_width]
    gate = nn(normed2, gate_w)
    up = nn(normed2, up_w)
    sig = jax.nn.sigmoid(gate)
    hidden = (gate * sig * up).astype(BF16)
    mlp_part = nn(hidden, down_w).astype(BF16)
    mlp_part, gate, up = lax.optimization_barrier((mlp_part, gate, up))
    mlp_own = lax.psum_scatter(mlp_part, "tensor", scatter_dimension=0, tiled=True)
    sig = jax.nn.sigmoid(gate)
    d_hidden = nt(d_out, down_w)
    d_gate = (d_hidden * up * sig * (1.0 + gate * (1.0 - sig))).astype(BF16)
    d_up = (d_hidden * gate * sig).astype(BF16)
    d_normed2 = (nt(d_gate, gate_w) + nt(d_up, up_w)).astype(BF16)
    d_normed2, mlp_own = lax.optimization_barrier((d_normed2, mlp_own))
    d_resid, d_resid_own, d_mlp_gain = line_sum(
        d_normed2,
        (own(d_out), resid_own, mlp_gain[None]),
        (own_shape, gain_shape),
        finish_back,
        pieces,
        2,
    )
    g_gate = tn(d_gate, normed2).astype(BF16)
    g_up = tn(d_up, normed2).astype(BF16)
    g_down = tn(hidden, d_out).astype(BF16)
    g_gate, g_up, g_down = lax.psum((g_gate, g_up, g_down), "dp")

    after = d_mlp_gain[7, 0]
    block_own = (resid_own + after + mlp_own.astype(F32)).astype(BF16)
    block_own, d_resid = lax.optimization_barrier((block_own, d_resid))
    block_out = lax.all_gather(block_own, "tensor", axis=0, tiled=True)
    d_mixed = nt(d_resid, out_w).astype(BF16)
    dq, dk, dv = attn_bwd(
        lengths, q_pad, to_lanes(d_mixed), mixed_pad, inverse_sums, k_pad, v_pad, heads, group
    )
    dq, d_qgain = prepare_back(queries, query_gain, tables, dq[:, :q_width])
    dk, d_kgain = prepare_back(keys_val, key_gain, tables, dk[:, :k_width])
    d_q, d_k, d_v = dq.astype(BF16), dk.astype(BF16), dv[:, :k_width].astype(BF16)
    d_qkv = jnp.concatenate([d_q, d_k, d_v], axis=1)
    late_qkv, block_out = lax.optimization_barrier((d_qkv, block_out))
    d_normed = nt(late_qkv, qkv_w).astype(BF16)
    head_terms = jnp.concatenate([d_qgain, d_kgain])
    terms = jnp.concatenate(
        [
            jnp.zeros((1, width), F32),
            d_mlp_gain[:1],
            jnp.pad(head_terms[None], ((0, 0), (0, width - 2 * HEAD_SIZE))),
            jnp.zeros((5, width), F32),
        ]
    )
    whole_grads = widen((g_gate, g_up, g_down), (F32,) * 3, (96,), d_mlp_gain)
    d_normed, *whole_grads = lax.optimization_barrier((d_normed, *whole_grads))
    d_inputs, _, d_gains = line_sum(
        d_normed,
        (d_resid_own, inputs_own, norm_gain[None], terms),
        (own_shape, gain_shape),
        finish_back,
        pieces,
        3,
        True,
    )
    g_out = tn(mixed, d_resid).astype(BF16)
    g_qkv = tn(normed, d_qkv).astype(BF16)
    g_out, g_qkv, *whole_grads = lax.optimization_barrier((g_out, g_qkv, *whole_grads))
    g_out, g_qkv = lax.psum((g_out, g_qkv), "dp")
    g_query, g_key, g_value = (g.astype(F32) for g in jnp.split(g_qkv, edges, axis=1))
    d_inputs, block_out = widen((d_inputs, block_out), (F32, BF16), (256,), d_gains)
    return (
        block_out,
        d_inputs,
        d_gains[0],
        g_query,
        g_key,
        g_value,
        g_out.astype(F32),
        d_gains[2, :HEAD_SIZE],
        d_gains[2, HEAD_SIZE : 2 * HEAD_SIZE],
        d_gains[1],
        whole_grads[0].T,
        whole_grads[1].T,
        whole_grads[2],
    )


def solution(mesh):
    rows, whole = P("dp", None), P()
    columns, depth = P(None, "tensor"), P("tensor", None)
    return jax.shard_map(
        on_device,
        mesh=mesh,
        in_specs=(
            rows,
            P("dp"),
            rows,
            whole,
            columns,
            columns,
            columns,
            depth,
            whole,
            whole,
            whole,
            columns,
            columns,
            depth,
        ),
        out_specs=(
            rows,
            rows,
            whole,
            columns,
            columns,
            columns,
            depth,
            whole,
            whole,
            whole,
            columns,
            columns,
            depth,
        ),
        check_vma=False,
    )
```

```python
import functools
import math

import jax
import jax.numpy as jnp
from jax import lax
from jax.experimental import pallas as pl
from jax.experimental.pallas import tpu as pltpu
from jax.sharding import PartitionSpec as P

HEAD_SIZE = 64
LANES = 128
SCALE = HEAD_SIZE**-0.5
LOG2E = math.log2(math.e)
EPSILON = 1e-05
ROPE_BASE = 1000000.0
F32 = jnp.float32
BF16 = jnp.bfloat16
MESH = pl.DeviceIdType.MESH


def nt(a,b): return lax.dot_general(a,b,(((1,),(1,)),((),())),preferred_element_type=F32)
def tn(a,b): return lax.dot_general(a,b,(((0,),(0,)),((),())),preferred_element_type=F32)
def nn(a,b): return lax.dot_general(a,b,(((1,),(0,)),((),())),preferred_element_type=F32)

def head_places(heads, group):
    return [(h // 2, h % 2, h // group) for h in range(heads)]

def half_mask(half, dtype=F32):
    lane = lax.broadcasted_iota(jnp.int32, (1, LANES), 1)
    keep = lane < HEAD_SIZE if half == 0 else lane >= HEAD_SIZE
    return keep

def stack_heads(x, places):
    out = []
    for tile, half, kv in places:
        piece = x[:, tile * LANES:(tile + 1) * LANES]
        if half != kv:
            piece = pltpu.roll(piece, HEAD_SIZE, 1)
        out.append(jnp.where(half_mask(kv), piece, 0.0))
    return jnp.concatenate(out, axis=0)

def unstack_heads(x, places, tiles, n):
    pieces = {}
    for h, (tile, half, kv) in enumerate(places):
        piece = x[h * n:(h + 1) * n]
        if half != kv:
            piece = pltpu.roll(piece, HEAD_SIZE, 1)
        pieces[tile, half] = piece
    out = []
    for tile in range(tiles):
        low = pieces[tile, 0]
        high = pieces.get((tile, 1))
        out.append(jnp.where(half_mask(0), low, 0.0 if high is None else high))
    return jnp.concatenate(out, axis=1)

def bwd_kernel(places, tiles, bq, bk, len_ref, q_ref, do_ref, o_ref, linv_ref, k_ref, v_ref, dq_ref, dk_ref, dv_ref, q6, do6, d_row, kx, dq6):
    i = pl.program_id(0)
    rows = k_ref.shape[0]
    heads = len(places)
    @pl.when(i == 0)
    def _():
        live = lax.broadcasted_iota(jnp.int32, (rows, LANES), 0) < len_ref[0]
        kx[...] = jnp.where(live, k_ref[...].astype(F32), 0.0).astype(BF16)
        dk_ref[...] = jnp.zeros_like(dk_ref)
        dv_ref[...] = jnp.zeros_like(dv_ref)
    q6[...] = stack_heads(q_ref[...].astype(F32), places).astype(BF16)
    dob = do_ref[...].astype(F32) * linv_ref[...]
    do6[...] = stack_heads(dob, places).astype(BF16)
    prod = stack_heads(dob * o_ref[...].astype(F32), places)
    hi = prod.astype(BF16)
    lo = (prod - hi.astype(F32)).astype(BF16)
    ones = jnp.ones((16, LANES), BF16)
    d_row[...] = nt(ones, hi) + nt(ones, lo)
    dq6[...] = jnp.zeros_like(dq6)
    def step(j, masked):
        ks = pl.ds(pl.multiple_of(j * bk, bk), bk)
        st = nt(k_ref[ks, :], q6[...])
        pt = jnp.exp2(st * (SCALE * LOG2E))
        if masked:
            kp = j * bk + lax.broadcasted_iota(jnp.int32, st.shape, 0)
            qp = i * bq + (lax.broadcasted_iota(jnp.int32, st.shape, 1) & (bq - 1))
            pt = jnp.where(kp <= qp, pt, 0.0)
        dv_ref[ks, :] += nn(pt.astype(BF16), do6[...])
        dpt = nt(v_ref[ks, :], do6[...])
        dst = (pt * (dpt - d_row[0:1, :])).astype(BF16)
        dk_ref[ks, :] += nn(dst, q6[...])
        dq6[...] += tn(dst, kx[ks, :])
    full = (i * bq) // bk
    @pl.loop(0, full)
    def _(j): step(j, False)
    @pl.loop(full, full + max(bq // bk, 1))
    def _(j): step(j, True)
    dq_ref[...] = unstack_heads(dq6[...] * SCALE, places, tiles, bq)
    @pl.when(i == pl.num_programs(0) - 1)
    def _():
        live = lax.broadcasted_iota(jnp.int32, (rows, LANES), 0) < len_ref[0]
        dk_ref[...] = jnp.where(live, dk_ref[...] * SCALE, 0.0)
        dv_ref[...] = jnp.where(live, dv_ref[...], 0.0)

def attn_bwd(length, q, do, o, linv, k, v, heads, group, bq=256, bk=256):
    rows, width = q.shape
    tiles = width // LANES
    places = head_places(heads, group)
    blk = pl.BlockSpec((bq, width), lambda i, n: (i, 0))
    whole = pl.BlockSpec((rows, LANES), lambda i, n: (0, 0))
    return pl.pallas_call(
        functools.partial(bwd_kernel, places, tiles, bq, bk),
        out_shape=(jax.ShapeDtypeStruct((rows, width), F32), jax.ShapeDtypeStruct((rows, LANES), F32), jax.ShapeDtypeStruct((rows, LANES), F32)),
        grid_spec=pltpu.PrefetchScalarGridSpec(
            num_scalar_prefetch=1, grid=(rows // bq,),
            in_specs=[blk] * 4 + [whole] * 2,
            out_specs=[blk, whole, whole],
            scratch_shapes=[pltpu.VMEM((heads * bq, LANES), BF16), pltpu.VMEM((heads * bq, LANES), BF16),
                            pltpu.VMEM((16, heads * bq), F32), pltpu.VMEM((rows, LANES), BF16),
                            pltpu.VMEM((heads * bq, LANES), F32)]),
        compiler_params=pltpu.CompilerParams(dimension_semantics=("arbitrary",), vmem_limit_bytes=48 << 20),
        cost_estimate=pl.CostEstimate(flops=rows * width, transcendentals=0, bytes_accessed=rows * width * 2),
        name="attention_backward",
    )(length, q, do, o, linv, k, v)


def line_copy(src, dst, sems, where, to):
    return pltpu.make_async_remote_copy(
        src_ref=src,
        dst_ref=dst,
        send_sem=sems[0].at[where],
        recv_sem=sems[1].at[where],
        device_id={"tensor": to},
        device_id_type=MESH,
    )


def greet_line(count, ways=0):
    me = lax.axis_index("tensor")
    barrier = pltpu.get_barrier_semaphore()

    def greet(peer):
        pl.semaphore_signal(barrier, inc=1, device_id={"tensor": peer}, device_id_type=MESH)

    if ways:
        spot = lax.axis_index("dp")
        for peer in range(count):

            @pl.when(peer != me)
            def _():
                greet(peer)

        for peer in range(ways):

            @pl.when(peer != spot)
            def _():
                pl.semaphore_signal(barrier, inc=1, device_id={"dp": peer}, device_id_type=MESH)

        pl.semaphore_wait(barrier, count - 1 + ways - 1)
        return

    @pl.when(me > 0)
    def _():
        greet(me - 1)

    @pl.when(me < count - 1)
    def _():
        greet(me + 1)

    @pl.when((me > 0) & (me < count - 1))
    def _():
        pl.semaphore_wait(barrier, 2)

    @pl.when((me == 0) | (me == count - 1))
    def _():
        pl.semaphore_wait(barrier, 1)


def line_sum_kernel(
    count, pieces, finish, kinds, share_terms, part_ref, *refs
):
    (own_refs, full_ref, out_refs), scratch = split_refs(refs, kinds)
    up_buf, down_buf, acc, shared, shared_ways = scratch[:5]
    sems = scratch[5:]
    ways = shared_ways.shape[0]
    spot = lax.axis_index("dp")
    sum_up, sum_down, give_up, give_down = (sems[0:2], sems[2:4], sems[4:6], sems[6:8])
    me = lax.axis_index("tensor")
    last = count - 1
    own = part_ref.shape[0] // count
    size = own // pieces

    def rows(block, c):
        return pl.ds(pl.multiple_of(block * own + c * size, size), size)

    def sum_copy(c, s, upward):
        buf, sem = (up_buf, sum_up) if upward else (down_buf, sum_down)
        to = me + 1 if upward else me - 1
        return buf, lambda src: line_copy(src, buf.at[c, s - 1], sem, (c, s - 1), to)

    def sum_start(c, s, upward):
        buf, copy = sum_copy(c, s, upward)
        first = me == 0 if upward else me == last
        block = count - s + me if upward else me - (count - s)
        sends = me <= s - 1 if upward else me >= count - s
        sends = sends & (me < last if upward else me > 0)

        @pl.when(sends & first)
        def _():
            copy(part_ref.at[rows(block, c)]).start()

        if s > 1:

            @pl.when(sends & jnp.logical_not(first))
            def _():
                sum_wait(c, s - 1, upward)
                held = buf.at[c, s - 2]
                held[...] = (held[...].astype(F32) + part_ref[rows(block, c), :].astype(F32)).astype(BF16)
                copy(held).start()

    def sum_wait(c, s, upward):
        buf, copy = sum_copy(c, s, upward)
        copy(buf.at[c, s - 1]).wait_recv()

    def give_copy(c, s, upward):
        block = me - s + 1 if upward else me + s - 1
        sem = give_up if upward else give_down
        place = full_ref.at[rows(block, c)]
        return line_copy(place, place, sem, (c, s - 1), me + 1 if upward else me - 1)

    def give_wait(c, s, upward):
        block = me - s if upward else me + s
        sem = give_up if upward else give_down
        place = full_ref.at[rows(block, c)]
        line_copy(place, place, sem, (c, s - 1), me + 1 if upward else me - 1).wait_recv()

    def give_start(c, s, upward):
        sends = (me >= s - 1) & (me < last) if upward else (me > 0) & (me <= count - s)
        if s > 1:
            got = (me >= s - 1) if upward else (me <= count - s)

            @pl.when(got)
            def _():
                give_wait(c, s - 1, upward)

        @pl.when(sends)
        def _():
            give_copy(c, s, upward).start()

    def settle(c):
        acc[...] = part_ref[rows(me, c), :].astype(F32)

        @pl.when(me > 0)
        def _():
            sum_wait(c, last, True)
            acc[...] += up_buf[c, last - 1].astype(F32)

        @pl.when(me < last)
        def _():
            sum_wait(c, last, False)
            acc[...] += down_buf[c, last - 1].astype(F32)

        mine = pl.ds(pl.multiple_of(c * size, size), size)
        full_ref[rows(me, c), :] = finish(mine, acc[...], own_refs, out_refs)

    def share(axis, to, sender, at):
        here, place, sem = (me, shared, 8) if axis == "tensor" else (spot, shared_ways, 10)
        return pltpu.make_async_remote_copy(
            src_ref=out_refs[1],
            dst_ref=place.at[sender],
            send_sem=sems[sem].at[to],
            recv_sem=sems[sem + 1].at[sender],
            device_id={axis: to},
            device_id_type=MESH,
        )

    def share_start(axis, size_of, here):
        for to in range(size_of):

            @pl.when(to != here)
            def _():
                share(axis, to, here, here).start()

    def share_finish(axis, size_of, here, place):
        for peer in range(size_of):

            @pl.when(peer != here)
            def _():
                share(axis, peer, here, here).wait_send()
                share(axis, peer, peer, here).wait_recv()

            @pl.when(peer == here)
            def _():
                place[peer] = out_refs[1][...]

        terms = place[0]
        for peer in range(1, size_of):
            terms = terms + place[peer]
        out_refs[1][...] = terms

    greet_line(count, ways if share_terms else 0)
    if len(out_refs) > 1:
        out_refs[1][...] = own_refs[3][...] if len(own_refs) > 3 else jnp.zeros_like(out_refs[1])

    def stage(c, run):
        @pl.when((c >= 0) & (c < pieces))
        def _():
            run(c)

    def both(start, s):
        def run(c):
            for upward in (True, False):
                start(c, s, upward)

        return run

    def owner_turn(c):
        settle(c)
        both(give_start, 1)(c)

    @pl.loop(0, pieces + 2 * last)
    def _(slot):
        stage(slot, both(sum_start, 1))
        for s in range(last, 1, -1):
            stage(slot - last - (s - 1), both(give_start, s))
        stage(slot - last, owner_turn)
        if share_terms:

            @pl.when(slot == pieces - 1 + last)
            def _():
                share_start("tensor", count, me)

            @pl.when(slot == pieces + 2 * last - 2)
            def _():
                share_finish("tensor", count, me, shared)
                share_start("dp", ways, spot)

        for s in range(last, 1, -1):
            stage(slot - (s - 1), both(sum_start, s))

    @pl.loop(0, pieces)
    def _(c):
        @pl.when(me == last)
        def _():
            give_wait(c, last, True)

        @pl.when(me == 0)
        def _():
            give_wait(c, last, False)

        for s in range(1, count):
            for upward in (True, False):
                sends = me <= s - 1 if upward else me >= count - s
                sends = sends & (me < last if upward else me > 0)

                @pl.when(sends)
                def _():
                    buf, copy = sum_copy(c, s, upward)
                    copy(buf.at[c, s - 1]).wait_send()

                sends = (me >= s - 1) & (me < last) if upward else (me > 0) & (me <= count - s)

                @pl.when(sends)
                def _():
                    give_copy(c, s, upward).wait_send()

    if share_terms:
        share_finish("dp", ways, spot, shared_ways)


def split_refs(refs, kinds):
    n_own, n_out = kinds
    own_refs = refs[:n_own]
    full_ref = refs[n_own]
    out_refs = refs[n_own + 1 : n_own + 1 + n_out]
    return (own_refs, full_ref, out_refs), refs[n_own + 1 + n_out :]


def line_sum(part, owned, outs, finish, pieces, collective_id, share_terms=False):
    count = lax.axis_size("tensor")
    ways = lax.axis_size("dp")
    rows, width = part.shape
    size = rows // count // pieces
    vmem = pl.BlockSpec(memory_space=pltpu.VMEM)
    hops = (pieces, count - 1)
    return pl.pallas_call(
        functools.partial(line_sum_kernel, count, pieces, finish, (len(owned), len(outs)), share_terms),
        out_shape=(jax.ShapeDtypeStruct((rows, width), BF16), *outs),
        in_specs=[vmem] * (1 + len(owned)),
        out_specs=(vmem,) * (1 + len(outs)),
        scratch_shapes=[
            pltpu.VMEM((*hops, size, width), BF16),
            pltpu.VMEM((*hops, size, width), BF16),
            pltpu.VMEM((size, width), F32),
            pltpu.VMEM((count, 8, width), F32),
            pltpu.VMEM((ways, 8, width), F32),
        ]
        + [pltpu.SemaphoreType.DMA(hops)] * 8
        + [pltpu.SemaphoreType.DMA((count,))] * 2
        + [pltpu.SemaphoreType.DMA((ways,))] * 2,
        compiler_params=pltpu.CompilerParams(
            collective_id=collective_id, has_side_effects=True, vmem_limit_bytes=56 << 20
        ),
        cost_estimate=pl.CostEstimate(
            flops=rows * width * 8, transcendentals=0, bytes_accessed=rows * width * 200
        ),
        name="line_sum",
    )(part, *owned)


def finish_back(mine, total, own_refs, out_refs):
    base, value, gain = own_refs[:3]
    x = value[mine, :].astype(F32)
    r = inverse_rms(x)
    y = x * r
    e = gain[...] * total
    out = base[mine, :].astype(F32) + r * (e - y * jnp.mean(e * y, axis=-1, keepdims=True))
    out_refs[0][mine, :] = out
    out_refs[1][0:1, :] += jnp.sum(total * y, axis=0, keepdims=True)
    return out.astype(BF16)


def attn_gather_kernel(
    count,
    ways,
    places,
    tiles,
    bq,
    len_ref,
    q_ref,
    k_ref,
    v_ref,
    w_ref,
    tokens_ref,
    gain_ref,
    normed_ref,
    resid_ref,
    mixed_ref,
    linv_ref,
    full_ref,
    whole_ref,
    q6,
    vx,
    acc,
    *sems,
):
    give_up, give_down, line_sems, way_sems = sems[0:2], sems[2:4], sems[4:6], sems[6:8]
    load_tokens = pltpu.make_async_copy(tokens_ref, normed_ref, sems[8])
    me = lax.axis_index("tensor")
    spot = lax.axis_index("dp")
    piece = w_ref.shape[0] // ways
    weight_slots = {1: (1,), 3: (2,), 4: tuple(range(3, ways.bit_length() + 1))}
    levels = ways.bit_length() - 1
    last = count - 1
    rows, width = q_ref.shape
    chunks = rows // bq

    def place(block, c):
        at = pl.multiple_of(block * width, width)
        return full_ref.at[pl.ds(c * bq, bq), pl.ds(at, width)]

    def copy(c, s, upward):
        there = place(me - s + 1 if upward else me + s - 1, c)
        sem = give_up if upward else give_down
        return line_copy(there, there, sem, (c, s - 1), me + 1 if upward else me - 1)

    def wait(c, s, upward):
        there = place(me - s if upward else me + s, c)
        sem = give_up if upward else give_down
        line_copy(there, there, sem, (c, s - 1), me + 1 if upward else me - 1).wait_recv()

    def sends(s, upward):
        return (me >= s - 1) & (me < last) if upward else (me > 0) & (me <= count - s)

    def start(c, s, upward):
        if s > 1:

            @pl.when((me >= s - 1) if upward else (me <= count - s))
            def _():
                wait(c, s - 1, upward)

        @pl.when(sends(s, upward))
        def _():
            copy(c, s, upward).start()

    def attend(c):
        first = c * bq
        span = pl.ds(first, bq)
        q6[...] = stack_heads(q_ref[span, :].astype(F32), places).astype(BF16)
        acc[...] = jnp.zeros_like(acc)

        def step(j, masked):
            ks = pl.ds(pl.multiple_of(j * bq, bq), bq)
            prob = jnp.exp2(nt(q6[...], k_ref[ks, :]) * (SCALE * LOG2E))
            if masked:
                q_pos = lax.broadcasted_iota(jnp.int32, prob.shape, 0) & (bq - 1)
                k_pos = lax.broadcasted_iota(jnp.int32, prob.shape, 1)
                prob = jnp.where(k_pos <= q_pos, prob, 0.0)
            acc[...] += nn(prob.astype(BF16), vx[ks, :])

        if c > 0:

            @pl.loop(0, c)
            def _(j):
                step(j, False)

        step(c, True)
        inv = 1.0 / acc[:, LANES:]
        out = unstack_heads(acc[:, :LANES] * inv, places, tiles, bq)
        place(me, c)[...] = out.astype(BF16)
        mixed_ref[span, :] = out.astype(BF16)
        linv_ref[span, :] = unstack_heads(inv, places, tiles, bq)


    bits = [(spot // (1 << (levels - 1 - level))) % 2 for level in range(levels)]

    def own_part(peer, sender):
        return pltpu.make_async_remote_copy(
            src_ref=whole_ref.at[(me, *bits)],
            dst_ref=whole_ref.at[(sender, *bits)],
            send_sem=line_sems[0].at[peer],
            recv_sem=line_sems[1].at[sender],
            device_id={"tensor": peer},
            device_id_type=MESH,
        )

    def partner(level):
        return spot + (1 - 2 * bits[level]) * (1 << (levels - 1 - level))

    def held_parts(level, theirs=False):
        ours = [1 - bits[level] if theirs else bits[level], *bits[level + 1 :]]
        there = whole_ref.at[(slice(None),) * (level + 1) + tuple(ours)]
        return pltpu.make_async_remote_copy(
            src_ref=there,
            dst_ref=there,
            send_sem=way_sems[0].at[level],
            recv_sem=way_sems[1].at[level],
            device_id={"dp": partner(level)},
            device_id_type=MESH,
        )

    def weight_step(step):
        if step == 0:
            mine = pl.ds(pl.multiple_of(spot * piece, piece), piece)
            whole_ref[(me, *bits)] = w_ref[mine, :]
            for peer in range(count):

                @pl.when(peer != me)
                def _():
                    own_part(peer, me).start()

            return
        if step == 1:
            for peer in range(count):

                @pl.when(peer != me)
                def _():
                    own_part(peer, peer).wait_recv()

        else:
            held_parts(step - 2, True).wait_recv()
        if step - 1 < levels:
            held_parts(step - 1).start()

    def project(c):
        @pl.when(me == last)
        def _():
            wait(c, last, True)

        @pl.when(me == 0)
        def _():
            wait(c, last, False)

        span = pl.ds(c * bq, bq)
        resid = normed_ref[span, :].astype(F32)
        for block in range(count):
            weight = whole_ref[block].reshape(width, resid.shape[1])
            resid += nn(full_ref[span, pl.ds(block * width, width)], weight)
        normed_ref[span, :] = (resid * inverse_rms(resid) * gain_ref[...]).astype(BF16)
        own = resid_ref.shape[0]
        for j in range(bq // own):

            @pl.when(me == c * (bq // own) + j)
            def _():
                resid_ref[...] = resid[j * own : (j + 1) * own]

    load_tokens.start()
    barrier = pltpu.get_barrier_semaphore()
    for peer in range(count):

        @pl.when(peer != me)
        def _():
            pl.semaphore_signal(barrier, inc=1, device_id={"tensor": peer}, device_id_type=MESH)

    for level in range(levels):
        pl.semaphore_signal(
            barrier, inc=1, device_id={"dp": partner(level)}, device_id_type=MESH
        )
    pl.semaphore_wait(barrier, count - 1 + levels)
    weight_step(0)
    live = lax.broadcasted_iota(jnp.int32, (rows, LANES), 0) < len_ref[0]
    vx[:, :LANES] = jnp.where(live, v_ref[...].astype(F32), 0.0).astype(BF16)
    vx[:, LANES:] = jnp.where(live, 1.0, 0.0).astype(BF16)
    for slot in range(chunks + last - 1):
        if slot < chunks:
            attend(slot)
            for upward in (True, False):
                start(slot, 1, upward)
        for s in range(last, 1, -1):
            c = slot - (s - 1)
            if 0 <= c < chunks:
                for upward in (True, False):
                    start(c, s, upward)
        for step in weight_slots.get(slot, ()):
            weight_step(step)
        if slot == 4:
            load_tokens.wait()
        if slot >= max(4, last) and slot - max(4, last) < chunks:
            project(slot - max(4, last))
    for c in range(max(0, chunks + last - 1 - max(4, last)), chunks):
        project(c)
    for peer in range(count):

        @pl.when(peer != me)
        def _():
            own_part(peer, me).wait_send()

    for level in range(levels):
        held_parts(level).wait_send()
    for c in range(chunks):
        for s in range(1, count):
            for upward in (True, False):

                @pl.when(sends(s, upward))
                def _():
                    copy(c, s, upward).wait_send()


def attn_gather(length, q, k, v, w, tokens, gain, heads, group, bq, collective_id):
    count = lax.axis_size("tensor")
    ways = lax.axis_size("dp")
    rows, width = q.shape
    model = tokens.shape[1]
    vmem = pl.BlockSpec(memory_space=pltpu.VMEM)
    hops = (rows // bq, count - 1)
    levels = ways.bit_length() - 1
    return pl.pallas_call(
        functools.partial(
            attn_gather_kernel, count, ways, head_places(heads, group), width // LANES, bq
        ),
        out_shape=(
            jax.ShapeDtypeStruct((rows, model), BF16),
            jax.ShapeDtypeStruct((rows // count, model), F32),
            jax.ShapeDtypeStruct((rows, width), BF16),
            jax.ShapeDtypeStruct((rows, width), F32),
        ),
        in_specs=[pl.BlockSpec(memory_space=pltpu.SMEM)]
        + [vmem] * 4
        + [pl.BlockSpec(memory_space=pl.ANY), vmem],
        out_specs=(vmem,) * 4,
        scratch_shapes=[
            pltpu.VMEM((rows, count * width), BF16),
            pltpu.VMEM((count, *(2,) * levels, w.shape[0] // ways, model), BF16),
            pltpu.VMEM((heads * bq, LANES), BF16),
            pltpu.VMEM((rows, 2 * LANES), BF16),
            pltpu.VMEM((heads * bq, 2 * LANES), F32),
        ]
        + [pltpu.SemaphoreType.DMA(hops)] * 4
        + [pltpu.SemaphoreType.DMA((count,))] * 2
        + [pltpu.SemaphoreType.DMA((ways,))] * 2
        + [pltpu.SemaphoreType.DMA(())],
        compiler_params=pltpu.CompilerParams(
            collective_id=collective_id, has_side_effects=True, vmem_limit_bytes=58 << 20
        ),
        cost_estimate=pl.CostEstimate(
            flops=heads * rows * rows * 2 * LANES,
            transcendentals=heads * rows * rows // 2,
            bytes_accessed=rows * count * width * 120,
        ),
        name="attention_gather",
    )(length, q, k, v, w, tokens, gain)


def widen_kernel(after_ref, *refs):
    half = len(refs) // 2
    for narrow, wide in zip(refs[:half], refs[half:]):
        wide[...] = narrow[...].astype(wide.dtype)


def widen(arrays, types, sizes, after, vmem):
    rows, width = arrays[0].shape
    size = next(s for s in (*sizes, rows) if rows % s == 0)
    block = pl.BlockSpec((size, width), lambda i: (i, 0))
    return pl.pallas_call(
        widen_kernel,
        grid=(rows // size,),
        out_shape=tuple(jax.ShapeDtypeStruct((rows, width), t) for t in types),
        in_specs=[pl.BlockSpec((8, LANES), lambda i: (0, 0))] + [block] * len(arrays),
        out_specs=(block,) * len(arrays),
        compiler_params=pltpu.CompilerParams(
            dimension_semantics=("arbitrary",), vmem_limit_bytes=vmem << 20
        ),
        cost_estimate=pl.CostEstimate(flops=rows, transcendentals=0, bytes_accessed=rows * width),
        name="widen",
    )(after, *arrays)


def inverse_rms(x):
    return lax.rsqrt(jnp.mean(x * x, axis=-1, keepdims=True) + EPSILON)


def norm_back(x, r, gain, grad):
    y = x * r
    e = gain * grad
    return r * (e - y * jnp.mean(e * y, axis=-1, keepdims=True)), jnp.sum(grad * y, axis=0)


def rope_tables(row_count):
    half = HEAD_SIZE // 2
    positions = jnp.arange(row_count).astype(F32)[:, None]
    freq = jnp.exp(jnp.arange(half).astype(F32) * (-2.0 * math.log(ROPE_BASE) / HEAD_SIZE))
    angles = positions * freq[None, :]
    return jnp.cos(angles)[:, None, :], jnp.sin(angles)[:, None, :]


def turn(x, cosine, sine):
    half = HEAD_SIZE // 2
    low, high = x[..., :half], x[..., half:]
    return jnp.concatenate([low * cosine - high * sine, high * cosine + low * sine], axis=-1)


def by_head(x):
    return x.reshape(x.shape[0], x.shape[1] // HEAD_SIZE, HEAD_SIZE)


def flat(x):
    return x.reshape(x.shape[0], x.shape[1] * x.shape[2])


def prepare(x, gain, tables):
    heads = by_head(x)
    return flat(turn(heads * inverse_rms(heads) * gain, *tables))


def prepare_back(x, gain, tables, grad):
    heads = by_head(x)
    back = turn(by_head(grad), tables[0], -tables[1])
    dx, d_gain = norm_back(heads, inverse_rms(heads), gain, back)
    return flat(dx), jnp.sum(d_gain, axis=0)


def to_lanes(x):
    short = -x.shape[1] % LANES
    return x if short == 0 else jnp.pad(x, ((0, 0), (0, short)))


def pad_rows(w):
    short = -w.shape[0] % LANES
    return w if short == 0 else jnp.pad(w, ((0, short), (0, 0)))


def on_device(
    tokens,
    lengths,
    cotangent,
    norm_gain,
    query_w,
    key_weight,
    value_weight,
    out_w,
    query_gain,
    key_gain,
    mlp_gain,
    gate_w,
    up_w,
    down_w,
):
    row_count, width = tokens.shape
    me = lax.axis_index("tensor")
    count = lax.axis_size("tensor")
    m = row_count // count
    q_width = query_w.shape[1]
    k_width = key_weight.shape[1]
    heads = q_width // HEAD_SIZE
    group = q_width // k_width
    pieces = 64 // count
    own_shape = jax.ShapeDtypeStruct((m, width), F32)
    gain_shape = jax.ShapeDtypeStruct((8, width), F32)

    def own(x):
        return lax.dynamic_slice_in_dim(x, me * m, m, axis=0)

    live = (jnp.arange(row_count, dtype=jnp.int32) < lengths[0])[:, None]
    d_out = jnp.where(live, cotangent, jnp.zeros_like(cotangent))
    inputs = tokens.astype(F32)
    normed = (inputs * inverse_rms(inputs) * norm_gain).astype(BF16)
    inputs_own = own(tokens)
    qkv_w = jnp.concatenate([query_w, key_weight, value_weight], axis=1)
    edges = (q_width, q_width + k_width)
    queries, keys_val, values = jnp.split(nn(normed, qkv_w), edges, axis=1)
    tables = rope_tables(row_count)
    q_pad = to_lanes(prepare(queries, query_gain, tables).astype(BF16))
    k_pad = to_lanes(prepare(keys_val, key_gain, tables).astype(BF16))
    v_pad = to_lanes(values.astype(BF16))
    normed2, resid_own, mixed_pad, inverse_sums = attn_gather(
        lengths,
        q_pad,
        k_pad,
        v_pad,
        pad_rows(out_w),
        tokens,
        mlp_gain[None],
        heads,
        group,
        min(512, row_count),
        1,
    )
    mixed = mixed_pad[:, :q_width]
    gate = nn(normed2, gate_w)
    up = nn(normed2, up_w)
    sig = jax.nn.sigmoid(gate)
    hidden = (gate * sig * up).astype(BF16)
    mlp_part = nn(hidden, down_w).astype(BF16)
    mlp_part, gate, up = lax.optimization_barrier((mlp_part, gate, up))
    mlp_own = lax.psum_scatter(mlp_part, "tensor", scatter_dimension=0, tiled=True)
    sig = jax.nn.sigmoid(gate)
    d_hidden = nt(d_out, down_w)
    d_gate = (d_hidden * up * sig * (1.0 + gate * (1.0 - sig))).astype(BF16)
    d_up = (d_hidden * gate * sig).astype(BF16)
    d_normed2 = (nt(d_gate, gate_w) + nt(d_up, up_w)).astype(BF16)
    d_normed2, mlp_own = lax.optimization_barrier((d_normed2, mlp_own))
    d_resid, d_resid_own, d_mlp_gain = line_sum(
        d_normed2,
        (own(d_out), resid_own, mlp_gain[None]),
        (own_shape, gain_shape),
        finish_back,
        pieces,
        2,
    )
    g_gate = tn(d_gate, normed2).astype(BF16)
    g_up = tn(d_up, normed2).astype(BF16)
    g_down = tn(hidden, d_out).astype(BF16)
    g_gate, g_up, g_down = lax.psum((g_gate, g_up, g_down), "dp")

    after = d_mlp_gain[7, 0]
    block_own = (resid_own + after + mlp_own.astype(F32)).astype(BF16)
    block_own, d_resid = lax.optimization_barrier((block_own, d_resid))
    block_out = lax.all_gather(block_own, "tensor", axis=0, tiled=True)
    d_mixed = nt(d_resid, out_w).astype(BF16)
    dq, dk, dv = attn_bwd(
        lengths, q_pad, to_lanes(d_mixed), mixed_pad, inverse_sums, k_pad, v_pad, heads, group
    )
    dq, d_qgain = prepare_back(queries, query_gain, tables, dq[:, :q_width])
    dk, d_kgain = prepare_back(keys_val, key_gain, tables, dk[:, :k_width])
    d_q, d_k, d_v = dq.astype(BF16), dk.astype(BF16), dv[:, :k_width].astype(BF16)
    d_qkv = jnp.concatenate([d_q, d_k, d_v], axis=1)
    d_normed = nt(d_qkv, qkv_w).astype(BF16)
    head_terms = jnp.concatenate([d_qgain, d_kgain])
    terms = jnp.concatenate(
        [
            jnp.zeros((1, width), F32),
            d_mlp_gain[:1],
            jnp.pad(head_terms[None], ((0, 0), (0, width - 2 * HEAD_SIZE))),
            jnp.zeros((5, width), F32),
        ]
    )
    whole_grads = widen((g_gate, g_up, g_down), (F32,) * 3, (288, 96), d_mlp_gain, 58)
    d_normed, block_out, *whole_grads = lax.optimization_barrier(
        (d_normed, block_out, *whole_grads)
    )
    d_inputs, _, d_gains = line_sum(
        d_normed,
        (d_resid_own, inputs_own, norm_gain[None], terms),
        (own_shape, gain_shape),
        finish_back,
        pieces,
        3,
        True,
    )
    g_out = tn(mixed, d_resid).astype(BF16)
    g_qkv = tn(normed, d_qkv).astype(BF16)
    g_out, g_qkv, *whole_grads = lax.optimization_barrier((g_out, g_qkv, *whole_grads))
    g_out, g_qkv = lax.psum((g_out, g_qkv), "dp")
    g_query, g_key, g_value = (g.astype(F32) for g in jnp.split(g_qkv, edges, axis=1))
    d_inputs, block_out = widen((d_inputs, block_out), (F32, BF16), (256,), d_gains, 16)
    return (
        block_out,
        d_inputs,
        d_gains[0],
        g_query,
        g_key,
        g_value,
        g_out.astype(F32),
        d_gains[2, :HEAD_SIZE],
        d_gains[2, HEAD_SIZE : 2 * HEAD_SIZE],
        d_gains[1],
        whole_grads[0].T,
        whole_grads[1].T,
        whole_grads[2],
    )


def solution(mesh):
    rows, whole = P("dp", None), P()
    columns, depth = P(None, "tensor"), P("tensor", None)
    return jax.shard_map(
        on_device,
        mesh=mesh,
        in_specs=(
            rows,
            P("dp"),
            rows,
            whole,
            columns,
            columns,
            columns,
            depth,
            whole,
            whole,
            whole,
            columns,
            columns,
            depth,
        ),
        out_specs=(
            rows,
            rows,
            whole,
            columns,
            columns,
            columns,
            depth,
            whole,
            whole,
            whole,
            columns,
            columns,
            depth,
        ),
        check_vma=False,
    )
```

```python
import functools
import math

import jax
import jax.numpy as jnp
from jax import lax
from jax.experimental import pallas as pl
from jax.experimental.pallas import tpu as pltpu
from jax.sharding import PartitionSpec as P

HEAD_SIZE = 64
LANES = 128
SCALE = HEAD_SIZE**-0.5
LOG2E = math.log2(math.e)
EPSILON = 1e-05
ROPE_BASE = 1000000.0
F32 = jnp.float32
BF16 = jnp.bfloat16
MESH = pl.DeviceIdType.MESH


def nt(a,b): return lax.dot_general(a,b,(((1,),(1,)),((),())),preferred_element_type=F32)
def tn(a,b): return lax.dot_general(a,b,(((0,),(0,)),((),())),preferred_element_type=F32)
def nn(a,b): return lax.dot_general(a,b,(((1,),(0,)),((),())),preferred_element_type=F32)

def head_places(heads, group):
    return [(h // 2, h % 2, h // group) for h in range(heads)]

def half_mask(half, dtype=F32):
    lane = lax.broadcasted_iota(jnp.int32, (1, LANES), 1)
    keep = lane < HEAD_SIZE if half == 0 else lane >= HEAD_SIZE
    return keep

def stack_heads(x, places):
    out = []
    for tile, half, kv in places:
        piece = x[:, tile * LANES:(tile + 1) * LANES]
        if half != kv:
            piece = pltpu.roll(piece, HEAD_SIZE, 1)
        out.append(jnp.where(half_mask(kv), piece, 0.0))
    return jnp.concatenate(out, axis=0)

def unstack_heads(x, places, tiles, n):
    pieces = {}
    for h, (tile, half, kv) in enumerate(places):
        piece = x[h * n:(h + 1) * n]
        if half != kv:
            piece = pltpu.roll(piece, HEAD_SIZE, 1)
        pieces[tile, half] = piece
    out = []
    for tile in range(tiles):
        low = pieces[tile, 0]
        high = pieces.get((tile, 1))
        out.append(jnp.where(half_mask(0), low, 0.0 if high is None else high))
    return jnp.concatenate(out, axis=1)

def bwd_kernel(places, tiles, bq, bk, len_ref, q_ref, do_ref, o_ref, linv_ref, k_ref, v_ref, dq_ref, dk_ref, dv_ref, q6, do6, d_row, kx, dq6):
    i = pl.program_id(0)
    rows = k_ref.shape[0]
    heads = len(places)
    @pl.when(i == 0)
    def _():
        live = lax.broadcasted_iota(jnp.int32, (rows, LANES), 0) < len_ref[0]
        kx[...] = jnp.where(live, k_ref[...].astype(F32), 0.0).astype(BF16)
        dk_ref[...] = jnp.zeros_like(dk_ref)
        dv_ref[...] = jnp.zeros_like(dv_ref)
    q6[...] = stack_heads(q_ref[...].astype(F32), places).astype(BF16)
    dob = do_ref[...].astype(F32) * linv_ref[...]
    do6[...] = stack_heads(dob, places).astype(BF16)
    prod = stack_heads(dob * o_ref[...].astype(F32), places)
    hi = prod.astype(BF16)
    lo = (prod - hi.astype(F32)).astype(BF16)
    ones = jnp.ones((16, LANES), BF16)
    d_row[...] = nt(ones, hi) + nt(ones, lo)
    dq6[...] = jnp.zeros_like(dq6)
    def step(j, masked):
        ks = pl.ds(pl.multiple_of(j * bk, bk), bk)
        st = nt(k_ref[ks, :], q6[...])
        pt = jnp.exp2(st * (SCALE * LOG2E))
        if masked:
            kp = j * bk + lax.broadcasted_iota(jnp.int32, st.shape, 0)
            qp = i * bq + (lax.broadcasted_iota(jnp.int32, st.shape, 1) & (bq - 1))
            pt = jnp.where(kp <= qp, pt, 0.0)
        dv_ref[ks, :] += nn(pt.astype(BF16), do6[...])
        dpt = nt(v_ref[ks, :], do6[...])
        dst = (pt * (dpt - d_row[0:1, :])).astype(BF16)
        dk_ref[ks, :] += nn(dst, q6[...])
        dq6[...] += tn(dst, kx[ks, :])
    full = (i * bq) // bk
    @pl.loop(0, full)
    def _(j): step(j, False)
    @pl.loop(full, full + max(bq // bk, 1))
    def _(j): step(j, True)
    dq_ref[...] = unstack_heads(dq6[...] * SCALE, places, tiles, bq)
    @pl.when(i == pl.num_programs(0) - 1)
    def _():
        live = lax.broadcasted_iota(jnp.int32, (rows, LANES), 0) < len_ref[0]
        dk_ref[...] = jnp.where(live, dk_ref[...] * SCALE, 0.0)
        dv_ref[...] = jnp.where(live, dv_ref[...], 0.0)

def attn_bwd(length, q, do, o, linv, k, v, heads, group, bq=256, bk=256):
    rows, width = q.shape
    tiles = width // LANES
    places = head_places(heads, group)
    blk = pl.BlockSpec((bq, width), lambda i, n: (i, 0))
    whole = pl.BlockSpec((rows, LANES), lambda i, n: (0, 0))
    return pl.pallas_call(
        functools.partial(bwd_kernel, places, tiles, bq, bk),
        out_shape=(jax.ShapeDtypeStruct((rows, width), F32), jax.ShapeDtypeStruct((rows, LANES), F32), jax.ShapeDtypeStruct((rows, LANES), F32)),
        grid_spec=pltpu.PrefetchScalarGridSpec(
            num_scalar_prefetch=1, grid=(rows // bq,),
            in_specs=[blk] * 4 + [whole] * 2,
            out_specs=[blk, whole, whole],
            scratch_shapes=[pltpu.VMEM((heads * bq, LANES), BF16), pltpu.VMEM((heads * bq, LANES), BF16),
                            pltpu.VMEM((16, heads * bq), F32), pltpu.VMEM((rows, LANES), BF16),
                            pltpu.VMEM((heads * bq, LANES), F32)]),
        compiler_params=pltpu.CompilerParams(dimension_semantics=("arbitrary",), vmem_limit_bytes=48 << 20),
        cost_estimate=pl.CostEstimate(flops=rows * width, transcendentals=0, bytes_accessed=rows * width * 2),
        name="attention_backward",
    )(length, q, do, o, linv, k, v)


def line_copy(src, dst, sems, where, to):
    return pltpu.make_async_remote_copy(
        src_ref=src,
        dst_ref=dst,
        send_sem=sems[0].at[where],
        recv_sem=sems[1].at[where],
        device_id={"tensor": to},
        device_id_type=MESH,
    )


def greet_line(count, ways=0):
    me = lax.axis_index("tensor")
    barrier = pltpu.get_barrier_semaphore()

    def greet(peer):
        pl.semaphore_signal(barrier, inc=1, device_id={"tensor": peer}, device_id_type=MESH)

    if ways:
        spot = lax.axis_index("dp")
        for peer in range(count):

            @pl.when(peer != me)
            def _():
                greet(peer)

        for peer in range(ways):

            @pl.when(peer != spot)
            def _():
                pl.semaphore_signal(barrier, inc=1, device_id={"dp": peer}, device_id_type=MESH)

        pl.semaphore_wait(barrier, count - 1 + ways - 1)
        return

    @pl.when(me > 0)
    def _():
        greet(me - 1)

    @pl.when(me < count - 1)
    def _():
        greet(me + 1)

    @pl.when((me > 0) & (me < count - 1))
    def _():
        pl.semaphore_wait(barrier, 2)

    @pl.when((me == 0) | (me == count - 1))
    def _():
        pl.semaphore_wait(barrier, 1)


def line_sum_kernel(
    count, pieces, finish, kinds, share_terms, part_ref, *refs
):
    (own_refs, full_ref, out_refs), scratch = split_refs(refs, kinds)
    up_buf, down_buf, acc, shared, shared_ways = scratch[:5]
    sems = scratch[5:]
    ways = shared_ways.shape[0]
    spot = lax.axis_index("dp")
    sum_up, sum_down, give_up, give_down = (sems[0:2], sems[2:4], sems[4:6], sems[6:8])
    me = lax.axis_index("tensor")
    last = count - 1
    own = part_ref.shape[0] // count
    size = own // pieces

    def rows(block, c):
        return pl.ds(pl.multiple_of(block * own + c * size, size), size)

    def sum_copy(c, s, upward):
        buf, sem = (up_buf, sum_up) if upward else (down_buf, sum_down)
        to = me + 1 if upward else me - 1
        return buf, lambda src: line_copy(src, buf.at[c, s - 1], sem, (c, s - 1), to)

    def sum_start(c, s, upward):
        buf, copy = sum_copy(c, s, upward)
        first = me == 0 if upward else me == last
        block = count - s + me if upward else me - (count - s)
        sends = me <= s - 1 if upward else me >= count - s
        sends = sends & (me < last if upward else me > 0)

        @pl.when(sends & first)
        def _():
            copy(part_ref.at[rows(block, c)]).start()

        if s > 1:

            @pl.when(sends & jnp.logical_not(first))
            def _():
                sum_wait(c, s - 1, upward)
                held = buf.at[c, s - 2]
                held[...] = (held[...].astype(F32) + part_ref[rows(block, c), :].astype(F32)).astype(BF16)
                copy(held).start()

    def sum_wait(c, s, upward):
        buf, copy = sum_copy(c, s, upward)
        copy(buf.at[c, s - 1]).wait_recv()

    def give_copy(c, s, upward):
        block = me - s + 1 if upward else me + s - 1
        sem = give_up if upward else give_down
        place = full_ref.at[rows(block, c)]
        return line_copy(place, place, sem, (c, s - 1), me + 1 if upward else me - 1)

    def give_wait(c, s, upward):
        block = me - s if upward else me + s
        sem = give_up if upward else give_down
        place = full_ref.at[rows(block, c)]
        line_copy(place, place, sem, (c, s - 1), me + 1 if upward else me - 1).wait_recv()

    def give_start(c, s, upward):
        sends = (me >= s - 1) & (me < last) if upward else (me > 0) & (me <= count - s)
        if s > 1:
            got = (me >= s - 1) if upward else (me <= count - s)

            @pl.when(got)
            def _():
                give_wait(c, s - 1, upward)

        @pl.when(sends)
        def _():
            give_copy(c, s, upward).start()

    def settle(c):
        acc[...] = part_ref[rows(me, c), :].astype(F32)

        @pl.when(me > 0)
        def _():
            sum_wait(c, last, True)
            acc[...] += up_buf[c, last - 1].astype(F32)

        @pl.when(me < last)
        def _():
            sum_wait(c, last, False)
            acc[...] += down_buf[c, last - 1].astype(F32)

        mine = pl.ds(pl.multiple_of(c * size, size), size)
        full_ref[rows(me, c), :] = finish(mine, acc[...], own_refs, out_refs)

    def share(axis, to, sender, at):
        here, place, sem = (me, shared, 8) if axis == "tensor" else (spot, shared_ways, 10)
        return pltpu.make_async_remote_copy(
            src_ref=out_refs[1],
            dst_ref=place.at[sender],
            send_sem=sems[sem].at[to],
            recv_sem=sems[sem + 1].at[sender],
            device_id={axis: to},
            device_id_type=MESH,
        )

    def share_start(axis, size_of, here):
        for to in range(size_of):

            @pl.when(to != here)
            def _():
                share(axis, to, here, here).start()

    def share_finish(axis, size_of, here, place):
        for peer in range(size_of):

            @pl.when(peer != here)
            def _():
                share(axis, peer, here, here).wait_send()
                share(axis, peer, peer, here).wait_recv()

            @pl.when(peer == here)
            def _():
                place[peer] = out_refs[1][...]

        terms = place[0]
        for peer in range(1, size_of):
            terms = terms + place[peer]
        out_refs[1][...] = terms

    greet_line(count, ways if share_terms else 0)
    if len(out_refs) > 1:
        out_refs[1][...] = own_refs[3][...] if len(own_refs) > 3 else jnp.zeros_like(out_refs[1])

    def stage(c, run):
        @pl.when((c >= 0) & (c < pieces))
        def _():
            run(c)

    def both(start, s):
        def run(c):
            for upward in (True, False):
                start(c, s, upward)

        return run

    def owner_turn(c):
        settle(c)
        both(give_start, 1)(c)

    @pl.loop(0, pieces + 2 * last)
    def _(slot):
        stage(slot, both(sum_start, 1))
        for s in range(last, 1, -1):
            stage(slot - last - (s - 1), both(give_start, s))
        stage(slot - last, owner_turn)
        if share_terms:

            @pl.when(slot == pieces - 1 + last)
            def _():
                share_start("tensor", count, me)

            @pl.when(slot == pieces + 2 * last - 2)
            def _():
                share_finish("tensor", count, me, shared)
                share_start("dp", ways, spot)

        for s in range(last, 1, -1):
            stage(slot - (s - 1), both(sum_start, s))

    @pl.loop(0, pieces)
    def _(c):
        @pl.when(me == last)
        def _():
            give_wait(c, last, True)

        @pl.when(me == 0)
        def _():
            give_wait(c, last, False)

        for s in range(1, count):
            for upward in (True, False):
                sends = me <= s - 1 if upward else me >= count - s
                sends = sends & (me < last if upward else me > 0)

                @pl.when(sends)
                def _():
                    buf, copy = sum_copy(c, s, upward)
                    copy(buf.at[c, s - 1]).wait_send()

                sends = (me >= s - 1) & (me < last) if upward else (me > 0) & (me <= count - s)

                @pl.when(sends)
                def _():
                    give_copy(c, s, upward).wait_send()

    if share_terms:
        share_finish("dp", ways, spot, shared_ways)


def split_refs(refs, kinds):
    n_own, n_out = kinds
    own_refs = refs[:n_own]
    full_ref = refs[n_own]
    out_refs = refs[n_own + 1 : n_own + 1 + n_out]
    return (own_refs, full_ref, out_refs), refs[n_own + 1 + n_out :]


def line_sum(part, owned, outs, finish, pieces, collective_id, share_terms=False):
    count = lax.axis_size("tensor")
    ways = lax.axis_size("dp")
    rows, width = part.shape
    size = rows // count // pieces
    vmem = pl.BlockSpec(memory_space=pltpu.VMEM)
    hops = (pieces, count - 1)
    return pl.pallas_call(
        functools.partial(line_sum_kernel, count, pieces, finish, (len(owned), len(outs)), share_terms),
        out_shape=(jax.ShapeDtypeStruct((rows, width), BF16), *outs),
        in_specs=[vmem] * (1 + len(owned)),
        out_specs=(vmem,) * (1 + len(outs)),
        scratch_shapes=[
            pltpu.VMEM((*hops, size, width), BF16),
            pltpu.VMEM((*hops, size, width), BF16),
            pltpu.VMEM((size, width), F32),
            pltpu.VMEM((count, 8, width), F32),
            pltpu.VMEM((ways, 8, width), F32),
        ]
        + [pltpu.SemaphoreType.DMA(hops)] * 8
        + [pltpu.SemaphoreType.DMA((count,))] * 2
        + [pltpu.SemaphoreType.DMA((ways,))] * 2,
        compiler_params=pltpu.CompilerParams(
            collective_id=collective_id, has_side_effects=True, vmem_limit_bytes=56 << 20
        ),
        cost_estimate=pl.CostEstimate(
            flops=rows * width * 8, transcendentals=0, bytes_accessed=rows * width * 200
        ),
        name="line_sum",
    )(part, *owned)


def finish_back(mine, total, own_refs, out_refs):
    base, value, gain = own_refs[:3]
    x = value[mine, :].astype(F32)
    r = inverse_rms(x)
    y = x * r
    e = gain[...] * total
    out = base[mine, :].astype(F32) + r * (e - y * jnp.mean(e * y, axis=-1, keepdims=True))
    out_refs[0][mine, :] = out
    out_refs[1][0:1, :] += jnp.sum(total * y, axis=0, keepdims=True)
    return out.astype(BF16)


def attn_gather_kernel(
    count,
    ways,
    places,
    tiles,
    bq,
    len_ref,
    q_ref,
    k_ref,
    v_ref,
    w_ref,
    tokens_ref,
    gain_ref,
    normed_ref,
    resid_ref,
    mixed_ref,
    linv_ref,
    full_ref,
    whole_ref,
    q6,
    vx,
    acc,
    *sems,
):
    give_up, give_down, line_sems, way_sems = sems[0:2], sems[2:4], sems[4:6], sems[6:8]
    load_tokens = pltpu.make_async_copy(tokens_ref, normed_ref, sems[8])
    me = lax.axis_index("tensor")
    spot = lax.axis_index("dp")
    piece = w_ref.shape[0] // ways
    weight_slots = {1: (1,), 3: (2,), 4: tuple(range(3, ways.bit_length() + 1))}
    levels = ways.bit_length() - 1
    last = count - 1
    rows, width = q_ref.shape
    chunks = rows // bq

    def place(block, c):
        at = pl.multiple_of(block * width, width)
        return full_ref.at[pl.ds(c * bq, bq), pl.ds(at, width)]

    def copy(c, s, upward):
        there = place(me - s + 1 if upward else me + s - 1, c)
        sem = give_up if upward else give_down
        return line_copy(there, there, sem, (c, s - 1), me + 1 if upward else me - 1)

    def wait(c, s, upward):
        there = place(me - s if upward else me + s, c)
        sem = give_up if upward else give_down
        line_copy(there, there, sem, (c, s - 1), me + 1 if upward else me - 1).wait_recv()

    def sends(s, upward):
        return (me >= s - 1) & (me < last) if upward else (me > 0) & (me <= count - s)

    def start(c, s, upward):
        if s > 1:

            @pl.when((me >= s - 1) if upward else (me <= count - s))
            def _():
                wait(c, s - 1, upward)

        @pl.when(sends(s, upward))
        def _():
            copy(c, s, upward).start()

    def attend(c):
        first = c * bq
        span = pl.ds(first, bq)
        q6[...] = stack_heads(q_ref[span, :].astype(F32), places).astype(BF16)
        acc[...] = jnp.zeros_like(acc)

        def step(j, masked):
            ks = pl.ds(pl.multiple_of(j * bq, bq), bq)
            prob = jnp.exp2(nt(q6[...], k_ref[ks, :]) * (SCALE * LOG2E))
            if masked:
                q_pos = lax.broadcasted_iota(jnp.int32, prob.shape, 0) & (bq - 1)
                k_pos = lax.broadcasted_iota(jnp.int32, prob.shape, 1)
                prob = jnp.where(k_pos <= q_pos, prob, 0.0)
            acc[...] += nn(prob.astype(BF16), vx[ks, :])

        if c > 0:

            @pl.loop(0, c)
            def _(j):
                step(j, False)

        step(c, True)
        inv = 1.0 / acc[:, LANES:]
        out = unstack_heads(acc[:, :LANES] * inv, places, tiles, bq)
        place(me, c)[...] = out.astype(BF16)
        mixed_ref[span, :] = out.astype(BF16)
        linv_ref[span, :] = unstack_heads(inv, places, tiles, bq)


    bits = [(spot // (1 << (levels - 1 - level))) % 2 for level in range(levels)]

    def own_part(peer, sender):
        return pltpu.make_async_remote_copy(
            src_ref=whole_ref.at[(me, *bits)],
            dst_ref=whole_ref.at[(sender, *bits)],
            send_sem=line_sems[0].at[peer],
            recv_sem=line_sems[1].at[sender],
            device_id={"tensor": peer},
            device_id_type=MESH,
        )

    def partner(level):
        return spot + (1 - 2 * bits[level]) * (1 << (levels - 1 - level))

    def held_parts(level, theirs=False):
        ours = [1 - bits[level] if theirs else bits[level], *bits[level + 1 :]]
        there = whole_ref.at[(slice(None),) * (level + 1) + tuple(ours)]
        return pltpu.make_async_remote_copy(
            src_ref=there,
            dst_ref=there,
            send_sem=way_sems[0].at[level],
            recv_sem=way_sems[1].at[level],
            device_id={"dp": partner(level)},
            device_id_type=MESH,
        )

    def weight_step(step):
        if step == 0:
            mine = pl.ds(pl.multiple_of(spot * piece, piece), piece)
            whole_ref[(me, *bits)] = w_ref[mine, :]
            for peer in range(count):

                @pl.when(peer != me)
                def _():
                    own_part(peer, me).start()

            return
        if step == 1:
            for peer in range(count):

                @pl.when(peer != me)
                def _():
                    own_part(peer, peer).wait_recv()

        else:
            held_parts(step - 2, True).wait_recv()
        if step - 1 < levels:
            held_parts(step - 1).start()

    def project(c):
        @pl.when(me == last)
        def _():
            wait(c, last, True)

        @pl.when(me == 0)
        def _():
            wait(c, last, False)

        span = pl.ds(c * bq, bq)
        resid = normed_ref[span, :].astype(F32)
        for block in range(count):
            weight = whole_ref[block].reshape(width, resid.shape[1])
            resid += nn(full_ref[span, pl.ds(block * width, width)], weight)
        normed_ref[span, :] = (resid * inverse_rms(resid) * gain_ref[...]).astype(BF16)
        own = resid_ref.shape[0]
        for j in range(bq // own):

            @pl.when(me == c * (bq // own) + j)
            def _():
                resid_ref[...] = resid[j * own : (j + 1) * own]

    load_tokens.start()
    barrier = pltpu.get_barrier_semaphore()
    for peer in range(count):

        @pl.when(peer != me)
        def _():
            pl.semaphore_signal(barrier, inc=1, device_id={"tensor": peer}, device_id_type=MESH)

    for level in range(levels):
        pl.semaphore_signal(
            barrier, inc=1, device_id={"dp": partner(level)}, device_id_type=MESH
        )
    pl.semaphore_wait(barrier, count - 1 + levels)
    weight_step(0)
    live = lax.broadcasted_iota(jnp.int32, (rows, LANES), 0) < len_ref[0]
    vx[:, :LANES] = jnp.where(live, v_ref[...].astype(F32), 0.0).astype(BF16)
    vx[:, LANES:] = jnp.where(live, 1.0, 0.0).astype(BF16)
    for slot in range(chunks + last - 1):
        if slot < chunks:
            attend(slot)
            for upward in (True, False):
                start(slot, 1, upward)
        for s in range(last, 1, -1):
            c = slot - (s - 1)
            if 0 <= c < chunks:
                for upward in (True, False):
                    start(c, s, upward)
        for step in weight_slots.get(slot, ()):
            weight_step(step)
        if slot == 4:
            load_tokens.wait()
        if slot >= max(4, last) and slot - max(4, last) < chunks:
            project(slot - max(4, last))
    for c in range(max(0, chunks + last - 1 - max(4, last)), chunks):
        project(c)
    for peer in range(count):

        @pl.when(peer != me)
        def _():
            own_part(peer, me).wait_send()

    for level in range(levels):
        held_parts(level).wait_send()
    for c in range(chunks):
        for s in range(1, count):
            for upward in (True, False):

                @pl.when(sends(s, upward))
                def _():
                    copy(c, s, upward).wait_send()


def attn_gather(length, q, k, v, w, tokens, gain, heads, group, bq, collective_id):
    count = lax.axis_size("tensor")
    ways = lax.axis_size("dp")
    rows, width = q.shape
    model = tokens.shape[1]
    vmem = pl.BlockSpec(memory_space=pltpu.VMEM)
    hops = (rows // bq, count - 1)
    levels = ways.bit_length() - 1
    return pl.pallas_call(
        functools.partial(
            attn_gather_kernel, count, ways, head_places(heads, group), width // LANES, bq
        ),
        out_shape=(
            jax.ShapeDtypeStruct((rows, model), BF16),
            jax.ShapeDtypeStruct((rows // count, model), F32),
            jax.ShapeDtypeStruct((rows, width), BF16),
            jax.ShapeDtypeStruct((rows, width), F32),
        ),
        in_specs=[pl.BlockSpec(memory_space=pltpu.SMEM)]
        + [vmem] * 4
        + [pl.BlockSpec(memory_space=pl.ANY), vmem],
        out_specs=(vmem,) * 4,
        scratch_shapes=[
            pltpu.VMEM((rows, count * width), BF16),
            pltpu.VMEM((count, *(2,) * levels, w.shape[0] // ways, model), BF16),
            pltpu.VMEM((heads * bq, LANES), BF16),
            pltpu.VMEM((rows, 2 * LANES), BF16),
            pltpu.VMEM((heads * bq, 2 * LANES), F32),
        ]
        + [pltpu.SemaphoreType.DMA(hops)] * 4
        + [pltpu.SemaphoreType.DMA((count,))] * 2
        + [pltpu.SemaphoreType.DMA((ways,))] * 2
        + [pltpu.SemaphoreType.DMA(())],
        compiler_params=pltpu.CompilerParams(
            collective_id=collective_id, has_side_effects=True, vmem_limit_bytes=58 << 20
        ),
        cost_estimate=pl.CostEstimate(
            flops=heads * rows * rows * 2 * LANES,
            transcendentals=heads * rows * rows // 2,
            bytes_accessed=rows * count * width * 120,
        ),
        name="attention_gather",
    )(length, q, k, v, w, tokens, gain)


def widen_kernel(after_ref, *refs):
    half = len(refs) // 2
    for narrow, wide in zip(refs[:half], refs[half:]):
        wide[...] = narrow[...].astype(wide.dtype)


def widen(arrays, types, sizes, after, vmem):
    rows, width = arrays[0].shape
    size = next(s for s in (*sizes, rows) if rows % s == 0)
    block = pl.BlockSpec((size, width), lambda i: (i, 0))
    return pl.pallas_call(
        widen_kernel,
        grid=(rows // size,),
        out_shape=tuple(jax.ShapeDtypeStruct((rows, width), t) for t in types),
        in_specs=[pl.BlockSpec((8, LANES), lambda i: (0, 0))] + [block] * len(arrays),
        out_specs=(block,) * len(arrays),
        compiler_params=pltpu.CompilerParams(
            dimension_semantics=("arbitrary",), vmem_limit_bytes=vmem << 20
        ),
        cost_estimate=pl.CostEstimate(flops=rows, transcendentals=0, bytes_accessed=rows * width),
        name="widen",
    )(after, *arrays)


def inverse_rms(x):
    return lax.rsqrt(jnp.mean(x * x, axis=-1, keepdims=True) + EPSILON)


def norm_back(x, r, gain, grad):
    y = x * r
    e = gain * grad
    return r * (e - y * jnp.mean(e * y, axis=-1, keepdims=True)), jnp.sum(grad * y, axis=0)


def rope_tables(row_count):
    half = HEAD_SIZE // 2
    positions = jnp.arange(row_count).astype(F32)[:, None]
    freq = jnp.exp(jnp.arange(half).astype(F32) * (-2.0 * math.log(ROPE_BASE) / HEAD_SIZE))
    angles = positions * freq[None, :]
    return jnp.cos(angles)[:, None, :], jnp.sin(angles)[:, None, :]


def turn(x, cosine, sine):
    half = HEAD_SIZE // 2
    low, high = x[..., :half], x[..., half:]
    return jnp.concatenate([low * cosine - high * sine, high * cosine + low * sine], axis=-1)


def by_head(x):
    return x.reshape(x.shape[0], x.shape[1] // HEAD_SIZE, HEAD_SIZE)


def flat(x):
    return x.reshape(x.shape[0], x.shape[1] * x.shape[2])


def prepare(x, gain, tables):
    heads = by_head(x)
    return flat(turn(heads * inverse_rms(heads) * gain, *tables))


def prepare_back(x, gain, tables, grad):
    heads = by_head(x)
    back = turn(by_head(grad), tables[0], -tables[1])
    dx, d_gain = norm_back(heads, inverse_rms(heads), gain, back)
    return flat(dx), jnp.sum(d_gain, axis=0)


def to_lanes(x):
    short = -x.shape[1] % LANES
    return x if short == 0 else jnp.pad(x, ((0, 0), (0, short)))


def pad_rows(w):
    short = -w.shape[0] % LANES
    return w if short == 0 else jnp.pad(w, ((0, short), (0, 0)))


def on_device(
    tokens,
    lengths,
    cotangent,
    norm_gain,
    query_w,
    key_weight,
    value_weight,
    out_w,
    query_gain,
    key_gain,
    mlp_gain,
    gate_w,
    up_w,
    down_w,
):
    row_count, width = tokens.shape
    me = lax.axis_index("tensor")
    count = lax.axis_size("tensor")
    m = row_count // count
    q_width = query_w.shape[1]
    k_width = key_weight.shape[1]
    heads = q_width // HEAD_SIZE
    group = q_width // k_width
    pieces = 64 // count
    own_shape = jax.ShapeDtypeStruct((m, width), F32)
    gain_shape = jax.ShapeDtypeStruct((8, width), F32)

    def own(x):
        return lax.dynamic_slice_in_dim(x, me * m, m, axis=0)

    live = (jnp.arange(row_count, dtype=jnp.int32) < lengths[0])[:, None]
    d_out = jnp.where(live, cotangent, jnp.zeros_like(cotangent))
    inputs = tokens.astype(F32)
    normed = (inputs * inverse_rms(inputs) * norm_gain).astype(BF16)
    inputs_own = own(tokens)
    own_live = (me * m + jnp.arange(m, dtype=jnp.int32) < lengths[0])[:, None]
    d_out_own = jnp.where(own_live, own(cotangent), jnp.zeros((), BF16))
    qkv_w = jnp.concatenate([query_w, key_weight, value_weight], axis=1)
    edges = (q_width, q_width + k_width)
    queries, keys_val, values = jnp.split(nn(normed, qkv_w), edges, axis=1)
    tables = rope_tables(row_count)
    q_pad = to_lanes(prepare(queries, query_gain, tables).astype(BF16))
    k_pad = to_lanes(prepare(keys_val, key_gain, tables).astype(BF16))
    v_pad = to_lanes(values.astype(BF16))
    normed2, resid_own, mixed_pad, inverse_sums = attn_gather(
        lengths,
        q_pad,
        k_pad,
        v_pad,
        pad_rows(out_w),
        tokens,
        mlp_gain[None],
        heads,
        group,
        min(512, row_count),
        1,
    )
    mixed = mixed_pad[:, :q_width]
    gate = nn(normed2, gate_w)
    up = nn(normed2, up_w)
    sig = jax.nn.sigmoid(gate)
    hidden = (gate * sig * up).astype(BF16)
    mlp_part = nn(hidden, down_w).astype(BF16)
    mlp_part, gate, up = lax.optimization_barrier((mlp_part, gate, up))
    mlp_own = lax.psum_scatter(mlp_part, "tensor", scatter_dimension=0, tiled=True)
    sig = jax.nn.sigmoid(gate)
    d_hidden = jnp.where(live, nt(cotangent, down_w), 0.0)
    d_gate = (d_hidden * up * sig * (1.0 + gate * (1.0 - sig))).astype(BF16)
    d_up = (d_hidden * gate * sig).astype(BF16)
    d_normed2 = (nt(d_gate, gate_w) + nt(d_up, up_w)).astype(BF16)
    d_normed2, mlp_own = lax.optimization_barrier((d_normed2, mlp_own))
    d_resid, d_resid_own, d_mlp_gain = line_sum(
        d_normed2,
        (d_out_own, resid_own, mlp_gain[None]),
        (own_shape, gain_shape),
        finish_back,
        pieces,
        2,
    )
    g_gate = tn(d_gate, normed2).astype(BF16)
    g_up = tn(d_up, normed2).astype(BF16)
    g_down = tn(hidden, d_out).astype(BF16)
    g_gate, g_up, g_down = lax.psum((g_gate, g_up, g_down), "dp")

    after = d_mlp_gain[7, 0]
    block_own = (resid_own + after + mlp_own.astype(F32)).astype(BF16)
    block_own, d_resid = lax.optimization_barrier((block_own, d_resid))
    block_out = lax.all_gather(block_own, "tensor", axis=0, tiled=True)
    d_mixed = nt(d_resid, out_w).astype(BF16)
    dq, dk, dv = attn_bwd(
        lengths, q_pad, to_lanes(d_mixed), mixed_pad, inverse_sums, k_pad, v_pad, heads, group
    )
    dq, d_qgain = prepare_back(queries, query_gain, tables, dq[:, :q_width])
    dk, d_kgain = prepare_back(keys_val, key_gain, tables, dk[:, :k_width])
    d_q, d_k, d_v = dq.astype(BF16), dk.astype(BF16), dv[:, :k_width].astype(BF16)
    d_qkv = jnp.concatenate([d_q, d_k, d_v], axis=1)
    d_normed = nt(d_qkv, qkv_w).astype(BF16)
    head_terms = jnp.concatenate([d_qgain, d_kgain])
    terms = jnp.concatenate(
        [
            jnp.zeros((1, width), F32),
            d_mlp_gain[:1],
            jnp.pad(head_terms[None], ((0, 0), (0, width - 2 * HEAD_SIZE))),
            jnp.zeros((5, width), F32),
        ]
    )
    whole_grads = widen((g_gate, g_up, g_down), (F32,) * 3, (288, 96), d_mlp_gain, 58)
    d_normed, block_out, *whole_grads = lax.optimization_barrier(
        (d_normed, block_out, *whole_grads)
    )
    d_inputs, _, d_gains = line_sum(
        d_normed,
        (d_resid_own, inputs_own, norm_gain[None], terms),
        (own_shape, gain_shape),
        finish_back,
        pieces,
        3,
        True,
    )
    g_out = tn(mixed, d_resid).astype(BF16)
    g_qkv = tn(normed, d_qkv).astype(BF16)
    g_out, g_qkv, *whole_grads = lax.optimization_barrier((g_out, g_qkv, *whole_grads))
    g_out, g_qkv = lax.psum((g_out, g_qkv), "dp")
    g_query, g_key, g_value = (g.astype(F32) for g in jnp.split(g_qkv, edges, axis=1))
    d_inputs, block_out = widen((d_inputs, block_out), (F32, BF16), (256,), d_gains, 16)
    return (
        block_out,
        d_inputs,
        d_gains[0],
        g_query,
        g_key,
        g_value,
        g_out.astype(F32),
        d_gains[2, :HEAD_SIZE],
        d_gains[2, HEAD_SIZE : 2 * HEAD_SIZE],
        d_gains[1],
        whole_grads[0].T,
        whole_grads[1].T,
        whole_grads[2],
    )


def solution(mesh):
    rows, whole = P("dp", None), P()
    columns, depth = P(None, "tensor"), P("tensor", None)
    return jax.shard_map(
        on_device,
        mesh=mesh,
        in_specs=(
            rows,
            P("dp"),
            rows,
            whole,
            columns,
            columns,
            columns,
            depth,
            whole,
            whole,
            whole,
            columns,
            columns,
            depth,
        ),
        out_specs=(
            rows,
            rows,
            whole,
            columns,
            columns,
            columns,
            depth,
            whole,
            whole,
            whole,
            columns,
            columns,
            depth,
        ),
        check_vma=False,
    )
```
